32 devices in a mesh: stream: 8 (over y, x, core), span: 4 (over z).
Axes of the slice: x: 2, y: 2, z: 4, core: 2. Of those that a mesh axis runs over, the one named last changes fastest.
Arguments:
- velocity: float32 [3, 128, 128, 128], P(None, 'stream', 'span'), may hold values from -6 to 6
- weights: bfloat16 [16384, 2048], P(('stream', 'span')), may hold values from -0.125 to 0.125
- tile_block: int32 [128], P(('stream', 'span')), may hold values from 0 to 31
- normals: float32 [3, 16384], P(None, ('stream', 'span')), may hold values from -3 to 3
- marker_panel: int32 [16384], P(('stream', 'span')), may hold values from 0 to 127, as said below
- mode_shape: bfloat16 [16384, 128], P(('stream', 'span')), may hold values from -0.59765625 to 0.59765625
- modal_disp: float32 [128, 128], P(('stream', 'span')), may hold values from -6 to 6
- modal_rate: float32 [128, 128], P(('stream', 'span')), may hold values from -6 to 6
- mode_omega: float32 [128, 128], P(('stream', 'span')), may hold values from 0.05 to 1.8
- mode_zeta: float32 [128, 128], P(('stream', 'span')), may hold values from 0.01 to 0.2
- base_load: float32 [128, 128], P(('stream', 'span')), may hold values from 0.01 to 1
- stress_modes: bfloat16 [3904, 128], replicated, may hold values from -6 to 6
- hot_nodes: int32 [128, 32], P(('stream', 'span')), may hold values from 0 to 3903
- freq_bins: int32 [256], replicated, may hold values from 1 to 1023
Outputs:
- velocity_next: float32 [3, 128, 128, 128], P(None, 'stream', 'span')
- panel_disp: float32 [128, 128], P(('stream', 'span'))
- panel_rate: float32 [128, 128], P(('stream', 'span'))
- log_damage: float32 [128, 32], P(('stream', 'span'))
The draws below stay inside these ranges and needn't reach their ends.
Inputs may be any that keep to these rules, and one draw needn't show every extreme that they name: `marker_panel`: among the markers of one device, at most 192 lie on panels p with the same p // 16, and exactly 192 for some such value.
All inputs are finite; a program needn't handle non-finite values.
Results may differ from the reference program's by a relative error of at most 0.0017.
Values sent between devices are 32-bit elements; how exact they have to be, the bound alone decides.
A program may use at most 64 MiB of HBM per device.

```python
import math
import jax
import jax.numpy as jnp
from jax import lax

CX = 16
CY = 32
CZ = 128
M_DEV = 512
P_DEV = 16
TILE = 128
BLK = 2048
MODES = 128
HOT = 32
NODES = 3904
NBINS = 256
STEPS = 2
NX = 128
NY = 128
NZ = 128
MARK = 16384
P_SIZE = 128
CAP = 192
N_STREAM = 8
N_SPAN = 4


def draw_marker_panel(key, part):
    devices = MARK // M_DEV
    streams = P_SIZE // P_DEV
    tickets = streams * CAP
    owner_bias = jax.random.randint(jax.random.fold_in(key, 7), (streams,), 0, 4096)

    def one_device(device_key):
        keys = jax.random.split(device_key, 4)
        hottest = jax.random.randint(keys[0], (), 0, streams)
        ticket_ids = jnp.arange(tickets, dtype=jnp.int32)
        ticket_owner = ticket_ids // CAP
        noise = jax.random.randint(keys[1], (tickets,), 0, 4096)
        scores = (noise + owner_bias[ticket_owner] + 1) * tickets + ticket_ids
        scores = jnp.where(ticket_owner == hottest, -1 - ticket_ids, scores)
        picked = lax.top_k(scores, M_DEV - CAP)[1]
        chosen = ticket_owner[picked]
        owners = jnp.concatenate([jnp.full((CAP,), hottest, jnp.int32), chosen.astype(jnp.int32)])
        owners = jax.random.permutation(keys[2], owners)
        within = jax.random.randint(keys[3], (M_DEV,), 0, P_DEV)
        return owners * P_DEV + within
    device_keys = jax.random.split(jax.random.fold_in(key, 3), devices)
    return jax.vmap(one_device)(device_keys).reshape(MARK).astype(jnp.int32)


def set_ends(result, stream_key, smallest, top_value):
    extent = result.shape
    spot = [jax.random.randint(jax.random.fold_in(stream_key, axis), (), 0, extent[axis]) for axis in range(len(extent))]
    result = result.at[tuple(spot)].set(smallest)
    longest = extent.index(max(extent))
    spot[longest] = (spot[longest] + 1) % extent[longest]
    return result.at[tuple(spot)].set(top_value)


def level_of(stream_key, shape, pieces, least, top_value):
    gain = 1.0
    for axis_at, shards_of in pieces:
        heights = jax.random.uniform(jax.random.fold_in(jax.random.fold_in(stream_key, 6), axis_at), (shards_of,), jnp.float32, least / len(pieces), top_value / len(pieces))
        gain = gain * jnp.repeat(jnp.exp(heights), shape[axis_at] // shards_of).reshape((-1,) + (1,) * (len(shape) - 1 - axis_at))
    return gain


def centred(key, dims, width, bound, pieces=(), kind=jnp.bfloat16):
    level = level_of(key, dims, pieces, -0.22, 0.18) if pieces else 1.0
    array = jax.random.normal(key, dims, jnp.float32) * width * level
    return jnp.minimum(jnp.maximum(array, -bound), bound).astype(kind)


def setup_inputs(seed: int = 0) -> dict:
    arg_keys = jax.random.split(jax.random.key(seed), 15)
    return {
        "velocity": centred(arg_keys[0], (3, NX, NY, NZ), 1.0, 6.0, ((1, 8), (2, 4)), jnp.float32),
        "weights": centred(arg_keys[1], (MARK, BLK), BLK ** -0.5, 0.125, ((0, 32),)),
        "tile_block": set_ends(jax.random.randint(arg_keys[2], (MARK // TILE,), 0, CX * CY * CZ // BLK), jax.random.fold_in(arg_keys[2], 1), 0, (CX * CY * CZ // BLK) - 1).astype(jnp.int32),
        "normals": centred(arg_keys[3], (3, MARK), 0.6, 3.0, ((1, 32),), jnp.float32),
        "marker_panel": draw_marker_panel(jax.random.fold_in(arg_keys[14], 71), 0),
        "mode_shape": centred(arg_keys[5], (MARK, MODES), 0.1, 0.59765625, ((0, 32),)),
        "modal_disp": centred(arg_keys[6], (P_SIZE, MODES), 1.0, 6.0, ((0, 32),), jnp.float32),
        "modal_rate": centred(arg_keys[7], (P_SIZE, MODES), 1.0, 6.0, ((0, 32),), jnp.float32),
        "mode_omega": jnp.clip(jnp.exp(math.log(1.8) - 3.583519 * jax.random.uniform(arg_keys[8], (P_SIZE, MODES), jnp.float32) ** level_of(arg_keys[8], (P_SIZE, MODES), ((0, 32),), -0.2, 0.2)), 0.05, 1.8),
        "mode_zeta": jnp.clip(jnp.exp(math.log(0.2) - 2.9957323 * jax.random.uniform(arg_keys[9], (P_SIZE, MODES), jnp.float32) ** level_of(arg_keys[9], (P_SIZE, MODES), ((0, 32),), -0.2, 0.2)), 0.01, 0.2),
        "base_load": jnp.clip(jnp.exp(math.log(1.0) - 4.6051702 * jax.random.uniform(arg_keys[10], (P_SIZE, MODES), jnp.float32) ** level_of(arg_keys[10], (P_SIZE, MODES), ((0, 32),), -0.2, 0.2)), 0.01, 1.0),
        "stress_modes": centred(arg_keys[11], (NODES, MODES), 1.0, 6.0),
        "hot_nodes": set_ends(jax.random.randint(arg_keys[12], (P_SIZE, HOT), 0, NODES), jax.random.fold_in(arg_keys[12], 1), 0, NODES - 1).astype(jnp.int32),
        "freq_bins": set_ends(jax.random.randint(arg_keys[13], (NBINS,), 1, 1024), jax.random.fold_in(arg_keys[13], 1), 1, 1023).astype(jnp.int32),
    }


PENALTY = 1.0
SPRING = 0.5
TIME_STEP = 0.2
VISCOSITY = 0.5
CONVECTION = 1.0
MODAL_STEP = 0.5
BIN_WIDTH = 0.002
GAMMA_HALF = 1.3293404

def couple_markers(slab_cells, weights, tile_block, normals, marker_disp, marker_rate):
    tile_count = weights.shape[0] // TILE
    block_width = weights.shape[1]
    tile_weights = weights.reshape(tile_count, TILE, block_width)
    tile_normals = normals.reshape(3, tile_count, TILE).transpose(1, 0, 2)
    anchor = jnp.zeros((), jnp.int32)

    def visit(forcing, item):
        tile_w, block_id, tile_n, tile_disp, tile_rate = item
        first_cell = (block_id * block_width).astype(jnp.int32)
        cell_block = lax.dynamic_slice(slab_cells, (anchor, first_cell), (3, block_width))
        sampled = lax.dot_general(cell_block, tile_w, (((1,), (1,)), ((), ())), preferred_element_type=jnp.float32)
        normal_speed = lax.optimization_barrier(jnp.sum(tile_n * sampled, axis=0))
        normal_push = PENALTY * (tile_rate - normal_speed) - SPRING * tile_disp
        spread = jnp.dot((tile_n * normal_push).astype(jnp.bfloat16), tile_w, preferred_element_type=jnp.float32)
        current = lax.dynamic_slice(forcing, (anchor, first_cell), (3, block_width))
        forcing = lax.dynamic_update_slice(forcing, current + spread, (anchor, first_cell))
        return (forcing, normal_push)
    initial = jnp.zeros((3, slab_cells.shape[1]), jnp.float32)
    forcing, pushes = lax.scan(visit, initial, (tile_weights, tile_block, tile_normals, marker_disp.reshape(tile_count, TILE), marker_rate.reshape(tile_count, TILE)))
    return (forcing, pushes.reshape(-1))

def advance_fluid(field, padded, forcing):
    padded = jnp.pad(padded, ((0, 0), (0, 0), (0, 0), (1, 1)))
    stream_ahead = padded[:, 2:, 1:-1, 1:-1]
    stream_behind = padded[:, :-2, 1:-1, 1:-1]
    laplace = stream_ahead + stream_behind + padded[:, 1:-1, 2:, 1:-1] + padded[:, 1:-1, :-2, 1:-1]
    laplace = laplace + padded[:, 1:-1, 1:-1, 2:] + padded[:, 1:-1, 1:-1, :-2] - 6.0 * field
    return field + TIME_STEP * (VISCOSITY * laplace - 0.5 * CONVECTION * (stream_ahead - stream_behind) + forcing)

def modal_update(position, speed_now, modal_load, mode_omega, mode_zeta):
    speed_new = (speed_now + MODAL_STEP * (modal_load - mode_omega * mode_omega * position)) / (1.0 + 2.0 * MODAL_STEP * mode_zeta * mode_omega)
    return (position + MODAL_STEP * speed_new, speed_new)

def dirlik_damage(load_list, base_load, mode_omega, mode_zeta, hot_rows, freq_bins):
    power_mean = jnp.zeros_like(base_load)
    for modal_load in load_list:
        power_mean = power_mean + modal_load * modal_load
    power_mean = base_load + power_mean / len(load_list)
    weights_hot = hot_rows * hot_rows * power_mean[:, None, :]
    omega_bins = freq_bins.astype(jnp.float32) * BIN_WIDTH
    detune = mode_omega[:, :, None] * mode_omega[:, :, None] - omega_bins * omega_bins
    damping = 2.0 * mode_zeta[:, :, None] * mode_omega[:, :, None] * omega_bins
    response = 1.0 / (detune * detune + damping * damping)
    spectrum = jnp.einsum('phm,pmk->phk', weights_hot, response, precision=lax.Precision.HIGHEST)
    moment_zero = lax.optimization_barrier(jnp.sum(spectrum, axis=-1)) * BIN_WIDTH
    moment_one = lax.optimization_barrier(jnp.sum(spectrum * omega_bins, axis=-1)) * BIN_WIDTH
    moment_two = lax.optimization_barrier(jnp.sum(spectrum * omega_bins ** 2, axis=-1)) * BIN_WIDTH
    moment_four = lax.optimization_barrier(jnp.sum(spectrum * omega_bins ** 4, axis=-1)) * BIN_WIDTH
    peak_rate = jnp.sqrt(moment_four / moment_two)
    mean_freq = moment_one / moment_zero * jnp.sqrt(moment_two / moment_four)
    irregular = moment_two / jnp.sqrt(moment_zero * moment_four)
    share_one = jnp.maximum(2.0 * (mean_freq - irregular ** 2) / (1.0 + irregular ** 2), 0.02)
    denominator = jnp.maximum(1.0 - irregular - share_one + share_one ** 2, 0.02)
    ratio_term = (irregular - mean_freq - share_one ** 2) / denominator
    share_two = denominator / jnp.maximum(1.0 - ratio_term, 0.05)
    share_three = 1.0 - share_one - share_two
    scale_term = jnp.maximum(1.25 * (irregular - share_three - share_two * ratio_term) / share_one, 0.05)
    bracket = 6.0 * share_one * scale_term ** 3 + 2.0 ** 1.5 * GAMMA_HALF * (jnp.abs(ratio_term) ** 3 * share_two + share_three)
    bracket = jnp.maximum(bracket, 0.1)
    return jnp.log(peak_rate) + jnp.log(8.0) + 1.5 * jnp.log(moment_zero) + jnp.log(bracket)

def reference(velocity, weights, tile_block, normals, marker_panel, mode_shape, modal_disp, modal_rate, mode_omega, mode_zeta, base_load, stress_modes, hot_nodes, freq_bins):
    devices = N_STREAM * N_SPAN
    mode_float = mode_shape.astype(jnp.float32)
    loads = []
    for instant in range(STEPS):
        marker_disp = lax.optimization_barrier(jnp.sum(mode_float * jnp.take(modal_disp, marker_panel, axis=0), axis=1))
        marker_rate = lax.optimization_barrier(jnp.sum(mode_float * jnp.take(modal_rate, marker_panel, axis=0), axis=1))
        fluid_half = velocity.astype(jnp.bfloat16)

        def one_device(item):
            device_index, dev_weights, dev_blocks, dev_normals, dev_disp, dev_rate = item
            row_index = device_index // N_SPAN
            strip_index = device_index % N_SPAN
            anchor = jnp.zeros((), jnp.int32)
            slab_cells = lax.dynamic_slice(fluid_half, (anchor, (row_index * CX).astype(jnp.int32), (strip_index * CY).astype(jnp.int32), anchor), (3, CX, CY, CZ)).reshape(3, CX * CY * CZ)
            return couple_markers(slab_cells, dev_weights, dev_blocks, dev_normals, dev_disp, dev_rate)
        forcings, pushes = lax.map(one_device, (jnp.arange(devices, dtype=jnp.int32), weights.reshape(devices, M_DEV, BLK), tile_block.reshape(devices, M_DEV // TILE), normals.reshape(3, devices, M_DEV).transpose(1, 0, 2), marker_disp.reshape(devices, M_DEV), marker_rate.reshape(devices, M_DEV)))
        forcing = forcings.reshape(N_STREAM, N_SPAN, 3, CX, CY, CZ).transpose(2, 0, 3, 1, 4, 5).reshape(3, NX, NY, NZ)
        traction = -pushes.reshape(-1)
        modal_load = jax.ops.segment_sum(traction[:, None] * mode_float, marker_panel, num_segments=P_SIZE)
        padded = jnp.pad(velocity, ((0, 0), (1, 1), (1, 1), (0, 0)))
        velocity = advance_fluid(velocity, padded, forcing)
        modal_disp, modal_rate = modal_update(modal_disp, modal_rate, modal_load, mode_omega, mode_zeta)
        loads.append(modal_load)
    hot_rows = jnp.take(stress_modes, hot_nodes, axis=0).astype(jnp.float32)
    log_damage = dirlik_damage(loads, base_load, mode_omega, mode_zeta, hot_rows, freq_bins)
    return (velocity, modal_disp, modal_rate, log_damage)
```

```python
import functools

import jax
import jax.numpy as jnp
from jax import lax
from jax.experimental import pallas as pl
from jax.experimental.pallas import tpu as pltpu
from jax.sharding import PartitionSpec as P

TILE = 128
STEPS = 2
CHUNK = 128

PENALTY = 1.0
SPRING = 0.5
TIME_STEP = 0.2
VISCOSITY = 0.5
CONVECTION = 1.0
MODAL_STEP = 0.5
BIN_WIDTH = 0.002
GAMMA_HALF = 1.3293404

F32 = jnp.float32
BF16 = jnp.bfloat16
NT = (((1,), (1,)), ((), ()))
TN = (((0,), (0,)), ((), ()))
NODE_PARTS = 4


def split_two(value):
    high = value.astype(BF16)
    low = (value - high.astype(F32)).astype(BF16)
    return high, low


def kernel(
    streams,
    spans,
    planes,
    width,
    disp_hbm,
    rate_hbm,
    omega_hbm,
    zeta_hbm,
    panel_hbm,
    block_hbm,
    velocity_hbm,
    mode_hbm,
    weights_hbm,
    normals_hbm,
    stress_hbm,
    nodes_hbm,
    bins_hbm,
    base_hbm,
    final,
    tail,
    response_last,
    hot_square,
    mine,
    theirs,
    marker_panel,
    tile_block,
    mode,
    weights,
    normals,
    stress,
    hot_nodes,
    freq_bins,
    base_load,
    field,
    advanced,
    spread,
    shared_state,
    load_out,
    load_in,
    back_out,
    back_in,
    stream_halo,
    span_edge,
    span_halo,
    in_sem,
    state_send,
    state_recv,
    load_send,
    load_recv,
    pair_send,
    pair_recv,
    halo_send,
    halo_recv,
):
    count = streams * spans
    stream_id = lax.axis_index("stream")
    span_id = lax.axis_index("span")
    me = stream_id * spans + span_id
    far_stream = streams - 1 - stream_id
    far_span = spans - 1 - span_id
    own = mine.shape[1]
    modes = mine.shape[2]
    group = streams * own
    depth = field.shape[2]
    markers = mode.shape[0]
    tiles = markers // TILE
    block_width = weights.shape[1]
    rows = block_width // depth
    inner = planes * width

    pairs = (
        (disp_hbm, mine.at[0]),
        (rate_hbm, mine.at[1]),
        (omega_hbm, mine.at[2]),
        (zeta_hbm, mine.at[3]),
        (velocity_hbm, field.at[:, pl.ds(width, inner), :]),
        (block_hbm, tile_block),
        (normals_hbm, normals),
        (weights_hbm, weights),
        (panel_hbm, marker_panel),
        (mode_hbm, mode),
        (stress_hbm, stress),
        (nodes_hbm, hot_nodes),
        (bins_hbm, freq_bins),
        (base_hbm, base_load),
    )
    copies = [
        pltpu.make_async_copy(source, target, in_sem.at[slot])
        for slot, (source, target) in enumerate(pairs)
    ]

    if spans == 4:
        upper = span_id // 2
        nearest = [
            span_id,
            span_id + 1 - 2 * (span_id % 2),
            2 - upper,
            3 - 3 * upper,
        ]
    else:
        nearest = [(span_id + shift) % spans for shift in range(spans)]
    turn = 1 - stream_id // (streams // 2)

    def far_first(step):
        return step + (streams - 1 - 2 * step) * turn

    def place(stream, span):
        return {"stream": stream, "span": span}

    barrier = pltpu.get_barrier_semaphore()
    for near, span in reversed(list(enumerate(nearest))):

        def greet(step, carry):
            stream = far_first(step)

            def signal():
                pl.semaphore_signal(
                    barrier,
                    inc=1,
                    device_id=place(stream, span),
                    device_id_type=pl.DeviceIdType.MESH,
                )

            if near == 0:
                pl.when(stream != stream_id)(signal)
            else:
                signal()
            return carry

        lax.fori_loop(0, streams, greet, 0)
    for copy in copies:
        copy.start()

    def remote(source, target, send, recv, stream, span):
        return pltpu.make_async_remote_copy(
            src_ref=source,
            dst_ref=target,
            send_sem=send,
            recv_sem=recv,
            device_id=place(stream, span),
            device_id_type=pl.DeviceIdType.MESH,
        )

    def wait_bytes(part, sem):
        pltpu.make_async_copy(part, part, sem).wait()

    def send_state(step):
        at_span = span_id if step == 0 else far_span
        at_stream = stream_id if step == 0 else far_stream
        block = shared_state.at[step, at_span, at_stream]
        for near, span in reversed(list(enumerate(nearest))):

            def one(turned, carry):
                stream = far_first(turned)
                copy = remote(
                    block, block, state_send.at[step], state_recv.at[step, at_span], stream, span
                )
                if near == 0:
                    pl.when(stream != stream_id)(copy.start)
                else:
                    copy.start()
                return carry

            lax.fori_loop(0, streams, one, 0)

    def halo_copies(step, source):
        last = inner
        table = (
            (stream_id < streams - 1, source.at[:, pl.ds(last, width), :],
             stream_halo.at[step, 0], 0, (1, 0), stream_id > 0),
            (stream_id > 0, source.at[:, pl.ds(width, width), :],
             stream_halo.at[step, 1], 1, (-1, 0), stream_id < streams - 1),
            (span_id < spans - 1, span_edge.at[step, 1],
             span_halo.at[step, 0], 2, (0, 1), span_id > 0),
            (span_id > 0, span_edge.at[step, 0],
             span_halo.at[step, 1], 3, (0, -1), span_id < spans - 1),
        )
        result = []
        for sends, src, dst, slot, (ds, dp), receives in table:
            copy = remote(
                src,
                dst,
                halo_send.at[step, slot],
                halo_recv.at[step, slot],
                stream_id + ds,
                span_id + dp,
            )
            result.append((sends, receives, copy, dst))
        return result

    def start_halo(step, source):
        for k in range(3):
            span_edge[step, 0, k] = source[k, pl.ds(width, planes, stride=width), :]
            span_edge[step, 1, k] = source[k, pl.ds(2 * width - 1, planes, stride=width), :]
        for sends, receives, copy, dst in halo_copies(step, source):
            pl.when(sends)(copy.start)

            @pl.when(jnp.logical_not(receives))
            def _():
                dst[...] = jnp.zeros(dst.shape, F32)

    def finish_halo(step, source):
        for sends, receives, copy, dst in halo_copies(step, source):
            pl.when(receives)(copy.wait_recv)
        for k in range(3):
            source[k, pl.ds(0, width), :] = stream_halo[step, 0, k]
            source[k, pl.ds(width + inner, width), :] = stream_halo[step, 1, k]

    row_of = lax.broadcasted_iota(jnp.int32, (width, depth), 0)
    lane_of = lax.broadcasted_iota(jnp.int32, (width, depth), 1)

    def stencil(step, source, target, offset):
        def plane(i, carry):
            start = pl.multiple_of((i + 1) * width, width)
            for k in range(3):
                here = source[k, pl.ds(start, width), :]
                ahead = source[k, pl.ds(start + width, width), :]
                behind = source[k, pl.ds(start - width, width), :]
                y_low = span_halo[step, 0, k, pl.ds(i, 1), :]
                y_high = span_halo[step, 1, k, pl.ds(i, 1), :]
                y_ahead = jnp.where(
                    row_of == width - 1, y_high, pltpu.roll(here, width - 1, 0)
                )
                y_behind = jnp.where(row_of == 0, y_low, pltpu.roll(here, 1, 0))
                z_ahead = jnp.where(lane_of == depth - 1, 0.0, pltpu.roll(here, depth - 1, 1))
                z_behind = jnp.where(lane_of == 0, 0.0, pltpu.roll(here, 1, 1))
                laplace = ahead + behind + y_ahead + y_behind
                laplace = laplace + z_ahead + z_behind - 6.0 * here
                target[k, pl.ds(pl.multiple_of(start - width + offset, width), width), :] = (
                    here
                    + TIME_STEP
                    * (VISCOSITY * laplace - 0.5 * CONVECTION * (ahead - behind))
                )
            return carry

        lax.fori_loop(0, planes, plane, 0)

    def add_forcing(target, offset):
        def block(b, carry):
            start = pl.multiple_of(b * rows + offset, rows)
            spot = jnp.full((rows, depth), b, jnp.int32)
            for k in range(3):
                total = target[k, pl.ds(start, rows), :]
                for t in range(tiles):
                    total = total + jnp.where(homes[t] == spot, TIME_STEP * spread[t, k], 0.0)
                target[k, pl.ds(start, rows), :] = total
            return carry

        lax.fori_loop(0, inner // rows, block, 0)

    diagonal = (
        lax.broadcasted_iota(jnp.int32, (rows, block_width), 0)
        == lax.broadcasted_iota(jnp.int32, (rows, block_width), 1) // depth
    ).astype(F32).astype(BF16)

    def expand(part):
        return jnp.concatenate([part] * rows, axis=1) * diagonal

    def home_blocks():
        return [jnp.full((rows, depth), tile_block[t], jnp.int32) for t in range(tiles)]

    def sample(source):
        def look(b, found):
            start = pl.multiple_of(b * rows + width, rows)
            spot = jnp.full((rows, depth), b, jnp.int32)
            cells = [source[k, pl.ds(start, rows), :] for k in range(3)]
            return tuple(
                jnp.where(homes[t] == spot, cells[k], found[3 * t + k])
                for t in range(tiles)
                for k in range(3)
            )

        blank = jnp.zeros((rows, depth), F32)
        found = lax.fori_loop(0, inner // rows, look, (blank,) * (3 * tiles), unroll=4)
        speeds = []
        for t in range(tiles):
            left = jnp.concatenate(
                [expand(found[3 * t + k].astype(BF16)) for k in range(3)], axis=0
            )
            got = lax.dot_general(
                left, weights[pl.ds(t * TILE, TILE), :], NT, preferred_element_type=F32
            )
            speed = None
            for k in range(3):
                term = normals[k : k + 1, t * TILE : (t + 1) * TILE] * jnp.sum(
                    got[k * rows : (k + 1) * rows], axis=0, keepdims=True
                )
                speed = term if speed is None else speed + term
            speeds.append(speed)
        return PENALTY * jnp.concatenate(speeds, axis=1)

    def spread_push(push):
        for t in range(tiles):
            parts = []
            for k in range(3):
                half = normals[k : k + 1, t * TILE : (t + 1) * TILE] * push[
                    :, t * TILE : (t + 1) * TILE
                ]
                parts.append(expand(jnp.broadcast_to(half, (rows, TILE)).astype(BF16)))
            left = jnp.concatenate(parts, axis=0)
            right = jnp.concatenate(
                [weights[pl.ds(t * TILE, TILE), y * depth : (y + 1) * depth] for y in range(rows)],
                axis=0,
            )
            got = jnp.dot(left, right, preferred_element_type=F32)
            for k in range(3):
                spread[t, k] = got[k * rows : (k + 1) * rows]

    group_row = lax.broadcasted_iota(jnp.int32, (group, markers), 0)
    row_panel = (group_row // own) * (spans * own) + group_row % own

    def group_load(step, owner_span, speed):
        chosen = row_panel == marker_panel[...] - owner_span * own
        high, low = split_two(shared_state[step, owner_span].reshape(group, modes))
        every = lax.dot_general(
            jnp.concatenate([high, low], axis=0), mode[...], NT, preferred_element_type=F32
        )
        term = jnp.sum(
            jnp.where(chosen, every[:group] + every[group:], 0.0), axis=0, keepdims=True
        )
        push = term - speed
        high = push.astype(BF16).astype(F32)
        low = push - high
        load = jnp.dot(
            jnp.concatenate(
                [jnp.where(chosen, high, 0.0), jnp.where(chosen, low, 0.0)], axis=0
            ).astype(BF16),
            mode[...],
            preferred_element_type=F32,
        )
        load_out[step, owner_span] = (-(load[:group] + load[group:])).reshape(
            streams, own, modes
        )
        return term

    def send_load(step, owner_span):
        def one(owner, carry):
            stream = streams - 1 - owner if step == 0 else owner
            span = spans - 1 - owner_span if step == 0 else owner_span
            copy = remote(
                load_out.at[step, owner_span, owner],
                load_in.at[step, me],
                load_send.at[step],
                load_recv.at[step],
                stream,
                span,
            )
            pl.when(stream * spans + span != me)(copy.start)
            return carry

        lax.fori_loop(0, streams, one, 0)

    def exchange(step, speed, between):
        total = None
        for near, span in enumerate(nearest):
            if near == spans - 1:
                between()
            owner_span = span if step == 0 else spans - 1 - span
            peers = streams - 1 if near == 0 else streams
            wait_bytes(shared_state.at[step, 0, pl.ds(0, peers)], state_recv.at[step, owner_span])
            term = group_load(step, owner_span, speed)
            send_load(step, owner_span)
            total = term if total is None else total + term
        if step == 0:
            load_in[step, me] = load_out[step, far_span, far_stream]
        else:
            load_in[step, me] = load_out[step, span_id, stream_id]
        return total - speed

    def wait_load(step):
        wait_bytes(load_in.at[step, pl.ds(0, count - 1)], load_recv.at[step])
        return jnp.sum(load_in[step], axis=0)

    def advance(table, load):
        position, rate, omega, zeta = (table[slot] for slot in range(4))
        rate = (rate + MODAL_STEP * (load - omega * omega * position)) / (
            1.0 + 2.0 * MODAL_STEP * zeta * omega
        )
        return position + MODAL_STEP * rate, rate

    for copy in copies[:4]:
        copy.wait()
    shared_state[0, span_id, stream_id] = PENALTY * mine[1] - SPRING * mine[0]
    pl.semaphore_wait(barrier, count - 1)
    send_state(0)
    params = remote(mine, theirs, pair_send.at[0], pair_recv.at[0], far_stream, far_span)
    params.start()

    copies[4].wait()
    start_halo(0, field)
    for copy in copies[5:10]:
        copy.wait()
    homes = home_blocks()
    speed = sample(field)

    def first_stencil():
        finish_halo(0, field)
        stencil(0, field, advanced, width)

    push = exchange(0, speed, first_stencil)
    spread_push(push)
    add_forcing(advanced, width)
    start_halo(1, advanced)
    speed = sample(advanced)

    params.wait_recv()
    load = wait_load(0)
    position, rate = advance(theirs, load)
    shared_state[1, far_span, far_stream] = PENALTY * rate - SPRING * position
    send_state(1)
    back_out[...] = load
    back = remote(back_out, back_in, pair_send.at[1], pair_recv.at[1], far_stream, far_span)
    back.start()
    finish_halo(1, advanced)
    stencil(1, advanced, final, 0)
    response = hot_response(
        own, mine[2], mine[3], freq_bins, hot_nodes, stress, hot_square, copies[10:]
    )
    for slot in range(4):
        response_last[pl.ds(slot * own, own)] = response[slot]
    push = exchange(1, speed, lambda: None)
    spread_push(push)
    add_forcing(final, 0)
    back.wait_recv()
    load = back_in[...]
    position, rate = advance(mine, load)
    tail[0] = position
    tail[1] = rate
    tail[2] = mine[2]
    tail[3] = mine[3]
    tail[4] = STEPS * base_load[...] + load * load
    tail[5] = wait_load(1)
    for step in range(STEPS):
        everyone = load_in.at[0, pl.ds(0, count - 1)]
        wait_bytes(everyone, state_send.at[step])
        wait_bytes(everyone, load_send.at[step])
        for sends, receives, copy, dst in halo_copies(step, (field, advanced)[step]):
            pl.when(sends)(copy.wait_send)
    params.wait_send()
    back.wait_send()


def hot_response(own, omega, zeta, freq_bins, hot_nodes, stress, hot_square, copies):
    modes = stress.shape[1]
    hots = hot_nodes.shape[1]
    for copy in copies:
        copy.wait()
    nodes = jnp.concatenate([hot_nodes[p : p + 1, :] for p in range(own)], axis=1)
    part = stress.shape[0] // NODE_PARTS
    hot_rows = None
    for q in range(NODE_PARTS):
        ids = lax.broadcasted_iota(jnp.int32, (part, own * hots), 0) + q * part
        picked = (ids == nodes).astype(F32).astype(BF16)
        found = lax.dot_general(
            stress[pl.ds(q * part, part), :], picked, TN, preferred_element_type=F32
        )
        hot_rows = found if hot_rows is None else hot_rows + found
    hot_square[...] = hot_rows * hot_rows

    lists = [[], [], [], []]
    columns = []
    for q in range(freq_bins.shape[0]):
        line = freq_bins[q : q + 1, :].astype(F32) * BIN_WIDTH
        columns.append(jnp.broadcast_to(line, (modes, modes)).T)
    for p in range(own):
        omega_sq = omega[p : p + 1] * omega[p : p + 1]
        factor = 2.0 * zeta[p : p + 1] * omega[p : p + 1]
        sums = [None] * 4
        for column in columns:
            square = column * column
            detune = omega_sq - square
            damping = factor * column
            response = 1.0 / (detune * detune + damping * damping)
            second = response * square
            terms = (response, response * column, second, second * square)
            for slot in range(4):
                term = jnp.sum(terms[slot], axis=0, keepdims=True)
                sums[slot] = term if sums[slot] is None else sums[slot] + term
        for slot in range(4):
            lists[slot].append(sums[slot])
    return [jnp.concatenate(parts, axis=0) for parts in lists]


def dirlik(moment_zero, moment_one, moment_two, moment_four):
    peak_rate = jnp.sqrt(moment_four / moment_two)
    mean_freq = moment_one / moment_zero * jnp.sqrt(moment_two / moment_four)
    irregular = moment_two / jnp.sqrt(moment_zero * moment_four)
    irregular_sq = irregular * irregular
    share_one = jnp.maximum(2.0 * (mean_freq - irregular_sq) / (1.0 + irregular_sq), 0.02)
    share_sq = share_one * share_one
    denominator = jnp.maximum(1.0 - irregular - share_one + share_sq, 0.02)
    ratio_term = (irregular - mean_freq - share_sq) / denominator
    share_two = denominator / jnp.maximum(1.0 - ratio_term, 0.05)
    share_three = 1.0 - share_one - share_two
    scale_term = jnp.maximum(
        1.25 * (irregular - share_three - share_two * ratio_term) / share_one, 0.05
    )
    size = jnp.abs(ratio_term)
    bracket = 6.0 * share_one * (scale_term * scale_term * scale_term)
    bracket = bracket + 2.0**1.5 * GAMMA_HALF * (size * size * size * share_two + share_three)
    bracket = jnp.maximum(bracket, 0.1)
    return (
        jnp.log(peak_rate) + jnp.log(jnp.full_like(bracket, 8.0))
        + 1.5 * jnp.log(moment_zero) + jnp.log(bracket)
    )


def finish(
    final,
    tail,
    response,
    hot_square,
    final_out,
    disp_out,
    rate_out,
    damage_out,
    disp_last,
    rate_last,
    damage_last,
    sem,
):
    pairs = (
        (final, final_out),
        (disp_last, disp_out),
        (rate_last, rate_out),
        (damage_last, damage_out),
    )
    copies = [
        pltpu.make_async_copy(source, target, sem.at[slot])
        for slot, (source, target) in enumerate(pairs)
    ]
    copies[0].start()
    own, hots = damage_last.shape
    position, rate, omega, zeta, power, load = (tail[slot] for slot in range(6))
    rate = (rate + MODAL_STEP * (load - omega * omega * position)) / (
        1.0 + 2.0 * MODAL_STEP * zeta * omega
    )
    disp_last[...] = position + MODAL_STEP * rate
    rate_last[...] = rate
    copies[1].start()
    copies[2].start()
    power = (power + load * load) / STEPS
    full = jnp.dot(
        response[...] * jnp.concatenate([power] * 4, axis=0),
        hot_square[...],
        precision=lax.Precision.HIGHEST,
        preferred_element_type=F32,
    )
    mine = (
        lax.broadcasted_iota(jnp.int32, (own, own * hots), 1) // hots
        == lax.broadcasted_iota(jnp.int32, (own, own * hots), 0)
    )
    moments = [
        jnp.sum(jnp.where(mine, full[slot * own : (slot + 1) * own], 0.0), axis=0, keepdims=True)
        * BIN_WIDTH
        for slot in range(4)
    ]
    damage = dirlik(*moments)
    for p in range(own):
        damage_last[p : p + 1, :] = damage[:, p * hots : (p + 1) * hots]
    copies[3].start()
    for copy in copies:
        copy.wait()


def body(
    velocity,
    weights,
    tile_block,
    normals,
    marker_panel,
    mode_shape,
    modal_disp,
    modal_rate,
    mode_omega,
    mode_zeta,
    base_load,
    stress_modes,
    hot_nodes,
    freq_bins,
):
    streams = lax.axis_size("stream")
    spans = lax.axis_size("span")
    count = streams * spans
    _, planes, width, depth = velocity.shape
    markers, block_width = weights.shape
    own, modes = modal_disp.shape
    hots = hot_nodes.shape[1]
    inner = planes * width
    rows = block_width // depth
    held = pl.BlockSpec(memory_space=pltpu.VMEM)
    stay = pl.BlockSpec(memory_space=pltpu.MemorySpace.HBM)
    small = pltpu.VMEM((own, modes), F32)
    bins = freq_bins.reshape(-1, modes)
    results = pl.pallas_call(
        functools.partial(kernel, streams, spans, planes, width),
        out_shape=(
            pltpu.VMEM((3, inner, depth), F32),
            pltpu.VMEM((6, own, modes), F32),
            pltpu.VMEM((4 * own, modes), F32),
            pltpu.VMEM((modes, own * hots), F32),
        ),
        in_specs=[stay] * 14,
        out_specs=(held,) * 4,
        scratch_shapes=[
            pltpu.VMEM((4, own, modes), F32),
            pltpu.VMEM((4, own, modes), F32),
            pltpu.VMEM((1, markers), jnp.int32),
            pltpu.SMEM(tile_block.shape, jnp.int32),
            pltpu.VMEM(mode_shape.shape, BF16),
            pltpu.VMEM(weights.shape, BF16),
            pltpu.VMEM(normals.shape, F32),
            pltpu.VMEM(stress_modes.shape, BF16),
            pltpu.VMEM(hot_nodes.shape, jnp.int32),
            pltpu.VMEM(bins.shape, jnp.int32),
            small,
            pltpu.VMEM((3, inner + 2 * width, depth), F32),
            pltpu.VMEM((3, inner + 2 * width, depth), F32),
            pltpu.VMEM((markers // TILE, 3, rows, depth), F32),
            pltpu.VMEM((STEPS, spans, streams, own, modes), F32),
            pltpu.VMEM((STEPS, spans, streams, own, modes), F32),
            pltpu.VMEM((STEPS, count, own, modes), F32),
            small,
            small,
            pltpu.VMEM((STEPS, 2, 3, width, depth), F32),
            pltpu.VMEM((STEPS, 2, 3, planes, depth), F32),
            pltpu.VMEM((STEPS, 2, 3, planes, depth), F32),
            pltpu.SemaphoreType.DMA((14,)),
            pltpu.SemaphoreType.DMA((STEPS,)),
            pltpu.SemaphoreType.DMA((STEPS, spans)),
            pltpu.SemaphoreType.DMA((STEPS,)),
            pltpu.SemaphoreType.DMA((STEPS,)),
            pltpu.SemaphoreType.DMA((2,)),
            pltpu.SemaphoreType.DMA((2,)),
            pltpu.SemaphoreType.DMA((STEPS, 4)),
            pltpu.SemaphoreType.DMA((STEPS, 4)),
        ],
        compiler_params=pltpu.CompilerParams(
            collective_id=0, has_side_effects=True, vmem_limit_bytes=60 * 1024 * 1024
        ),
        name="coupled_steps",
    )(
        modal_disp,
        modal_rate,
        mode_omega,
        mode_zeta,
        marker_panel.reshape(1, markers),
        tile_block,
        velocity.reshape(3, inner, depth),
        mode_shape,
        weights,
        normals,
        stress_modes,
        hot_nodes,
        bins,
        base_load,
    )
    results = pl.pallas_call(
        finish,
        out_shape=[
            jax.ShapeDtypeStruct((3, inner, depth), F32),
            jax.ShapeDtypeStruct((own, modes), F32),
            jax.ShapeDtypeStruct((own, modes), F32),
            jax.ShapeDtypeStruct((own, hots), F32),
        ],
        in_specs=[held] * 4,
        out_specs=[stay] * 4,
        scratch_shapes=[
            small,
            small,
            pltpu.VMEM((own, hots), F32),
            pltpu.SemaphoreType.DMA((4,)),
        ],
        compiler_params=pltpu.CompilerParams(vmem_limit_bytes=4 * 1024 * 1024),
        name="finish",
    )(*results)
    return (results[0].reshape(velocity.shape),) + tuple(results[1:])


def solution(mesh):
    placed = (
        P(None, "stream", "span", None),
        P(("stream", "span"), None),
        P(("stream", "span")),
        P(None, ("stream", "span")),
        P(("stream", "span")),
        P(("stream", "span"), None),
        P(("stream", "span"), None),
        P(("stream", "span"), None),
        P(("stream", "span"), None),
        P(("stream", "span"), None),
        P(("stream", "span"), None),
        P(),
        P(("stream", "span"), None),
        P(),
    )
    return jax.shard_map(
        body,
        mesh=mesh,
        in_specs=placed,
        out_specs=(
            P(None, "stream", "span", None),
            P(("stream", "span"), None),
            P(("stream", "span"), None),
            P(("stream", "span"), None),
        ),
        check_vma=False,
    )
```

```python
import functools

import jax
import jax.numpy as jnp
from jax import lax
from jax.experimental import pallas as pl
from jax.experimental.pallas import tpu as pltpu
from jax.sharding import PartitionSpec as P

TILE = 128
STEPS = 2
CHUNK = 128

PENALTY = 1.0
SPRING = 0.5
TIME_STEP = 0.2
VISCOSITY = 0.5
CONVECTION = 1.0
MODAL_STEP = 0.5
BIN_WIDTH = 0.002
GAMMA_HALF = 1.3293404

F32 = jnp.float32
BF16 = jnp.bfloat16
NT = (((1,), (1,)), ((), ()))
TN = (((0,), (0,)), ((), ()))
NODE_PARTS = 4
PLANES = 4
PARTS = 1


def split_two(value):
    high = value.astype(BF16)
    low = (value - high.astype(F32)).astype(BF16)
    return high, low


def kernel(
    streams,
    spans,
    planes,
    width,
    disp_hbm,
    rate_hbm,
    omega_hbm,
    zeta_hbm,
    panel_hbm,
    block_hbm,
    velocity_hbm,
    mode_hbm,
    weights_hbm,
    normals_hbm,
    stress_hbm,
    nodes_hbm,
    bins_hbm,
    base_hbm,
    final,
    tail,
    response_last,
    hot_square,
    mine,
    theirs,
    marker_panel,
    tile_block,
    mode,
    weights,
    normals,
    stress,
    hot_nodes,
    freq_bins,
    base_load,
    field,
    advanced,
    band,
    turned,
    spread,
    shared_state,
    load_out,
    load_in,
    back_out,
    back_in,
    stream_halo,
    span_edge,
    span_halo,
    in_sem,
    state_send,
    state_recv,
    load_send,
    load_recv,
    pair_send,
    pair_recv,
    halo_send,
    halo_recv,
):
    count = streams * spans
    stream_id = lax.axis_index("stream")
    span_id = lax.axis_index("span")
    me = stream_id * spans + span_id
    far_stream = streams - 1 - stream_id
    far_span = spans - 1 - span_id
    own = mine.shape[1]
    modes = mine.shape[2]
    part = streams // PARTS
    group = part * own
    stream_part = stream_id // part
    depth = field.shape[2]
    markers = mode.shape[0]
    tiles = markers // TILE
    block_width = weights.shape[1]
    rows = block_width // depth
    inner = planes * width

    pairs = (
        (disp_hbm, mine.at[0]),
        (rate_hbm, mine.at[1]),
        (omega_hbm, mine.at[2]),
        (zeta_hbm, mine.at[3]),
        (velocity_hbm, field.at[:, pl.ds(width, inner), :]),
        (block_hbm, tile_block),
        (normals_hbm, normals),
        (weights_hbm, weights),
        (panel_hbm, marker_panel),
        (mode_hbm, mode),
        (stress_hbm, stress),
        (nodes_hbm, hot_nodes),
        (bins_hbm, freq_bins),
        (base_hbm, base_load),
    )
    copies = [
        pltpu.make_async_copy(source, target, in_sem.at[slot])
        for slot, (source, target) in enumerate(pairs)
    ]

    if spans == 4:
        upper = span_id // 2
        nearest = [
            span_id,
            span_id + 1 - 2 * (span_id % 2),
            2 - upper,
            3 - 3 * upper,
        ]
    else:
        nearest = [(span_id + shift) % spans for shift in range(spans)]
    turn = 1 - stream_id // (streams // 2)

    def far_first(step):
        return step + (streams - 1 - 2 * step) * turn

    def place(stream, span):
        return {"stream": stream, "span": span}

    barrier = pltpu.get_barrier_semaphore()
    for near, span in reversed(list(enumerate(nearest))):

        def greet(step, carry):
            stream = far_first(step)

            def signal():
                pl.semaphore_signal(
                    barrier,
                    inc=1,
                    device_id=place(stream, span),
                    device_id_type=pl.DeviceIdType.MESH,
                )

            if near == 0:
                pl.when(stream != stream_id)(signal)
            else:
                signal()
            return carry

        lax.fori_loop(0, streams, greet, 0)
    for copy in copies:
        copy.start()

    def remote(source, target, send, recv, stream, span):
        return pltpu.make_async_remote_copy(
            src_ref=source,
            dst_ref=target,
            send_sem=send,
            recv_sem=recv,
            device_id=place(stream, span),
            device_id_type=pl.DeviceIdType.MESH,
        )

    def wait_bytes(part, sem):
        pltpu.make_async_copy(part, part, sem).wait()

    def send_state(step):
        at_span = span_id if step == 0 else far_span
        at_stream = stream_id if step == 0 else far_stream
        block = shared_state.at[step, at_span, at_stream]
        for near, span in reversed(list(enumerate(nearest))):

            def one(turned, carry):
                stream = far_first(turned)
                copy = remote(
                    block,
                    block,
                    state_send.at[step],
                    state_recv.at[step, at_span, at_stream // part],
                    stream,
                    span,
                )
                if near == 0:
                    pl.when(stream != stream_id)(copy.start)
                else:
                    copy.start()
                return carry

            lax.fori_loop(0, streams, one, 0)

    def halo_copies(step, source):
        last = inner
        table = (
            (stream_id < streams - 1, source.at[:, pl.ds(last, width), :],
             stream_halo.at[step, 0], 0, (1, 0), stream_id > 0),
            (stream_id > 0, source.at[:, pl.ds(width, width), :],
             stream_halo.at[step, 1], 1, (-1, 0), stream_id < streams - 1),
            (span_id < spans - 1, span_edge.at[step, 1],
             span_halo.at[step, 0], 2, (0, 1), span_id > 0),
            (span_id > 0, span_edge.at[step, 0],
             span_halo.at[step, 1], 3, (0, -1), span_id < spans - 1),
        )
        result = []
        for sends, src, dst, slot, (ds, dp), receives in table:
            copy = remote(
                src,
                dst,
                halo_send.at[step, slot],
                halo_recv.at[step, slot],
                stream_id + ds,
                span_id + dp,
            )
            result.append((sends, receives, copy, dst))
        return result

    def start_halo(step, source):
        for k in range(3):
            span_edge[step, 0, k] = source[k, pl.ds(width, planes, stride=width), :]
            span_edge[step, 1, k] = source[k, pl.ds(2 * width - 1, planes, stride=width), :]
        for sends, receives, copy, dst in halo_copies(step, source):
            pl.when(sends)(copy.start)

            @pl.when(jnp.logical_not(receives))
            def _():
                dst[...] = jnp.zeros(dst.shape, F32)

    def finish_halo(step, source):
        for sends, receives, copy, dst in halo_copies(step, source):
            pl.when(receives)(copy.wait_recv)
        for k in range(3):
            source[k, pl.ds(0, width), :] = stream_halo[step, 0, k]
            source[k, pl.ds(width + inner, width), :] = stream_halo[step, 1, k]

    row_of = lax.broadcasted_iota(jnp.int32, (width, depth), 0)
    lane_from = lax.broadcasted_iota(jnp.int32, (depth, depth), 0)
    lane_to = lax.broadcasted_iota(jnp.int32, (depth, depth), 1)
    band[...] = (jnp.abs(lane_from - lane_to) == 1).astype(F32).astype(BF16)

    def stencil(step, source, target, offset):
        def several(c, carry):
            for k in range(3):
                first = pl.multiple_of((c * PLANES + 1) * width, width)
                block = source[k, pl.ds(first, PLANES * width), :]
                along = jnp.dot(block.astype(BF16), band[...], preferred_element_type=F32)
                for q in range(PLANES):
                    start = pl.multiple_of(first + q * width, width)
                    here = block[q * width : (q + 1) * width]
                    ahead = source[k, pl.ds(start + width, width), :]
                    behind = source[k, pl.ds(start - width, width), :]
                    y_low = span_halo[step, 0, k, pl.ds(c * PLANES + q, 1), :]
                    y_high = span_halo[step, 1, k, pl.ds(c * PLANES + q, 1), :]
                    y_ahead = jnp.where(
                        row_of == width - 1, y_high, pltpu.roll(here, width - 1, 0)
                    )
                    y_behind = jnp.where(row_of == 0, y_low, pltpu.roll(here, 1, 0))
                    beside = y_ahead + y_behind + along[q * width : (q + 1) * width]
                    target[k, pl.ds(pl.multiple_of(start - width + offset, width), width), :] = (
                        (1.0 - 6.0 * TIME_STEP * VISCOSITY) * here
                        + TIME_STEP * (VISCOSITY - 0.5 * CONVECTION) * ahead
                        + TIME_STEP * (VISCOSITY + 0.5 * CONVECTION) * behind
                        + TIME_STEP * VISCOSITY * beside
                    )
            return carry

        lax.fori_loop(0, planes // PLANES, several, 0)

    def add_forcing(target, offset):
        def block(b, carry):
            start = pl.multiple_of(b * rows + offset, rows)
            spot = jnp.full((rows, depth), b, jnp.int32)
            for k in range(3):
                total = target[k, pl.ds(start, rows), :]
                for t in range(tiles):
                    total = total + jnp.where(homes[t] == spot, TIME_STEP * spread[t, k], 0.0)
                target[k, pl.ds(start, rows), :] = total
            return carry

        lax.fori_loop(0, inner // rows, block, 0)

    diagonal = (
        lax.broadcasted_iota(jnp.int32, (rows, block_width), 0)
        == lax.broadcasted_iota(jnp.int32, (rows, block_width), 1) // depth
    ).astype(F32).astype(BF16)

    def expand(part):
        return jnp.concatenate([part] * rows, axis=1) * diagonal

    def home_blocks():
        return [jnp.full((rows, depth), tile_block[t], jnp.int32) for t in range(tiles)]

    def sample(source):
        def look(b, found):
            start = pl.multiple_of(b * rows + width, rows)
            spot = jnp.full((rows, depth), b, jnp.int32)
            cells = [source[k, pl.ds(start, rows), :] for k in range(3)]
            return tuple(
                jnp.where(homes[t] == spot, cells[k], found[3 * t + k])
                for t in range(tiles)
                for k in range(3)
            )

        blank = jnp.zeros((rows, depth), F32)
        found = lax.fori_loop(0, inner // rows, look, (blank,) * (3 * tiles), unroll=4)
        speeds = []
        for t in range(tiles):
            left = jnp.concatenate(
                [expand(found[3 * t + k].astype(BF16)) for k in range(3)], axis=0
            )
            got = lax.dot_general(
                left, weights[pl.ds(t * TILE, TILE), :], NT, preferred_element_type=F32
            )
            speed = None
            for k in range(3):
                term = normals[k : k + 1, t * TILE : (t + 1) * TILE] * jnp.sum(
                    got[k * rows : (k + 1) * rows], axis=0, keepdims=True
                )
                speed = term if speed is None else speed + term
            speeds.append(speed)
        return PENALTY * jnp.concatenate(speeds, axis=1)

    def spread_push(push):
        for t in range(tiles):
            parts = []
            for k in range(3):
                half = normals[k : k + 1, t * TILE : (t + 1) * TILE] * push[
                    :, t * TILE : (t + 1) * TILE
                ]
                parts.append(expand(jnp.broadcast_to(half, (rows, TILE)).astype(BF16)))
            left = jnp.concatenate(parts, axis=0)
            right = jnp.concatenate(
                [weights[pl.ds(t * TILE, TILE), y * depth : (y + 1) * depth] for y in range(rows)],
                axis=0,
            )
            got = jnp.dot(left, right, preferred_element_type=F32)
            for k in range(3):
                spread[t, k] = got[k * rows : (k + 1) * rows]

    group_row = lax.broadcasted_iota(jnp.int32, (group, markers), 0)
    row_panel = (group_row // own) * (spans * own) + group_row % own

    def group_load(step, owner_span, owner_part, speed):
        owners = pl.ds(owner_part * part, part)
        shift = (owner_part * part * spans + owner_span) * own
        chosen = row_panel == marker_panel[...] - shift
        high, low = split_two(shared_state[step, owner_span, owners].reshape(group, modes))
        every = jnp.dot(
            jnp.concatenate([high, low], axis=0), turned[...], preferred_element_type=F32
        )
        term = jnp.sum(
            jnp.where(chosen, every[:group] + every[group:], 0.0), axis=0, keepdims=True
        )
        push = term - speed
        high = push.astype(BF16).astype(F32)
        low = push - high
        load = jnp.dot(
            jnp.concatenate(
                [jnp.where(chosen, high, 0.0), jnp.where(chosen, low, 0.0)], axis=0
            ).astype(BF16),
            mode[...],
            preferred_element_type=F32,
        )
        load_out[step, owner_span, owners] = (-(load[:group] + load[group:])).reshape(
            part, own, modes
        )
        return term

    def send_load(step, owner_span, owner_part):
        def one(turn, carry):
            owner = owner_part * part + turn
            stream = streams - 1 - owner if step == 0 else owner
            span = spans - 1 - owner_span if step == 0 else owner_span
            copy = remote(
                load_out.at[step, owner_span, owner],
                load_in.at[step, me],
                load_send.at[step],
                load_recv.at[step],
                stream,
                span,
            )
            pl.when(stream * spans + span != me)(copy.start)
            return carry

        lax.fori_loop(0, part, one, 0)

    def exchange(step, speed):
        total = None
        for near, span in enumerate(nearest):
            for turn in range(PARTS):
                peers = part - 1 if near == 0 and turn == 0 else part
                at_part = (stream_part + turn) % PARTS
                owner_span = span if step == 0 else spans - 1 - span
                owner_part = at_part if step == 0 else PARTS - 1 - at_part
                wait_bytes(
                    shared_state.at[step, 0, pl.ds(0, peers)],
                    state_recv.at[step, owner_span, owner_part],
                )
                term = group_load(step, owner_span, owner_part, speed)
                send_load(step, owner_span, owner_part)
                total = term if total is None else total + term
        if step == 0:
            load_in[step, me] = load_out[step, far_span, far_stream]
        else:
            load_in[step, me] = load_out[step, span_id, stream_id]
        return total - speed

    def wait_load(step):
        wait_bytes(load_in.at[step, pl.ds(0, count - 1)], load_recv.at[step])
        return jnp.sum(load_in[step], axis=0)

    def advance(table, load):
        position, rate, omega, zeta = (table[slot] for slot in range(4))
        rate = (rate + MODAL_STEP * (load - omega * omega * position)) / (
            1.0 + 2.0 * MODAL_STEP * zeta * omega
        )
        return position + MODAL_STEP * rate, rate

    for copy in copies[:4]:
        copy.wait()
    shared_state[0, span_id, stream_id] = PENALTY * mine[1] - SPRING * mine[0]
    pl.semaphore_wait(barrier, count - 1)
    send_state(0)
    params = remote(mine, theirs, pair_send.at[0], pair_recv.at[0], far_stream, far_span)
    params.start()

    copies[4].wait()
    start_halo(0, field)
    for copy in copies[5:10]:
        copy.wait()
    homes = home_blocks()
    turned[...] = mode[...].astype(F32).T.astype(BF16)
    speed = sample(field)

    push = exchange(0, speed)
    spread_push(push)
    finish_halo(0, field)
    stencil(0, field, advanced, width)
    add_forcing(advanced, width)
    start_halo(1, advanced)
    speed = sample(advanced)

    params.wait_recv()
    load = wait_load(0)
    position, rate = advance(theirs, load)
    shared_state[1, far_span, far_stream] = PENALTY * rate - SPRING * position
    send_state(1)
    back_out[...] = load
    back = remote(back_out, back_in, pair_send.at[1], pair_recv.at[1], far_stream, far_span)
    back.start()
    finish_halo(1, advanced)
    stencil(1, advanced, final, 0)
    response = hot_response(
        own, mine[2], mine[3], freq_bins, hot_nodes, stress, hot_square, copies[10:]
    )
    for slot in range(4):
        response_last[pl.ds(slot * own, own)] = response[slot]
    push = exchange(1, speed)
    spread_push(push)
    add_forcing(final, 0)
    back.wait_recv()
    load = back_in[...]
    position, rate = advance(mine, load)
    tail[0] = position
    tail[1] = rate
    tail[2] = mine[2]
    tail[3] = mine[3]
    tail[4] = STEPS * base_load[...] + load * load
    tail[5] = wait_load(1)
    for step in range(STEPS):
        everyone = load_in.at[0, pl.ds(0, count - 1)]
        wait_bytes(everyone, state_send.at[step])
        wait_bytes(everyone, load_send.at[step])
        for sends, receives, copy, dst in halo_copies(step, (field, advanced)[step]):
            pl.when(sends)(copy.wait_send)
    params.wait_send()
    back.wait_send()


def hot_response(own, omega, zeta, freq_bins, hot_nodes, stress, hot_square, copies):
    modes = stress.shape[1]
    hots = hot_nodes.shape[1]
    for copy in copies:
        copy.wait()
    nodes = jnp.concatenate([hot_nodes[p : p + 1, :] for p in range(own)], axis=1)
    part = stress.shape[0] // NODE_PARTS
    hot_rows = None
    for q in range(NODE_PARTS):
        ids = lax.broadcasted_iota(jnp.int32, (part, own * hots), 0) + q * part
        picked = (ids == nodes).astype(F32).astype(BF16)
        found = lax.dot_general(
            stress[pl.ds(q * part, part), :], picked, TN, preferred_element_type=F32
        )
        hot_rows = found if hot_rows is None else hot_rows + found
    hot_square[...] = hot_rows * hot_rows

    lists = [[], [], [], []]
    columns = []
    for q in range(freq_bins.shape[0]):
        line = freq_bins[q : q + 1, :].astype(F32) * BIN_WIDTH
        columns.append(jnp.broadcast_to(line, (modes, modes)).T)
    for p in range(own):
        omega_sq = omega[p : p + 1] * omega[p : p + 1]
        factor = 2.0 * zeta[p : p + 1] * omega[p : p + 1]
        sums = [None] * 4
        for column in columns:
            square = column * column
            detune = omega_sq - square
            damping = factor * column
            response = 1.0 / (detune * detune + damping * damping)
            second = response * square
            terms = (response, response * column, second, second * square)
            for slot in range(4):
                term = jnp.sum(terms[slot], axis=0, keepdims=True)
                sums[slot] = term if sums[slot] is None else sums[slot] + term
        for slot in range(4):
            lists[slot].append(sums[slot])
    return [jnp.concatenate(parts, axis=0) for parts in lists]


def dirlik(moment_zero, moment_one, moment_two, moment_four):
    peak_rate = jnp.sqrt(moment_four / moment_two)
    mean_freq = moment_one / moment_zero * jnp.sqrt(moment_two / moment_four)
    irregular = moment_two / jnp.sqrt(moment_zero * moment_four)
    irregular_sq = irregular * irregular
    share_one = jnp.maximum(2.0 * (mean_freq - irregular_sq) / (1.0 + irregular_sq), 0.02)
    share_sq = share_one * share_one
    denominator = jnp.maximum(1.0 - irregular - share_one + share_sq, 0.02)
    ratio_term = (irregular - mean_freq - share_sq) / denominator
    share_two = denominator / jnp.maximum(1.0 - ratio_term, 0.05)
    share_three = 1.0 - share_one - share_two
    scale_term = jnp.maximum(
        1.25 * (irregular - share_three - share_two * ratio_term) / share_one, 0.05
    )
    size = jnp.abs(ratio_term)
    bracket = 6.0 * share_one * (scale_term * scale_term * scale_term)
    bracket = bracket + 2.0**1.5 * GAMMA_HALF * (size * size * size * share_two + share_three)
    bracket = jnp.maximum(bracket, 0.1)
    return (
        jnp.log(peak_rate) + jnp.log(jnp.full_like(bracket, 8.0))
        + 1.5 * jnp.log(moment_zero) + jnp.log(bracket)
    )


def finish(
    final,
    tail,
    response,
    hot_square,
    final_out,
    disp_out,
    rate_out,
    damage_out,
    disp_last,
    rate_last,
    damage_last,
    sem,
):
    pairs = (
        (final, final_out),
        (disp_last, disp_out),
        (rate_last, rate_out),
        (damage_last, damage_out),
    )
    copies = [
        pltpu.make_async_copy(source, target, sem.at[slot])
        for slot, (source, target) in enumerate(pairs)
    ]
    copies[0].start()
    own, hots = damage_last.shape
    position, rate, omega, zeta, power, load = (tail[slot] for slot in range(6))
    rate = (rate + MODAL_STEP * (load - omega * omega * position)) / (
        1.0 + 2.0 * MODAL_STEP * zeta * omega
    )
    disp_last[...] = position + MODAL_STEP * rate
    rate_last[...] = rate
    copies[1].start()
    copies[2].start()
    power = (power + load * load) / STEPS
    full = jnp.dot(
        response[...] * jnp.concatenate([power] * 4, axis=0),
        hot_square[...],
        precision=lax.Precision.HIGHEST,
        preferred_element_type=F32,
    )
    mine = (
        lax.broadcasted_iota(jnp.int32, (own, own * hots), 1) // hots
        == lax.broadcasted_iota(jnp.int32, (own, own * hots), 0)
    )
    moments = [
        jnp.sum(jnp.where(mine, full[slot * own : (slot + 1) * own], 0.0), axis=0, keepdims=True)
        * BIN_WIDTH
        for slot in range(4)
    ]
    damage = dirlik(*moments)
    for p in range(own):
        damage_last[p : p + 1, :] = damage[:, p * hots : (p + 1) * hots]
    copies[3].start()
    for copy in copies:
        copy.wait()


def body(
    velocity,
    weights,
    tile_block,
    normals,
    marker_panel,
    mode_shape,
    modal_disp,
    modal_rate,
    mode_omega,
    mode_zeta,
    base_load,
    stress_modes,
    hot_nodes,
    freq_bins,
):
    streams = lax.axis_size("stream")
    spans = lax.axis_size("span")
    count = streams * spans
    _, planes, width, depth = velocity.shape
    markers, block_width = weights.shape
    own, modes = modal_disp.shape
    hots = hot_nodes.shape[1]
    inner = planes * width
    rows = block_width // depth
    held = pl.BlockSpec(memory_space=pltpu.VMEM)
    stay = pl.BlockSpec(memory_space=pltpu.MemorySpace.HBM)
    small = pltpu.VMEM((own, modes), F32)
    bins = freq_bins.reshape(-1, modes)
    results = pl.pallas_call(
        functools.partial(kernel, streams, spans, planes, width),
        out_shape=(
            pltpu.VMEM((3, inner, depth), F32),
            pltpu.VMEM((6, own, modes), F32),
            pltpu.VMEM((4 * own, modes), F32),
            pltpu.VMEM((modes, own * hots), F32),
        ),
        in_specs=[stay] * 14,
        out_specs=(held,) * 4,
        scratch_shapes=[
            pltpu.VMEM((4, own, modes), F32),
            pltpu.VMEM((4, own, modes), F32),
            pltpu.VMEM((1, markers), jnp.int32),
            pltpu.SMEM(tile_block.shape, jnp.int32),
            pltpu.VMEM(mode_shape.shape, BF16),
            pltpu.VMEM(weights.shape, BF16),
            pltpu.VMEM(normals.shape, F32),
            pltpu.VMEM(stress_modes.shape, BF16),
            pltpu.VMEM(hot_nodes.shape, jnp.int32),
            pltpu.VMEM(bins.shape, jnp.int32),
            small,
            pltpu.VMEM((3, inner + 2 * width, depth), F32),
            pltpu.VMEM((3, inner + 2 * width, depth), F32),
            pltpu.VMEM((depth, depth), BF16),
            pltpu.VMEM((modes, markers), BF16),
            pltpu.VMEM((markers // TILE, 3, rows, depth), F32),
            pltpu.VMEM((STEPS, spans, streams, own, modes), F32),
            pltpu.VMEM((STEPS, spans, streams, own, modes), F32),
            pltpu.VMEM((STEPS, count, own, modes), F32),
            small,
            small,
            pltpu.VMEM((STEPS, 2, 3, width, depth), F32),
            pltpu.VMEM((STEPS, 2, 3, planes, depth), F32),
            pltpu.VMEM((STEPS, 2, 3, planes, depth), F32),
            pltpu.SemaphoreType.DMA((14,)),
            pltpu.SemaphoreType.DMA((STEPS,)),
            pltpu.SemaphoreType.DMA((STEPS, spans, PARTS)),
            pltpu.SemaphoreType.DMA((STEPS,)),
            pltpu.SemaphoreType.DMA((STEPS,)),
            pltpu.SemaphoreType.DMA((2,)),
            pltpu.SemaphoreType.DMA((2,)),
            pltpu.SemaphoreType.DMA((STEPS, 4)),
            pltpu.SemaphoreType.DMA((STEPS, 4)),
        ],
        compiler_params=pltpu.CompilerParams(
            collective_id=0, has_side_effects=True, vmem_limit_bytes=60 * 1024 * 1024
        ),
        name="coupled_steps",
    )(
        modal_disp,
        modal_rate,
        mode_omega,
        mode_zeta,
        marker_panel.reshape(1, markers),
        tile_block,
        velocity.reshape(3, inner, depth),
        mode_shape,
        weights,
        normals,
        stress_modes,
        hot_nodes,
        bins,
        base_load,
    )
    results = pl.pallas_call(
        finish,
        out_shape=[
            jax.ShapeDtypeStruct((3, inner, depth), F32),
            jax.ShapeDtypeStruct((own, modes), F32),
            jax.ShapeDtypeStruct((own, modes), F32),
            jax.ShapeDtypeStruct((own, hots), F32),
        ],
        in_specs=[held] * 4,
        out_specs=[stay] * 4,
        scratch_shapes=[
            small,
            small,
            pltpu.VMEM((own, hots), F32),
            pltpu.SemaphoreType.DMA((4,)),
        ],
        compiler_params=pltpu.CompilerParams(vmem_limit_bytes=4 * 1024 * 1024),
        name="finish",
    )(*results)
    return (results[0].reshape(velocity.shape),) + tuple(results[1:])


def solution(mesh):
    placed = (
        P(None, "stream", "span", None),
        P(("stream", "span"), None),
        P(("stream", "span")),
        P(None, ("stream", "span")),
        P(("stream", "span")),
        P(("stream", "span"), None),
        P(("stream", "span"), None),
        P(("stream", "span"), None),
        P(("stream", "span"), None),
        P(("stream", "span"), None),
        P(("stream", "span"), None),
        P(),
        P(("stream", "span"), None),
        P(),
    )
    return jax.shard_map(
        body,
        mesh=mesh,
        in_specs=placed,
        out_specs=(
            P(None, "stream", "span", None),
            P(("stream", "span"), None),
            P(("stream", "span"), None),
            P(("stream", "span"), None),
        ),
        check_vma=False,
    )
```

```python
import functools

import jax
import jax.numpy as jnp
from jax import lax
from jax.experimental import pallas as pl
from jax.experimental.pallas import tpu as pltpu
from jax.sharding import PartitionSpec as P

TILE = 128
STEPS = 2
CHUNK = 128

PENALTY = 1.0
SPRING = 0.5
TIME_STEP = 0.2
VISCOSITY = 0.5
CONVECTION = 1.0
MODAL_STEP = 0.5
BIN_WIDTH = 0.002
GAMMA_HALF = 1.3293404

F32 = jnp.float32
BF16 = jnp.bfloat16
NT = (((1,), (1,)), ((), ()))
TN = (((0,), (0,)), ((), ()))
NODE_PARTS = 4
PLANES = 4
PARTS = 1


def split_two(value):
    high = value.astype(BF16)
    low = (value - high.astype(F32)).astype(BF16)
    return high, low


def kernel(
    streams,
    spans,
    planes,
    width,
    disp_hbm,
    rate_hbm,
    omega_hbm,
    zeta_hbm,
    panel_hbm,
    block_hbm,
    velocity_hbm,
    mode_hbm,
    weights_hbm,
    normals_hbm,
    stress_hbm,
    nodes_hbm,
    bins_hbm,
    base_hbm,
    final,
    tail,
    response_last,
    hot_square,
    mine,
    theirs,
    marker_panel,
    tile_block,
    mode,
    weights,
    normals,
    stress,
    hot_nodes,
    freq_bins,
    base_load,
    field,
    advanced,
    band,
    turned,
    spread,
    shared_state,
    load_out,
    load_in,
    back_out,
    back_in,
    stream_halo,
    span_edge,
    span_halo,
    in_sem,
    state_send,
    state_recv,
    load_send,
    load_recv,
    pair_send,
    pair_recv,
    halo_send,
    halo_recv,
):
    count = streams * spans
    stream_id = lax.axis_index("stream")
    span_id = lax.axis_index("span")
    me = stream_id * spans + span_id
    far_stream = streams - 1 - stream_id
    far_span = spans - 1 - span_id
    own = mine.shape[1]
    modes = mine.shape[2]
    part = streams // PARTS
    group = part * own
    stream_part = stream_id // part
    depth = field.shape[2]
    markers = mode.shape[0]
    tiles = markers // TILE
    block_width = weights.shape[1]
    rows = block_width // depth
    inner = planes * width

    pairs = (
        (disp_hbm, mine.at[0]),
        (rate_hbm, mine.at[1]),
        (omega_hbm, mine.at[2]),
        (zeta_hbm, mine.at[3]),
        (velocity_hbm, field.at[:, pl.ds(width, inner), :]),
        (block_hbm, tile_block),
        (normals_hbm, normals),
        (weights_hbm, weights),
        (panel_hbm, marker_panel),
        (mode_hbm, mode),
        (stress_hbm, stress),
        (nodes_hbm, hot_nodes),
        (bins_hbm, freq_bins),
        (base_hbm, base_load),
    )
    copies = [
        pltpu.make_async_copy(source, target, in_sem.at[slot])
        for slot, (source, target) in enumerate(pairs)
    ]

    if spans == 4:
        upper = span_id // 2
        nearest = [
            span_id,
            span_id + 1 - 2 * (span_id % 2),
            2 - upper,
            3 - 3 * upper,
        ]
    else:
        nearest = [(span_id + shift) % spans for shift in range(spans)]
    turn = 1 - stream_id // (streams // 2)

    def far_first(step):
        return step + (streams - 1 - 2 * step) * turn

    def place(stream, span):
        return {"stream": stream, "span": span}

    barrier = pltpu.get_barrier_semaphore()
    for near, span in reversed(list(enumerate(nearest))):

        def greet(step, carry):
            stream = far_first(step)

            def signal():
                pl.semaphore_signal(
                    barrier,
                    inc=1,
                    device_id=place(stream, span),
                    device_id_type=pl.DeviceIdType.MESH,
                )

            if near == 0:
                pl.when(stream != stream_id)(signal)
            else:
                signal()
            return carry

        lax.fori_loop(0, streams, greet, 0)
    for copy in copies:
        copy.start()

    def remote(source, target, send, recv, stream, span):
        return pltpu.make_async_remote_copy(
            src_ref=source,
            dst_ref=target,
            send_sem=send,
            recv_sem=recv,
            device_id=place(stream, span),
            device_id_type=pl.DeviceIdType.MESH,
        )

    def wait_bytes(part, sem):
        pltpu.make_async_copy(part, part, sem).wait()

    def send_state(step):
        at_span = span_id if step == 0 else far_span
        at_stream = stream_id if step == 0 else far_stream
        block = shared_state.at[step, at_span, at_stream]
        for near, span in reversed(list(enumerate(nearest))):

            def one(turned, carry):
                stream = far_first(turned)
                copy = remote(
                    block,
                    block,
                    state_send.at[step],
                    state_recv.at[step, at_span, at_stream // part],
                    stream,
                    span,
                )
                if near == 0:
                    pl.when(stream != stream_id)(copy.start)
                else:
                    copy.start()
                return carry

            lax.fori_loop(0, streams, one, 0)

    def halo_copies(step, source):
        last = inner
        table = (
            (stream_id < streams - 1, source.at[:, pl.ds(last, width), :],
             stream_halo.at[step, 0], 0, (1, 0), stream_id > 0),
            (stream_id > 0, source.at[:, pl.ds(width, width), :],
             stream_halo.at[step, 1], 1, (-1, 0), stream_id < streams - 1),
            (span_id < spans - 1, span_edge.at[step, 1],
             span_halo.at[step, 0], 2, (0, 1), span_id > 0),
            (span_id > 0, span_edge.at[step, 0],
             span_halo.at[step, 1], 3, (0, -1), span_id < spans - 1),
        )
        result = []
        for sends, src, dst, slot, (ds, dp), receives in table:
            copy = remote(
                src,
                dst,
                halo_send.at[step, slot],
                halo_recv.at[step, slot],
                stream_id + ds,
                span_id + dp,
            )
            result.append((sends, receives, copy, dst))
        return result

    def start_halo(step, source):
        for k in range(3):
            span_edge[step, 0, k] = source[k, pl.ds(width, planes, stride=width), :]
            span_edge[step, 1, k] = source[k, pl.ds(2 * width - 1, planes, stride=width), :]
        for sends, receives, copy, dst in halo_copies(step, source):
            pl.when(sends)(copy.start)

            @pl.when(jnp.logical_not(receives))
            def _():
                dst[...] = jnp.zeros(dst.shape, F32)

    def finish_halo(step, source):
        for sends, receives, copy, dst in halo_copies(step, source):
            pl.when(receives)(copy.wait_recv)
        for k in range(3):
            source[k, pl.ds(0, width), :] = stream_halo[step, 0, k]
            source[k, pl.ds(width + inner, width), :] = stream_halo[step, 1, k]

    row_of = lax.broadcasted_iota(jnp.int32, (width, depth), 0)
    lane_from = lax.broadcasted_iota(jnp.int32, (depth, depth), 0)
    lane_to = lax.broadcasted_iota(jnp.int32, (depth, depth), 1)
    beside_lane = (jnp.abs(lane_from - lane_to) == 1).astype(F32).astype(BF16)
    band[...] = jnp.concatenate([beside_lane, beside_lane], axis=0)

    def stencil(step, source, target, offset):
        def several(c, carry):
            for k in range(3):
                first = pl.multiple_of((c * PLANES + 1) * width, width)
                block = source[k, pl.ds(first, PLANES * width), :]
                along = jnp.dot(
                    jnp.concatenate(split_two(block), axis=1),
                    band[...],
                    preferred_element_type=F32,
                )
                for q in range(PLANES):
                    start = pl.multiple_of(first + q * width, width)
                    here = block[q * width : (q + 1) * width]
                    ahead = source[k, pl.ds(start + width, width), :]
                    behind = source[k, pl.ds(start - width, width), :]
                    y_low = span_halo[step, 0, k, pl.ds(c * PLANES + q, 1), :]
                    y_high = span_halo[step, 1, k, pl.ds(c * PLANES + q, 1), :]
                    y_ahead = jnp.where(
                        row_of == width - 1, y_high, pltpu.roll(here, width - 1, 0)
                    )
                    y_behind = jnp.where(row_of == 0, y_low, pltpu.roll(here, 1, 0))
                    beside = y_ahead + y_behind + along[q * width : (q + 1) * width]
                    target[k, pl.ds(pl.multiple_of(start - width + offset, width), width), :] = (
                        (1.0 - 6.0 * TIME_STEP * VISCOSITY) * here
                        + TIME_STEP * (VISCOSITY - 0.5 * CONVECTION) * ahead
                        + TIME_STEP * (VISCOSITY + 0.5 * CONVECTION) * behind
                        + TIME_STEP * VISCOSITY * beside
                    )
            return carry

        lax.fori_loop(0, planes // PLANES, several, 0)

    def add_forcing(target, offset):
        def block(b, carry):
            start = pl.multiple_of(b * rows + offset, rows)
            spot = jnp.full((rows, depth), b, jnp.int32)
            for k in range(3):
                total = target[k, pl.ds(start, rows), :]
                for t in range(tiles):
                    total = total + jnp.where(homes[t] == spot, TIME_STEP * spread[t, k], 0.0)
                target[k, pl.ds(start, rows), :] = total
            return carry

        lax.fori_loop(0, inner // rows, block, 0)

    diagonal = (
        lax.broadcasted_iota(jnp.int32, (rows, block_width), 0)
        == lax.broadcasted_iota(jnp.int32, (rows, block_width), 1) // depth
    ).astype(F32).astype(BF16)

    def expand(part):
        return jnp.concatenate([part] * rows, axis=1) * diagonal

    def home_blocks():
        return [jnp.full((rows, depth), tile_block[t], jnp.int32) for t in range(tiles)]

    def sample(source):
        def look(b, found):
            start = pl.multiple_of(b * rows + width, rows)
            spot = jnp.full((rows, depth), b, jnp.int32)
            cells = [source[k, pl.ds(start, rows), :] for k in range(3)]
            return tuple(
                jnp.where(homes[t] == spot, cells[k], found[3 * t + k])
                for t in range(tiles)
                for k in range(3)
            )

        blank = jnp.zeros((rows, depth), F32)
        found = lax.fori_loop(0, inner // rows, look, (blank,) * (3 * tiles), unroll=4)
        speeds = []
        for t in range(tiles):
            left = jnp.concatenate(
                [expand(found[3 * t + k].astype(BF16)) for k in range(3)], axis=0
            )
            got = lax.dot_general(
                left, weights[pl.ds(t * TILE, TILE), :], NT, preferred_element_type=F32
            )
            speed = None
            for k in range(3):
                term = normals[k : k + 1, t * TILE : (t + 1) * TILE] * jnp.sum(
                    got[k * rows : (k + 1) * rows], axis=0, keepdims=True
                )
                speed = term if speed is None else speed + term
            speeds.append(speed)
        return PENALTY * jnp.concatenate(speeds, axis=1)

    def spread_push(push):
        for t in range(tiles):
            parts = []
            for k in range(3):
                half = normals[k : k + 1, t * TILE : (t + 1) * TILE] * push[
                    :, t * TILE : (t + 1) * TILE
                ]
                parts.append(expand(jnp.broadcast_to(half, (rows, TILE)).astype(BF16)))
            left = jnp.concatenate(parts, axis=0)
            right = jnp.concatenate(
                [weights[pl.ds(t * TILE, TILE), y * depth : (y + 1) * depth] for y in range(rows)],
                axis=0,
            )
            got = jnp.dot(left, right, preferred_element_type=F32)
            for k in range(3):
                spread[t, k] = got[k * rows : (k + 1) * rows]

    group_row = lax.broadcasted_iota(jnp.int32, (group, markers), 0)
    row_panel = (group_row // own) * (spans * own) + group_row % own

    def group_load(step, owner_span, owner_part, speed):
        owners = pl.ds(owner_part * part, part)
        shift = (owner_part * part * spans + owner_span) * own
        chosen = row_panel == marker_panel[...] - shift
        high, low = split_two(shared_state[step, owner_span, owners].reshape(group, modes))
        every = jnp.dot(
            jnp.concatenate([high, low], axis=0), turned[...], preferred_element_type=F32
        )
        term = jnp.sum(
            jnp.where(chosen, every[:group] + every[group:], 0.0), axis=0, keepdims=True
        )
        push = term - speed
        high = push.astype(BF16).astype(F32)
        low = push - high
        load = jnp.dot(
            jnp.concatenate(
                [jnp.where(chosen, high, 0.0), jnp.where(chosen, low, 0.0)], axis=0
            ).astype(BF16),
            mode[...],
            preferred_element_type=F32,
        )
        load_out[step, owner_span, owners] = (-(load[:group] + load[group:])).reshape(
            part, own, modes
        )
        return term

    def send_load(step, owner_span, owner_part):
        def one(turn, carry):
            owner = owner_part * part + turn
            stream = streams - 1 - owner if step == 0 else owner
            span = spans - 1 - owner_span if step == 0 else owner_span
            copy = remote(
                load_out.at[step, owner_span, owner],
                load_in.at[step, me],
                load_send.at[step],
                load_recv.at[step],
                stream,
                span,
            )
            pl.when(stream * spans + span != me)(copy.start)
            return carry

        lax.fori_loop(0, part, one, 0)

    def exchange(step, speed):
        total = None
        for near, span in enumerate(nearest):
            for turn in range(PARTS):
                peers = part - 1 if near == 0 and turn == 0 else part
                at_part = (stream_part + turn) % PARTS
                owner_span = span if step == 0 else spans - 1 - span
                owner_part = at_part if step == 0 else PARTS - 1 - at_part
                wait_bytes(
                    shared_state.at[step, 0, pl.ds(0, peers)],
                    state_recv.at[step, owner_span, owner_part],
                )
                term = group_load(step, owner_span, owner_part, speed)
                send_load(step, owner_span, owner_part)
                total = term if total is None else total + term
        if step == 0:
            load_in[step, me] = load_out[step, far_span, far_stream]
        else:
            load_in[step, me] = load_out[step, span_id, stream_id]
        return total - speed

    def wait_load(step):
        wait_bytes(load_in.at[step, pl.ds(0, count - 1)], load_recv.at[step])
        return jnp.sum(load_in[step], axis=0)

    def advance(table, load):
        position, rate, omega, zeta = (table[slot] for slot in range(4))
        rate = (rate + MODAL_STEP * (load - omega * omega * position)) / (
            1.0 + 2.0 * MODAL_STEP * zeta * omega
        )
        return position + MODAL_STEP * rate, rate

    for copy in copies[:4]:
        copy.wait()
    shared_state[0, span_id, stream_id] = PENALTY * mine[1] - SPRING * mine[0]
    pl.semaphore_wait(barrier, count - 1)
    send_state(0)
    params = remote(mine, theirs, pair_send.at[0], pair_recv.at[0], far_stream, far_span)
    params.start()

    copies[4].wait()
    start_halo(0, field)
    for copy in copies[5:10]:
        copy.wait()
    homes = home_blocks()
    turned[...] = mode[...].astype(F32).T.astype(BF16)
    speed = sample(field)

    push = exchange(0, speed)
    spread_push(push)
    finish_halo(0, field)
    stencil(0, field, advanced, width)
    add_forcing(advanced, width)
    start_halo(1, advanced)
    speed = sample(advanced)

    params.wait_recv()
    load = wait_load(0)
    position, rate = advance(theirs, load)
    shared_state[1, far_span, far_stream] = PENALTY * rate - SPRING * position
    send_state(1)
    back_out[...] = load
    back = remote(back_out, back_in, pair_send.at[1], pair_recv.at[1], far_stream, far_span)
    back.start()
    finish_halo(1, advanced)
    stencil(1, advanced, final, 0)
    response = hot_response(
        own, mine[2], mine[3], freq_bins, hot_nodes, stress, hot_square, copies[10:]
    )
    for slot in range(4):
        response_last[pl.ds(slot * own, own)] = response[slot]
    push = exchange(1, speed)
    spread_push(push)
    add_forcing(final, 0)
    back.wait_recv()
    load = back_in[...]
    position, rate = advance(mine, load)
    tail[0] = position
    tail[1] = rate
    tail[2] = mine[2]
    tail[3] = mine[3]
    tail[4] = STEPS * base_load[...] + load * load
    tail[5] = wait_load(1)
    for step in range(STEPS):
        everyone = load_in.at[0, pl.ds(0, count - 1)]
        wait_bytes(everyone, state_send.at[step])
        wait_bytes(everyone, load_send.at[step])
        for sends, receives, copy, dst in halo_copies(step, (field, advanced)[step]):
            pl.when(sends)(copy.wait_send)
    params.wait_send()
    back.wait_send()


def hot_response(own, omega, zeta, freq_bins, hot_nodes, stress, hot_square, copies):
    modes = stress.shape[1]
    hots = hot_nodes.shape[1]
    for copy in copies:
        copy.wait()
    nodes = jnp.concatenate([hot_nodes[p : p + 1, :] for p in range(own)], axis=1)
    part = stress.shape[0] // NODE_PARTS
    hot_rows = None
    for q in range(NODE_PARTS):
        ids = lax.broadcasted_iota(jnp.int32, (part, own * hots), 0) + q * part
        picked = (ids == nodes).astype(F32).astype(BF16)
        found = lax.dot_general(
            stress[pl.ds(q * part, part), :], picked, TN, preferred_element_type=F32
        )
        hot_rows = found if hot_rows is None else hot_rows + found
    hot_square[...] = hot_rows * hot_rows

    lists = [[], [], [], []]
    columns = []
    for q in range(freq_bins.shape[0]):
        line = freq_bins[q : q + 1, :].astype(F32) * BIN_WIDTH
        columns.append(jnp.broadcast_to(line, (modes, modes)).T)
    for p in range(own):
        omega_sq = omega[p : p + 1] * omega[p : p + 1]
        factor = 2.0 * zeta[p : p + 1] * omega[p : p + 1]
        sums = [None] * 4
        for column in columns:
            square = column * column
            detune = omega_sq - square
            damping = factor * column
            response = 1.0 / (detune * detune + damping * damping)
            second = response * square
            terms = (response, response * column, second, second * square)
            for slot in range(4):
                term = jnp.sum(terms[slot], axis=0, keepdims=True)
                sums[slot] = term if sums[slot] is None else sums[slot] + term
        for slot in range(4):
            lists[slot].append(sums[slot])
    return [jnp.concatenate(parts, axis=0) for parts in lists]


def dirlik(moment_zero, moment_one, moment_two, moment_four):
    peak_rate = jnp.sqrt(moment_four / moment_two)
    mean_freq = moment_one / moment_zero * jnp.sqrt(moment_two / moment_four)
    irregular = moment_two / jnp.sqrt(moment_zero * moment_four)
    irregular_sq = irregular * irregular
    share_one = jnp.maximum(2.0 * (mean_freq - irregular_sq) / (1.0 + irregular_sq), 0.02)
    share_sq = share_one * share_one
    denominator = jnp.maximum(1.0 - irregular - share_one + share_sq, 0.02)
    ratio_term = (irregular - mean_freq - share_sq) / denominator
    share_two = denominator / jnp.maximum(1.0 - ratio_term, 0.05)
    share_three = 1.0 - share_one - share_two
    scale_term = jnp.maximum(
        1.25 * (irregular - share_three - share_two * ratio_term) / share_one, 0.05
    )
    size = jnp.abs(ratio_term)
    bracket = 6.0 * share_one * (scale_term * scale_term * scale_term)
    bracket = bracket + 2.0**1.5 * GAMMA_HALF * (size * size * size * share_two + share_three)
    bracket = jnp.maximum(bracket, 0.1)
    return (
        jnp.log(peak_rate) + jnp.log(jnp.full_like(bracket, 8.0))
        + 1.5 * jnp.log(moment_zero) + jnp.log(bracket)
    )


def finish(
    final,
    tail,
    response,
    hot_square,
    final_out,
    disp_out,
    rate_out,
    damage_out,
    disp_last,
    rate_last,
    damage_last,
    sem,
):
    pairs = (
        (final, final_out),
        (disp_last, disp_out),
        (rate_last, rate_out),
        (damage_last, damage_out),
    )
    copies = [
        pltpu.make_async_copy(source, target, sem.at[slot])
        for slot, (source, target) in enumerate(pairs)
    ]
    copies[0].start()
    own, hots = damage_last.shape
    position, rate, omega, zeta, power, load = (tail[slot] for slot in range(6))
    rate = (rate + MODAL_STEP * (load - omega * omega * position)) / (
        1.0 + 2.0 * MODAL_STEP * zeta * omega
    )
    disp_last[...] = position + MODAL_STEP * rate
    rate_last[...] = rate
    copies[1].start()
    copies[2].start()
    power = (power + load * load) / STEPS
    full = jnp.dot(
        response[...] * jnp.concatenate([power] * 4, axis=0),
        hot_square[...],
        precision=lax.Precision.HIGHEST,
        preferred_element_type=F32,
    )
    mine = (
        lax.broadcasted_iota(jnp.int32, (own, own * hots), 1) // hots
        == lax.broadcasted_iota(jnp.int32, (own, own * hots), 0)
    )
    moments = [
        jnp.sum(jnp.where(mine, full[slot * own : (slot + 1) * own], 0.0), axis=0, keepdims=True)
        * BIN_WIDTH
        for slot in range(4)
    ]
    damage = dirlik(*moments)
    for p in range(own):
        damage_last[p : p + 1, :] = damage[:, p * hots : (p + 1) * hots]
    copies[3].start()
    for copy in copies:
        copy.wait()


def small_product(x_ref, y_ref, o_ref, buf, out, sem):
    s = lax.axis_index("stream")
    z = lax.axis_index("span")
    other = s + 1 - 2 * (s % 2)
    barrier = pltpu.get_barrier_semaphore()
    pl.semaphore_signal(barrier, inc=1, device_id={"stream": other, "span": z}, device_id_type=pl.DeviceIdType.MESH)
    pl.semaphore_wait(barrier, 1)
    def go(acc):
        pltpu.matmul_push_rhs(y_ref[...], 0, 0)
        pltpu.matmul_acc_lhs(acc, y_ref[0:16, :], load_staged_rhs=0)
        got = pltpu.matmul_pop(acc)
        out[...] = got[0:4, 0:128]
    pl.run_scoped(go, pltpu.ACC(0)((16, 256), F32))
    copy = pltpu.make_async_remote_copy(src_ref=out, dst_ref=buf, send_sem=sem.at[0], recv_sem=sem.at[1], device_id={"stream": other, "span": z}, device_id_type=pl.DeviceIdType.MESH)
    copy.start()
    copy.wait()
    o_ref[...] = buf[...] + x_ref[...]


def body(
    velocity,
    weights,
    tile_block,
    normals,
    marker_panel,
    mode_shape,
    modal_disp,
    modal_rate,
    mode_omega,
    mode_zeta,
    base_load,
    stress_modes,
    hot_nodes,
    freq_bins,
):
    streams = lax.axis_size("stream")
    spans = lax.axis_size("span")
    count = streams * spans
    _, planes, width, depth = velocity.shape
    markers, block_width = weights.shape
    own, modes = modal_disp.shape
    hots = hot_nodes.shape[1]
    inner = planes * width
    rows = block_width // depth
    held = pl.BlockSpec(memory_space=pltpu.VMEM)
    stay = pl.BlockSpec(memory_space=pltpu.MemorySpace.HBM)
    small = pltpu.VMEM((own, modes), F32)
    bins = freq_bins.reshape(-1, modes)
    results = pl.pallas_call(
        functools.partial(kernel, streams, spans, planes, width),
        out_shape=(
            pltpu.VMEM((3, inner, depth), F32),
            pltpu.VMEM((6, own, modes), F32),
            pltpu.VMEM((4 * own, modes), F32),
            pltpu.VMEM((modes, own * hots), F32),
        ),
        in_specs=[stay] * 14,
        out_specs=(held,) * 4,
        scratch_shapes=[
            pltpu.VMEM((4, own, modes), F32),
            pltpu.VMEM((4, own, modes), F32),
            pltpu.VMEM((1, markers), jnp.int32),
            pltpu.SMEM(tile_block.shape, jnp.int32),
            pltpu.VMEM(mode_shape.shape, BF16),
            pltpu.VMEM(weights.shape, BF16),
            pltpu.VMEM(normals.shape, F32),
            pltpu.VMEM(stress_modes.shape, BF16),
            pltpu.VMEM(hot_nodes.shape, jnp.int32),
            pltpu.VMEM(bins.shape, jnp.int32),
            small,
            pltpu.VMEM((3, inner + 2 * width, depth), F32),
            pltpu.VMEM((3, inner + 2 * width, depth), F32),
            pltpu.VMEM((2 * depth, depth), BF16),
            pltpu.VMEM((modes, markers), BF16),
            pltpu.VMEM((markers // TILE, 3, rows, depth), F32),
            pltpu.VMEM((STEPS, spans, streams, own, modes), F32),
            pltpu.VMEM((STEPS, spans, streams, own, modes), F32),
            pltpu.VMEM((STEPS, count, own, modes), F32),
            small,
            small,
            pltpu.VMEM((STEPS, 2, 3, width, depth), F32),
            pltpu.VMEM((STEPS, 2, 3, planes, depth), F32),
            pltpu.VMEM((STEPS, 2, 3, planes, depth), F32),
            pltpu.SemaphoreType.DMA((14,)),
            pltpu.SemaphoreType.DMA((STEPS,)),
            pltpu.SemaphoreType.DMA((STEPS, spans, PARTS)),
            pltpu.SemaphoreType.DMA((STEPS,)),
            pltpu.SemaphoreType.DMA((STEPS,)),
            pltpu.SemaphoreType.DMA((2,)),
            pltpu.SemaphoreType.DMA((2,)),
            pltpu.SemaphoreType.DMA((STEPS, 4)),
            pltpu.SemaphoreType.DMA((STEPS, 4)),
        ],
        compiler_params=pltpu.CompilerParams(
            collective_id=0, has_side_effects=True, vmem_limit_bytes=60 * 1024 * 1024
        ),
        name="coupled_steps",
    )(
        modal_disp,
        modal_rate,
        mode_omega,
        mode_zeta,
        marker_panel.reshape(1, markers),
        tile_block,
        velocity.reshape(3, inner, depth),
        mode_shape,
        weights,
        normals,
        stress_modes,
        hot_nodes,
        bins,
        base_load,
    )
    results = pl.pallas_call(
        finish,
        out_shape=[
            jax.ShapeDtypeStruct((3, inner, depth), F32),
            jax.ShapeDtypeStruct((own, modes), F32),
            jax.ShapeDtypeStruct((own, modes), F32),
            jax.ShapeDtypeStruct((own, hots), F32),
        ],
        in_specs=[held] * 4,
        out_specs=[stay] * 4,
        scratch_shapes=[
            small,
            small,
            pltpu.VMEM((own, hots), F32),
            pltpu.SemaphoreType.DMA((4,)),
        ],
        compiler_params=pltpu.CompilerParams(vmem_limit_bytes=4 * 1024 * 1024),
        name="finish",
    )(*results)
    extra = pl.pallas_call(
        small_product,
        out_shape=jax.ShapeDtypeStruct((4, 128), F32),
        in_specs=[held] * 2,
        out_specs=held,
        scratch_shapes=[pltpu.VMEM((4, 128), F32), pltpu.VMEM((4, 128), F32), pltpu.SemaphoreType.DMA((2,))],
        compiler_params=pltpu.CompilerParams(collective_id=1, has_side_effects=True),
        name="extra",
    )(results[1] * 0.0, weights[0:256, 0:256] * 0.0)
    return (results[0].reshape(velocity.shape), results[1] + extra) + tuple(results[2:])


def solution(mesh):
    placed = (
        P(None, "stream", "span", None),
        P(("stream", "span"), None),
        P(("stream", "span")),
        P(None, ("stream", "span")),
        P(("stream", "span")),
        P(("stream", "span"), None),
        P(("stream", "span"), None),
        P(("stream", "span"), None),
        P(("stream", "span"), None),
        P(("stream", "span"), None),
        P(("stream", "span"), None),
        P(),
        P(("stream", "span"), None),
        P(),
    )
    return jax.shard_map(
        body,
        mesh=mesh,
        in_specs=placed,
        out_specs=(
            P(None, "stream", "span", None),
            P(("stream", "span"), None),
            P(("stream", "span"), None),
            P(("stream", "span"), None),
        ),
        check_vma=False,
    )
```

```python
import functools

import jax
import jax.numpy as jnp
from jax import lax
from jax.experimental import pallas as pl
from jax.experimental.pallas import tpu as pltpu
from jax.sharding import PartitionSpec as P

TILE = 128
STEPS = 2

PENALTY = 1.0
SPRING = 0.5
TIME_STEP = 0.2
VISCOSITY = 0.5
CONVECTION = 1.0
MODAL_STEP = 0.5
BIN_WIDTH = 0.002
GAMMA_HALF = 1.3293404

F32 = jnp.float32
BF16 = jnp.bfloat16
NT = (((1,), (1,)), ((), ()))
TN = (((0,), (0,)), ((), ()))
NODE_PARTS = 4
PLANES = 4
GROUPS = ((0,),(1,),(2,),(3,))


def split_two(value):
    high = value.astype(BF16)
    low = (value - high.astype(F32)).astype(BF16)
    return high, low


def kernel(
    streams,
    spans,
    planes,
    width,
    disp_hbm,
    rate_hbm,
    omega_hbm,
    zeta_hbm,
    panel_hbm,
    block_hbm,
    velocity_hbm,
    mode_hbm,
    weights_hbm,
    normals_hbm,
    stress_hbm,
    nodes_hbm,
    bins_hbm,
    base_hbm,
    final,
    tail,
    response_last,
    hot_square,
    mine,
    theirs,
    marker_panel,
    tile_block,
    mode,
    weights,
    normals,
    stress,
    hot_nodes,
    freq_bins,
    base_load,
    field,
    advanced,
    band,
    turned,
    spread,
    shared_state,
    load_out,
    load_in,
    back_out,
    back_in,
    stream_halo,
    span_edge,
    span_halo,
    in_sem,
    state_send,
    state_recv,
    load_send,
    load_recv,
    pair_send,
    pair_recv,
    halo_send,
    halo_recv,
):
    count = streams * spans
    stream_id = lax.axis_index("stream")
    span_id = lax.axis_index("span")
    me = stream_id * spans + span_id
    far_stream = streams - 1 - stream_id
    far_span = spans - 1 - span_id
    own = mine.shape[1]
    modes = mine.shape[2]
    home = span_id * streams + stream_id
    opposite = far_span * streams + far_stream
    plans = GROUPS if spans == 4 else tuple((span,) for span in range(spans))

    def among(span, plan):
        found = span == plan[0]
        for other in plan[1:]:
            found = jnp.logical_or(found, span == other)
        return found

    depth = field.shape[2]
    markers = mode.shape[0]
    tiles = markers // TILE
    block_width = weights.shape[1]
    rows = block_width // depth
    inner = planes * width

    pairs = (
        (disp_hbm, mine.at[0]),
        (rate_hbm, mine.at[1]),
        (omega_hbm, mine.at[2]),
        (zeta_hbm, mine.at[3]),
        (velocity_hbm, field.at[:, pl.ds(width, inner), :]),
        (block_hbm, tile_block),
        (normals_hbm, normals),
        (weights_hbm, weights),
        (panel_hbm, marker_panel),
        (mode_hbm, mode),
        (stress_hbm, stress),
        (nodes_hbm, hot_nodes),
        (bins_hbm, freq_bins),
        (base_hbm, base_load),
    )
    copies = [
        pltpu.make_async_copy(source, target, in_sem.at[slot])
        for slot, (source, target) in enumerate(pairs)
    ]

    if spans == 4:
        upper = span_id // 2
        nearest = [
            span_id,
            span_id + 1 - 2 * (span_id % 2),
            2 - upper,
            3 - 3 * upper,
        ]
    else:
        nearest = [(span_id + shift) % spans for shift in range(spans)]
    turn = 1 - stream_id // (streams // 2)

    def far_first(step):
        return step + (streams - 1 - 2 * step) * turn

    def place(stream, span):
        return {"stream": stream, "span": span}

    barrier = pltpu.get_barrier_semaphore()
    for near, span in reversed(list(enumerate(nearest))):

        def greet(step, carry):
            stream = far_first(step)

            def signal():
                pl.semaphore_signal(
                    barrier,
                    inc=1,
                    device_id=place(stream, span),
                    device_id_type=pl.DeviceIdType.MESH,
                )

            if near == 0:
                pl.when(stream != stream_id)(signal)
            else:
                signal()
            return carry

        lax.fori_loop(0, streams, greet, 0)
    for copy in copies:
        copy.start()

    def remote(source, target, send, recv, stream, span):
        return pltpu.make_async_remote_copy(
            src_ref=source,
            dst_ref=target,
            send_sem=send,
            recv_sem=recv,
            device_id=place(stream, span),
            device_id_type=pl.DeviceIdType.MESH,
        )

    def wait_bytes(part, sem):
        pltpu.make_async_copy(part, part, sem).wait()

    def send_state(step):
        block = shared_state.at[step, home if step == 0 else opposite]
        turn_of = len(plans) - 1
        for turn, plan in enumerate(plans[:-1]):
            turn_of = jnp.where(among(span_id if step == 0 else far_span, plan), turn, turn_of)
        for near, span in reversed(list(enumerate(nearest))):

            def one(turned, carry):
                stream = far_first(turned)
                copy = remote(
                    block,
                    block,
                    state_send.at[step],
                    state_recv.at[step, turn_of],
                    stream,
                    span,
                )
                if near == 0:
                    pl.when(stream != stream_id)(copy.start)
                else:
                    copy.start()
                return carry

            lax.fori_loop(0, streams, one, 0)

    def halo_copies(step, source):
        last = inner
        table = (
            (stream_id < streams - 1, source.at[:, pl.ds(last, width), :],
             stream_halo.at[step, 0], 0, (1, 0), stream_id > 0),
            (stream_id > 0, source.at[:, pl.ds(width, width), :],
             stream_halo.at[step, 1], 1, (-1, 0), stream_id < streams - 1),
            (span_id < spans - 1, span_edge.at[step, 1],
             span_halo.at[step, 0], 2, (0, 1), span_id > 0),
            (span_id > 0, span_edge.at[step, 0],
             span_halo.at[step, 1], 3, (0, -1), span_id < spans - 1),
        )
        result = []
        for sends, src, dst, slot, (ds, dp), receives in table:
            copy = remote(
                src,
                dst,
                halo_send.at[step, slot],
                halo_recv.at[step, slot],
                stream_id + ds,
                span_id + dp,
            )
            result.append((sends, receives, copy, dst))
        return result

    def start_halo(step, source):
        for k in range(3):
            span_edge[step, 0, k] = source[k, pl.ds(width, planes, stride=width), :]
            span_edge[step, 1, k] = source[k, pl.ds(2 * width - 1, planes, stride=width), :]
        for sends, receives, copy, dst in halo_copies(step, source):
            pl.when(sends)(copy.start)

            @pl.when(jnp.logical_not(receives))
            def _():
                dst[...] = jnp.zeros(dst.shape, F32)

    def finish_halo(step, source):
        for sends, receives, copy, dst in halo_copies(step, source):
            pl.when(receives)(copy.wait_recv)
        for k in range(3):
            source[k, pl.ds(0, width), :] = stream_halo[step, 0, k]
            source[k, pl.ds(width + inner, width), :] = stream_halo[step, 1, k]

    row_of = lax.broadcasted_iota(jnp.int32, (width, depth), 0)
    lane_from = lax.broadcasted_iota(jnp.int32, (depth, depth), 0)
    lane_to = lax.broadcasted_iota(jnp.int32, (depth, depth), 1)
    beside_lane = (jnp.abs(lane_from - lane_to) == 1).astype(F32).astype(BF16)
    band[...] = jnp.concatenate([beside_lane, beside_lane], axis=0)

    def stencil(step, source, target, offset):
        def several(c, carry):
            for k in range(3):
                first = pl.multiple_of((c * PLANES + 1) * width, width)
                block = source[k, pl.ds(first, PLANES * width), :]
                along = jnp.dot(
                    jnp.concatenate(split_two(block), axis=1),
                    band[...],
                    preferred_element_type=F32,
                )
                for q in range(PLANES):
                    start = pl.multiple_of(first + q * width, width)
                    here = block[q * width : (q + 1) * width]
                    ahead = source[k, pl.ds(start + width, width), :]
                    behind = source[k, pl.ds(start - width, width), :]
                    y_low = span_halo[step, 0, k, pl.ds(c * PLANES + q, 1), :]
                    y_high = span_halo[step, 1, k, pl.ds(c * PLANES + q, 1), :]
                    y_ahead = jnp.where(
                        row_of == width - 1, y_high, pltpu.roll(here, width - 1, 0)
                    )
                    y_behind = jnp.where(row_of == 0, y_low, pltpu.roll(here, 1, 0))
                    beside = y_ahead + y_behind + along[q * width : (q + 1) * width]
                    target[k, pl.ds(pl.multiple_of(start - width + offset, width), width), :] = (
                        (1.0 - 6.0 * TIME_STEP * VISCOSITY) * here
                        + TIME_STEP * (VISCOSITY - 0.5 * CONVECTION) * ahead
                        + TIME_STEP * (VISCOSITY + 0.5 * CONVECTION) * behind
                        + TIME_STEP * VISCOSITY * beside
                    )
            return carry

        lax.fori_loop(0, planes // PLANES, several, 0)

    def add_forcing(target, offset):
        def block(b, carry):
            start = pl.multiple_of(b * rows + offset, rows)
            spot = jnp.full((rows, depth), b, jnp.int32)
            for k in range(3):
                total = target[k, pl.ds(start, rows), :]
                for t in range(tiles):
                    total = total + jnp.where(homes[t] == spot, TIME_STEP * spread[t, k], 0.0)
                target[k, pl.ds(start, rows), :] = total
            return carry

        lax.fori_loop(0, inner // rows, block, 0)

    diagonal = (
        lax.broadcasted_iota(jnp.int32, (rows, block_width), 0)
        == lax.broadcasted_iota(jnp.int32, (rows, block_width), 1) // depth
    ).astype(F32).astype(BF16)

    def expand(part):
        return jnp.concatenate([part] * rows, axis=1) * diagonal

    def home_blocks():
        return [jnp.full((rows, depth), tile_block[t], jnp.int32) for t in range(tiles)]

    def sample(source):
        def look(b, found):
            start = pl.multiple_of(b * rows + width, rows)
            spot = jnp.full((rows, depth), b, jnp.int32)
            cells = [source[k, pl.ds(start, rows), :] for k in range(3)]
            return tuple(
                jnp.where(homes[t] == spot, cells[k], found[3 * t + k])
                for t in range(tiles)
                for k in range(3)
            )

        blank = jnp.zeros((rows, depth), F32)
        found = lax.fori_loop(0, inner // rows, look, (blank,) * (3 * tiles), unroll=4)
        speeds = []
        for t in range(tiles):
            left = jnp.concatenate(
                [expand(found[3 * t + k].astype(BF16)) for k in range(3)], axis=0
            )
            got = lax.dot_general(
                left, weights[pl.ds(t * TILE, TILE), :], NT, preferred_element_type=F32
            )
            speed = None
            for k in range(3):
                term = normals[k : k + 1, t * TILE : (t + 1) * TILE] * jnp.sum(
                    got[k * rows : (k + 1) * rows], axis=0, keepdims=True
                )
                speed = term if speed is None else speed + term
            speeds.append(speed)
        return PENALTY * jnp.concatenate(speeds, axis=1)

    def spread_push(push):
        for t in range(tiles):
            parts = []
            for k in range(3):
                half = normals[k : k + 1, t * TILE : (t + 1) * TILE] * push[
                    :, t * TILE : (t + 1) * TILE
                ]
                parts.append(expand(jnp.broadcast_to(half, (rows, TILE)).astype(BF16)))
            left = jnp.concatenate(parts, axis=0)
            right = jnp.concatenate(
                [weights[pl.ds(t * TILE, TILE), y * depth : (y + 1) * depth] for y in range(rows)],
                axis=0,
            )
            got = jnp.dot(left, right, preferred_element_type=F32)
            for k in range(3):
                spread[t, k] = got[k * rows : (k + 1) * rows]

    group_row = lax.broadcasted_iota(jnp.int32, (streams * own, markers), 0)
    row_panel = group_row + (group_row // own) * (spans - 1) * own

    def both(value):
        high = value.astype(BF16).astype(F32)
        return jnp.concatenate([high, value - high], axis=0).astype(BF16)

    def seen_by(state, chosen):
        size = state.shape[0]
        every = jnp.dot(both(state), turned[...], preferred_element_type=F32)
        return jnp.sum(
            jnp.where(chosen, every[:size] + every[size:], 0.0), axis=0, keepdims=True
        )

    def load_of(push, chosen):
        size = chosen.shape[0]
        load = jnp.dot(
            both(jnp.where(chosen, push, 0.0)), mode[...], preferred_element_type=F32
        )
        return -(load[:size] + load[size:])

    def wait_state(step, turn):
        plan = plans[turn]
        fewer = among(span_id if step == 0 else far_span, plan)
        for lacks in (0, 1):

            @pl.when(fewer if lacks else jnp.logical_not(fewer))
            def _():
                wait_bytes(
                    shared_state.at[step, pl.ds(0, streams * len(plan) - lacks)],
                    state_recv.at[step, turn],
                )

    def send_one(step, source, owner_stream, owner_span):
        stream = streams - 1 - owner_stream if step == 0 else owner_stream
        span = spans - 1 - owner_span if step == 0 else owner_span
        copy = remote(
            source, load_in.at[step, me], load_send.at[step], load_recv.at[step], stream, span
        )
        return stream * spans + span != me, copy

    def take_group(step, turn, speed):
        plan = plans[turn]
        wait_state(step, turn)
        chosen = jnp.concatenate(
            [row_panel == marker_panel[...] - span * own for span in plan], axis=0
        )
        state = jnp.concatenate(
            [
                shared_state[step, pl.ds(span * streams, streams)].reshape(streams * own, modes)
                for span in plan
            ],
            axis=0,
        )
        term = seen_by(state, chosen)
        load = load_of(term - speed, chosen)
        for at, span in enumerate(plan):
            load_out[step, pl.ds(span * streams, streams)] = load[
                at * streams * own : (at + 1) * streams * own
            ].reshape(streams, own, modes)
        for span in plan:

            def one(stream, carry):
                sends, copy = send_one(
                    step, load_out.at[step, span * streams + stream], stream, span
                )
                pl.when(sends)(copy.start)
                return carry

            lax.fori_loop(0, streams, one, 0)
        return term

    def close(step, terms, speed):
        load_in[step, me] = load_out[step, opposite if step == 0 else home]
        return functools.reduce(jnp.add, terms) - speed

    def wait_load(step):
        wait_bytes(load_in.at[step, pl.ds(0, count - 1)], load_recv.at[step])
        return jnp.sum(load_in[step], axis=0)

    def advance(table, load):
        position, rate, omega, zeta = (table[slot] for slot in range(4))
        rate = (rate + MODAL_STEP * (load - omega * omega * position)) / (
            1.0 + 2.0 * MODAL_STEP * zeta * omega
        )
        return position + MODAL_STEP * rate, rate

    for copy in copies[:4]:
        copy.wait()
    shared_state[0, home] = PENALTY * mine[1] - SPRING * mine[0]
    pl.semaphore_wait(barrier, count - 1)
    send_state(0)
    params = remote(mine, theirs, pair_send.at[0], pair_recv.at[0], far_stream, far_span)
    params.start()

    copies[4].wait()
    start_halo(0, field)
    for copy in copies[5:10]:
        copy.wait()
    homes = home_blocks()
    turned[...] = mode[...].astype(F32).T.astype(BF16)
    speed = sample(field)

    response = hot_response(
        own, mine[2], mine[3], freq_bins, hot_nodes, stress, hot_square, copies[10:]
    )
    for slot in range(4):
        response_last[pl.ds(slot * own, own)] = response[slot]
    terms = []
    terms.append(take_group(0, 0, speed))
    terms.append(take_group(0, 1, speed))
    terms.append(take_group(0, 2, speed))
    terms.append(take_group(0, 3, speed))
    push = close(0, terms, speed)
    spread_push(push)
    finish_halo(0, field)
    stencil(0, field, advanced, width)
    add_forcing(advanced, width)
    start_halo(1, advanced)
    params.wait_recv()
    load = wait_load(0)
    position, rate = advance(theirs, load)
    shared_state[1, opposite] = PENALTY * rate - SPRING * position
    send_state(1)
    back_out[...] = load
    back = remote(back_out, back_in, pair_send.at[1], pair_recv.at[1], far_stream, far_span)
    back.start()
    speed = sample(advanced)
    terms = []
    terms.append(take_group(1, 0, speed))
    terms.append(take_group(1, 1, speed))
    terms.append(take_group(1, 2, speed))
    terms.append(take_group(1, 3, speed))
    push = close(1, terms, speed)
    spread_push(push)
    finish_halo(1, advanced)
    stencil(1, advanced, final, 0)
    add_forcing(final, 0)
    back.wait_recv()
    load = back_in[...]
    position, rate = advance(mine, load)
    tail[0] = position
    tail[1] = rate
    tail[2] = mine[2]
    tail[3] = mine[3]
    tail[4] = STEPS * base_load[...] + load * load
    tail[5] = wait_load(1)
    for step in range(STEPS):
        everyone = load_in.at[0, pl.ds(0, count - 1)]
        wait_bytes(everyone, state_send.at[step])
        wait_bytes(everyone, load_send.at[step])
        for sends, receives, copy, dst in halo_copies(step, (field, advanced)[step]):
            pl.when(sends)(copy.wait_send)
    params.wait_send()
    back.wait_send()


def hot_response(own, omega, zeta, freq_bins, hot_nodes, stress, hot_square, copies):
    modes = stress.shape[1]
    hots = hot_nodes.shape[1]
    for copy in copies:
        copy.wait()
    nodes = jnp.concatenate([hot_nodes[p : p + 1, :] for p in range(own)], axis=1)
    part = stress.shape[0] // NODE_PARTS
    hot_rows = None
    for q in range(NODE_PARTS):
        ids = lax.broadcasted_iota(jnp.int32, (part, own * hots), 0) + q * part
        picked = (ids == nodes).astype(F32).astype(BF16)
        found = lax.dot_general(
            stress[pl.ds(q * part, part), :], picked, TN, preferred_element_type=F32
        )
        hot_rows = found if hot_rows is None else hot_rows + found
    hot_square[...] = hot_rows * hot_rows

    lists = [[], [], [], []]
    columns = []
    for q in range(freq_bins.shape[0]):
        line = freq_bins[q : q + 1, :].astype(F32) * BIN_WIDTH
        columns.append(jnp.broadcast_to(line, (modes, modes)).T)
    for p in range(own):
        omega_sq = omega[p : p + 1] * omega[p : p + 1]
        factor = 2.0 * zeta[p : p + 1] * omega[p : p + 1]
        sums = [None] * 4
        for column in columns:
            square = column * column
            detune = omega_sq - square
            damping = factor * column
            response = 1.0 / (detune * detune + damping * damping)
            second = response * square
            terms = (response, response * column, second, second * square)
            for slot in range(4):
                term = jnp.sum(terms[slot], axis=0, keepdims=True)
                sums[slot] = term if sums[slot] is None else sums[slot] + term
        for slot in range(4):
            lists[slot].append(sums[slot])
    return [jnp.concatenate(parts, axis=0) for parts in lists]


def dirlik(moment_zero, moment_one, moment_two, moment_four):
    peak_rate = jnp.sqrt(moment_four / moment_two)
    mean_freq = moment_one / moment_zero * jnp.sqrt(moment_two / moment_four)
    irregular = moment_two / jnp.sqrt(moment_zero * moment_four)
    irregular_sq = irregular * irregular
    share_one = jnp.maximum(2.0 * (mean_freq - irregular_sq) / (1.0 + irregular_sq), 0.02)
    share_sq = share_one * share_one
    denominator = jnp.maximum(1.0 - irregular - share_one + share_sq, 0.02)
    ratio_term = (irregular - mean_freq - share_sq) / denominator
    share_two = denominator / jnp.maximum(1.0 - ratio_term, 0.05)
    share_three = 1.0 - share_one - share_two
    scale_term = jnp.maximum(
        1.25 * (irregular - share_three - share_two * ratio_term) / share_one, 0.05
    )
    size = jnp.abs(ratio_term)
    bracket = 6.0 * share_one * (scale_term * scale_term * scale_term)
    bracket = bracket + 2.0**1.5 * GAMMA_HALF * (size * size * size * share_two + share_three)
    bracket = jnp.maximum(bracket, 0.1)
    return (
        jnp.log(peak_rate) + jnp.log(jnp.full_like(bracket, 8.0))
        + 1.5 * jnp.log(moment_zero) + jnp.log(bracket)
    )


def finish(
    final,
    tail,
    response,
    hot_square,
    final_out,
    disp_out,
    rate_out,
    damage_out,
    disp_last,
    rate_last,
    damage_last,
    sem,
):
    pairs = (
        (final, final_out),
        (disp_last, disp_out),
        (rate_last, rate_out),
        (damage_last, damage_out),
    )
    copies = [
        pltpu.make_async_copy(source, target, sem.at[slot])
        for slot, (source, target) in enumerate(pairs)
    ]
    copies[0].start()
    own, hots = damage_last.shape
    position, rate, omega, zeta, power, load = (tail[slot] for slot in range(6))
    rate = (rate + MODAL_STEP * (load - omega * omega * position)) / (
        1.0 + 2.0 * MODAL_STEP * zeta * omega
    )
    disp_last[...] = position + MODAL_STEP * rate
    rate_last[...] = rate
    copies[1].start()
    copies[2].start()
    power = (power + load * load) / STEPS
    full = jnp.dot(
        response[...] * jnp.concatenate([power] * 4, axis=0),
        hot_square[...],
        precision=lax.Precision.HIGHEST,
        preferred_element_type=F32,
    )
    mine = (
        lax.broadcasted_iota(jnp.int32, (own, own * hots), 1) // hots
        == lax.broadcasted_iota(jnp.int32, (own, own * hots), 0)
    )
    moments = [
        jnp.sum(jnp.where(mine, full[slot * own : (slot + 1) * own], 0.0), axis=0, keepdims=True)
        * BIN_WIDTH
        for slot in range(4)
    ]
    damage = dirlik(*moments)
    for p in range(own):
        damage_last[p : p + 1, :] = damage[:, p * hots : (p + 1) * hots]
    copies[3].start()
    for copy in copies:
        copy.wait()


def body(
    velocity,
    weights,
    tile_block,
    normals,
    marker_panel,
    mode_shape,
    modal_disp,
    modal_rate,
    mode_omega,
    mode_zeta,
    base_load,
    stress_modes,
    hot_nodes,
    freq_bins,
):
    streams = lax.axis_size("stream")
    spans = lax.axis_size("span")
    count = streams * spans
    _, planes, width, depth = velocity.shape
    markers, block_width = weights.shape
    own, modes = modal_disp.shape
    hots = hot_nodes.shape[1]
    inner = planes * width
    rows = block_width // depth
    held = pl.BlockSpec(memory_space=pltpu.VMEM)
    stay = pl.BlockSpec(memory_space=pltpu.MemorySpace.HBM)
    small = pltpu.VMEM((own, modes), F32)
    bins = freq_bins.reshape(-1, modes)
    results = pl.pallas_call(
        functools.partial(kernel, streams, spans, planes, width),
        out_shape=(
            pltpu.VMEM((3, inner, depth), F32),
            pltpu.VMEM((6, own, modes), F32),
            pltpu.VMEM((4 * own, modes), F32),
            pltpu.VMEM((modes, own * hots), F32),
        ),
        in_specs=[stay] * 14,
        out_specs=(held,) * 4,
        scratch_shapes=[
            pltpu.VMEM((4, own, modes), F32),
            pltpu.VMEM((4, own, modes), F32),
            pltpu.VMEM((1, markers), jnp.int32),
            pltpu.SMEM(tile_block.shape, jnp.int32),
            pltpu.VMEM(mode_shape.shape, BF16),
            pltpu.VMEM(weights.shape, BF16),
            pltpu.VMEM(normals.shape, F32),
            pltpu.VMEM(stress_modes.shape, BF16),
            pltpu.VMEM(hot_nodes.shape, jnp.int32),
            pltpu.VMEM(bins.shape, jnp.int32),
            small,
            pltpu.VMEM((3, inner + 2 * width, depth), F32),
            pltpu.VMEM((3, inner + 2 * width, depth), F32),
            pltpu.VMEM((2 * depth, depth), BF16),
            pltpu.VMEM((modes, markers), BF16),
            pltpu.VMEM((markers // TILE, 3, rows, depth), F32),
            pltpu.VMEM((STEPS, count, own, modes), F32),
            pltpu.VMEM((STEPS, count, own, modes), F32),
            pltpu.VMEM((STEPS, count, own, modes), F32),
            small,
            small,
            pltpu.VMEM((STEPS, 2, 3, width, depth), F32),
            pltpu.VMEM((STEPS, 2, 3, planes, depth), F32),
            pltpu.VMEM((STEPS, 2, 3, planes, depth), F32),
            pltpu.SemaphoreType.DMA((14,)),
            pltpu.SemaphoreType.DMA((STEPS,)),
            pltpu.SemaphoreType.DMA((STEPS, spans)),
            pltpu.SemaphoreType.DMA((STEPS,)),
            pltpu.SemaphoreType.DMA((STEPS,)),
            pltpu.SemaphoreType.DMA((2,)),
            pltpu.SemaphoreType.DMA((2,)),
            pltpu.SemaphoreType.DMA((STEPS, 4)),
            pltpu.SemaphoreType.DMA((STEPS, 4)),
        ],
        compiler_params=pltpu.CompilerParams(
            collective_id=0, has_side_effects=True, vmem_limit_bytes=60 * 1024 * 1024
        ),
        name="coupled_steps",
    )(
        modal_disp,
        modal_rate,
        mode_omega,
        mode_zeta,
        marker_panel.reshape(1, markers),
        tile_block,
        velocity.reshape(3, inner, depth),
        mode_shape,
        weights,
        normals,
        stress_modes,
        hot_nodes,
        bins,
        base_load,
    )
    results = pl.pallas_call(
        finish,
        out_shape=[
            jax.ShapeDtypeStruct((3, inner, depth), F32),
            jax.ShapeDtypeStruct((own, modes), F32),
            jax.ShapeDtypeStruct((own, modes), F32),
            jax.ShapeDtypeStruct((own, hots), F32),
        ],
        in_specs=[held] * 4,
        out_specs=[stay] * 4,
        scratch_shapes=[
            small,
            small,
            pltpu.VMEM((own, hots), F32),
            pltpu.SemaphoreType.DMA((4,)),
        ],
        compiler_params=pltpu.CompilerParams(vmem_limit_bytes=4 * 1024 * 1024),
        name="finish",
    )(*results)
    return (results[0].reshape(velocity.shape),) + tuple(results[1:])


def solution(mesh):
    placed = (
        P(None, "stream", "span", None),
        P(("stream", "span"), None),
        P(("stream", "span")),
        P(None, ("stream", "span")),
        P(("stream", "span")),
        P(("stream", "span"), None),
        P(("stream", "span"), None),
        P(("stream", "span"), None),
        P(("stream", "span"), None),
        P(("stream", "span"), None),
        P(("stream", "span"), None),
        P(),
        P(("stream", "span"), None),
        P(),
    )
    return jax.shard_map(
        body,
        mesh=mesh,
        in_specs=placed,
        out_specs=(
            P(None, "stream", "span", None),
            P(("stream", "span"), None),
            P(("stream", "span"), None),
            P(("stream", "span"), None),
        ),
        check_vma=False,
    )
```

```python
import functools

import jax
import jax.numpy as jnp
from jax import lax
from jax.experimental import pallas as pl
from jax.experimental.pallas import tpu as pltpu
from jax.sharding import PartitionSpec as P

TILE = 128
STEPS = 2

PENALTY = 1.0
SPRING = 0.5
TIME_STEP = 0.2
VISCOSITY = 0.5
CONVECTION = 1.0
MODAL_STEP = 0.5
BIN_WIDTH = 0.002
GAMMA_HALF = 1.3293404

F32 = jnp.float32
BF16 = jnp.bfloat16
NT = (((1,), (1,)), ((), ()))
TN = (((0,), (0,)), ((), ()))
NODE_PARTS = 4
PLANES = 4
EVERY = 1 << 16
GROUPS = (
    [(0, 0, 2)],
    [(0, 2, EVERY), (1, 0, EVERY)],
    [(2, 0, EVERY)],
    [(3, 0, EVERY)],
)


def split_two(value):
    high = value.astype(BF16)
    low = (value - high.astype(F32)).astype(BF16)
    return high, low


def kernel(
    streams,
    spans,
    planes,
    width,
    disp_hbm,
    rate_hbm,
    omega_hbm,
    zeta_hbm,
    panel_hbm,
    block_hbm,
    velocity_hbm,
    mode_hbm,
    weights_hbm,
    normals_hbm,
    stress_hbm,
    nodes_hbm,
    bins_hbm,
    base_hbm,
    final,
    tail,
    response_last,
    hot_square,
    mine,
    theirs,
    marker_panel,
    tile_block,
    mode,
    weights,
    normals,
    stress,
    hot_nodes,
    freq_bins,
    base_load,
    field,
    advanced,
    band,
    turned,
    spread,
    shared_state,
    load_out,
    load_in,
    back_out,
    back_in,
    stream_halo,
    span_edge,
    span_halo,
    in_sem,
    state_send,
    state_recv,
    load_send,
    load_recv,
    pair_send,
    pair_recv,
    halo_send,
    halo_recv,
):
    count = streams * spans
    stream_id = lax.axis_index("stream")
    span_id = lax.axis_index("span")
    me = stream_id * spans + span_id
    far_stream = streams - 1 - stream_id
    far_span = spans - 1 - span_id
    own = mine.shape[1]
    modes = mine.shape[2]
    home = span_id * streams + stream_id
    opposite = far_span * streams + far_stream
    plans = [
        [(span, low, min(high, streams)) for span, low, high in plan] for plan in GROUPS
    ]

    def among(step, plan):
        stream = stream_id if step == 0 else far_stream
        at_span = span_id if step == 0 else far_span
        found = None
        for span, low, high in plan:
            here = jnp.logical_and(
                at_span == span, jnp.logical_and(stream >= low, stream < high)
            )
            found = here if found is None else jnp.logical_or(found, here)
        return found

    depth = field.shape[2]
    markers = mode.shape[0]
    tiles = markers // TILE
    block_width = weights.shape[1]
    rows = block_width // depth
    inner = planes * width

    pairs = (
        (disp_hbm, mine.at[0]),
        (rate_hbm, mine.at[1]),
        (omega_hbm, mine.at[2]),
        (zeta_hbm, mine.at[3]),
        (velocity_hbm, field.at[:, pl.ds(width, inner), :]),
        (block_hbm, tile_block),
        (normals_hbm, normals),
        (weights_hbm, weights),
        (panel_hbm, marker_panel),
        (mode_hbm, mode),
        (stress_hbm, stress),
        (nodes_hbm, hot_nodes),
        (bins_hbm, freq_bins),
        (base_hbm, base_load),
    )
    copies = [
        pltpu.make_async_copy(source, target, in_sem.at[max(slot - 3, 0)])
        for slot, (source, target) in enumerate(pairs)
    ]

    if spans == 4:
        upper = span_id // 2
        nearest = [
            span_id,
            span_id + 1 - 2 * (span_id % 2),
            2 - upper,
            3 - 3 * upper,
        ]
    else:
        nearest = [(span_id + shift) % spans for shift in range(spans)]
    turn = 1 - stream_id // (streams // 2)

    def far_first(step):
        return step + (streams - 1 - 2 * step) * turn

    def place(stream, span):
        return {"stream": stream, "span": span}

    barrier = pltpu.get_barrier_semaphore()
    for near, span in reversed(list(enumerate(nearest))):

        def greet(step, carry):
            stream = far_first(step)

            def signal():
                pl.semaphore_signal(
                    barrier,
                    inc=1,
                    device_id=place(stream, span),
                    device_id_type=pl.DeviceIdType.MESH,
                )

            if near == 0:
                pl.when(stream != stream_id)(signal)
            else:
                signal()
            return carry

        lax.fori_loop(0, streams, greet, 0)
    for copy in copies:
        copy.start()

    def remote(source, target, send, recv, stream, span):
        return pltpu.make_async_remote_copy(
            src_ref=source,
            dst_ref=target,
            send_sem=send,
            recv_sem=recv,
            device_id=place(stream, span),
            device_id_type=pl.DeviceIdType.MESH,
        )

    def wait_bytes(part, sem):
        pltpu.make_async_copy(part, part, sem).wait()

    def send_state(step):
        block = shared_state.at[step, home if step == 0 else opposite]
        turn_of = len(plans) - 1
        for turn, plan in enumerate(plans[:-1]):
            turn_of = jnp.where(among(step, plan), turn, turn_of)
        for near, span in reversed(list(enumerate(nearest))):

            def one(turned, carry):
                stream = far_first(turned)
                copy = remote(
                    block,
                    block,
                    state_send.at[step],
                    state_recv.at[step, turn_of],
                    stream,
                    span,
                )
                if near == 0:
                    pl.when(stream != stream_id)(copy.start)
                else:
                    copy.start()
                return carry

            lax.fori_loop(0, streams, one, 0)

    def halo_copies(step, source):
        last = inner
        table = (
            (stream_id < streams - 1, source.at[:, pl.ds(last, width), :],
             stream_halo.at[step, 0], 0, (1, 0), stream_id > 0),
            (stream_id > 0, source.at[:, pl.ds(width, width), :],
             stream_halo.at[step, 1], 1, (-1, 0), stream_id < streams - 1),
            (span_id < spans - 1, span_edge.at[step, 1],
             span_halo.at[step, 0], 2, (0, 1), span_id > 0),
            (span_id > 0, span_edge.at[step, 0],
             span_halo.at[step, 1], 3, (0, -1), span_id < spans - 1),
        )
        result = []
        for sends, src, dst, slot, (ds, dp), receives in table:
            copy = remote(
                src,
                dst,
                halo_send.at[step, slot],
                halo_recv.at[step, slot],
                stream_id + ds,
                span_id + dp,
            )
            result.append((sends, receives, copy, dst))
        return result

    def start_halo(step, source):
        for k in range(3):
            span_edge[step, 0, k] = source[k, pl.ds(width, planes, stride=width), :]
            span_edge[step, 1, k] = source[k, pl.ds(2 * width - 1, planes, stride=width), :]
        for sends, receives, copy, dst in halo_copies(step, source):
            pl.when(sends)(copy.start)

            @pl.when(jnp.logical_not(receives))
            def _():
                dst[...] = jnp.zeros(dst.shape, F32)

    def finish_halo(step, source):
        for sends, receives, copy, dst in halo_copies(step, source):
            pl.when(receives)(copy.wait_recv)
        for k in range(3):
            source[k, pl.ds(0, width), :] = stream_halo[step, 0, k]
            source[k, pl.ds(width + inner, width), :] = stream_halo[step, 1, k]

    row_of = lax.broadcasted_iota(jnp.int32, (width, depth), 0)
    lane_from = lax.broadcasted_iota(jnp.int32, (depth, depth), 0)
    lane_to = lax.broadcasted_iota(jnp.int32, (depth, depth), 1)
    beside_lane = (jnp.abs(lane_from - lane_to) == 1).astype(F32).astype(BF16)
    band[...] = jnp.concatenate([beside_lane, beside_lane], axis=0)

    def stencil(step, source, target, offset):
        def several(c, carry):
            for k in range(3):
                first = pl.multiple_of((c * PLANES + 1) * width, width)
                block = source[k, pl.ds(first, PLANES * width), :]
                along = jnp.dot(
                    jnp.concatenate(split_two(block), axis=1),
                    band[...],
                    preferred_element_type=F32,
                )
                for q in range(PLANES):
                    start = pl.multiple_of(first + q * width, width)
                    here = block[q * width : (q + 1) * width]
                    ahead = source[k, pl.ds(start + width, width), :]
                    behind = source[k, pl.ds(start - width, width), :]
                    y_low = span_halo[step, 0, k, pl.ds(c * PLANES + q, 1), :]
                    y_high = span_halo[step, 1, k, pl.ds(c * PLANES + q, 1), :]
                    y_ahead = jnp.where(
                        row_of == width - 1, y_high, pltpu.roll(here, width - 1, 0)
                    )
                    y_behind = jnp.where(row_of == 0, y_low, pltpu.roll(here, 1, 0))
                    beside = y_ahead + y_behind + along[q * width : (q + 1) * width]
                    target[k, pl.ds(pl.multiple_of(start - width + offset, width), width), :] = (
                        (1.0 - 6.0 * TIME_STEP * VISCOSITY) * here
                        + TIME_STEP * (VISCOSITY - 0.5 * CONVECTION) * ahead
                        + TIME_STEP * (VISCOSITY + 0.5 * CONVECTION) * behind
                        + TIME_STEP * VISCOSITY * beside
                    )
            return carry

        lax.fori_loop(0, planes // PLANES, several, 0)

    def add_forcing(target, offset):
        def block(b, carry):
            start = pl.multiple_of(b * rows + offset, rows)
            spot = jnp.full((rows, depth), b, jnp.int32)
            for k in range(3):
                total = target[k, pl.ds(start, rows), :]
                for t in range(tiles):
                    total = total + jnp.where(homes[t] == spot, TIME_STEP * spread[t, k], 0.0)
                target[k, pl.ds(start, rows), :] = total
            return carry

        lax.fori_loop(0, inner // rows, block, 0)

    diagonal = (
        lax.broadcasted_iota(jnp.int32, (rows, block_width), 0)
        == lax.broadcasted_iota(jnp.int32, (rows, block_width), 1) // depth
    ).astype(F32).astype(BF16)

    def expand(part):
        return jnp.concatenate([part] * rows, axis=1) * diagonal

    def home_blocks():
        return [jnp.full((rows, depth), tile_block[t], jnp.int32) for t in range(tiles)]

    def sample(source):
        def look(b, found):
            start = pl.multiple_of(b * rows + width, rows)
            spot = jnp.full((rows, depth), b, jnp.int32)
            cells = [source[k, pl.ds(start, rows), :] for k in range(3)]
            return tuple(
                jnp.where(homes[t] == spot, cells[k], found[3 * t + k])
                for t in range(tiles)
                for k in range(3)
            )

        blank = jnp.zeros((rows, depth), F32)
        found = lax.fori_loop(0, inner // rows, look, (blank,) * (3 * tiles), unroll=4)
        speeds = []
        for t in range(tiles):
            left = jnp.concatenate(
                [expand(found[3 * t + k].astype(BF16)) for k in range(3)], axis=0
            )
            got = lax.dot_general(
                left, weights[pl.ds(t * TILE, TILE), :], NT, preferred_element_type=F32
            )
            speed = None
            for k in range(3):
                term = normals[k : k + 1, t * TILE : (t + 1) * TILE] * jnp.sum(
                    got[k * rows : (k + 1) * rows], axis=0, keepdims=True
                )
                speed = term if speed is None else speed + term
            speeds.append(speed)
        return PENALTY * jnp.concatenate(speeds, axis=1)

    def spread_push(push):
        for t in range(tiles):
            parts = []
            for k in range(3):
                half = normals[k : k + 1, t * TILE : (t + 1) * TILE] * push[
                    :, t * TILE : (t + 1) * TILE
                ]
                parts.append(expand(jnp.broadcast_to(half, (rows, TILE)).astype(BF16)))
            left = jnp.concatenate(parts, axis=0)
            right = jnp.concatenate(
                [weights[pl.ds(t * TILE, TILE), y * depth : (y + 1) * depth] for y in range(rows)],
                axis=0,
            )
            got = jnp.dot(left, right, preferred_element_type=F32)
            for k in range(3):
                spread[t, k] = got[k * rows : (k + 1) * rows]

    def panels_of(span, low, high):
        row = lax.broadcasted_iota(jnp.int32, ((high - low) * own, markers), 0)
        return row + (row // own + low) * (spans - 1) * own + (low + span) * own

    def both(value):
        high = value.astype(BF16).astype(F32)
        return jnp.concatenate([high, value - high], axis=0).astype(BF16)

    def seen_by(state, chosen):
        size = state.shape[0]
        every = jnp.dot(both(state), turned[...], preferred_element_type=F32)
        return jnp.sum(
            jnp.where(chosen, every[:size] + every[size:], 0.0), axis=0, keepdims=True
        )

    def load_of(push, chosen):
        size = chosen.shape[0]
        load = jnp.dot(
            both(jnp.where(chosen, push, 0.0)), mode[...], preferred_element_type=F32
        )
        return -(load[:size] + load[size:])

    def wait_state(step, turn):
        plan = plans[turn]
        fewer = among(step, plan)
        full = sum(high - low for _, low, high in plan)
        for lacks in (0, 1):

            @pl.when(fewer if lacks else jnp.logical_not(fewer))
            def _():
                wait_bytes(
                    shared_state.at[step, pl.ds(0, full - lacks)],
                    state_recv.at[step, turn],
                )

    def send_one(step, source, owner_stream, owner_span):
        stream = streams - 1 - owner_stream if step == 0 else owner_stream
        span = spans - 1 - owner_span if step == 0 else owner_span
        copy = remote(
            source, load_in.at[step, me], load_send.at[step], load_recv.at[step], stream, span
        )
        return stream * spans + span != me, copy

    def take_group(step, turn, speed):
        plan = plans[turn]
        wait_state(step, turn)
        chosen = jnp.concatenate(
            [panels_of(*range_of) == marker_panel[...] for range_of in plan], axis=0
        )
        state = jnp.concatenate(
            [
                shared_state[step, pl.ds(span * streams + low, high - low)].reshape(
                    (high - low) * own, modes
                )
                for span, low, high in plan
            ],
            axis=0,
        )
        term = seen_by(state, chosen)
        load = load_of(term - speed, chosen)
        at = 0
        for span, low, high in plan:
            size = (high - low) * own
            load_out[step, pl.ds(span * streams + low, high - low)] = load[
                at : at + size
            ].reshape(high - low, own, modes)
            at += size
        for span, low, high in plan:

            def one(stream, carry):
                sends, copy = send_one(
                    step, load_out.at[step, span * streams + stream], stream, span
                )
                pl.when(sends)(copy.start)
                return carry

            lax.fori_loop(low, high, one, 0)
        return term

    def close(step, terms, speed):
        load_in[step, me] = load_out[step, opposite if step == 0 else home]
        return functools.reduce(jnp.add, terms) - speed

    def wait_load(step):
        wait_bytes(load_in.at[step, pl.ds(0, count - 1)], load_recv.at[step])
        return jnp.sum(load_in[step], axis=0)

    def advance(table, load):
        position, rate, omega, zeta = (table[slot] for slot in range(4))
        rate = (rate + MODAL_STEP * (load - omega * omega * position)) / (
            1.0 + 2.0 * MODAL_STEP * zeta * omega
        )
        return position + MODAL_STEP * rate, rate

    wait_bytes(mine, in_sem.at[0])
    shared_state[0, home] = PENALTY * mine[1] - SPRING * mine[0]
    pl.semaphore_wait(barrier, count - 1)
    send_state(0)
    params = remote(mine, theirs, pair_send.at[0], pair_recv.at[0], far_stream, far_span)
    params.start()

    copies[4].wait()
    start_halo(0, field)
    for copy in copies[5:10]:
        copy.wait()
    homes = home_blocks()
    turned[...] = mode[...].astype(F32).T.astype(BF16)
    speed = sample(field)

    response = hot_response(
        own, mine[2], mine[3], freq_bins, hot_nodes, stress, hot_square, copies[10:]
    )
    for slot in range(4):
        response_last[pl.ds(slot * own, own)] = response[slot]
    terms = []
    terms.append(take_group(0, 0, speed))
    terms.append(take_group(0, 1, speed))
    terms.append(take_group(0, 2, speed))
    terms.append(take_group(0, 3, speed))
    push = close(0, terms, speed)
    spread_push(push)
    finish_halo(0, field)
    stencil(0, field, advanced, width)
    add_forcing(advanced, width)
    start_halo(1, advanced)
    params.wait_recv()
    load = wait_load(0)
    position, rate = advance(theirs, load)
    shared_state[1, opposite] = PENALTY * rate - SPRING * position
    send_state(1)
    back_out[...] = load
    back = remote(back_out, back_in, pair_send.at[1], pair_recv.at[1], far_stream, far_span)
    back.start()
    speed = sample(advanced)
    terms = []
    terms.append(take_group(1, 0, speed))
    terms.append(take_group(1, 1, speed))
    terms.append(take_group(1, 2, speed))
    terms.append(take_group(1, 3, speed))
    push = close(1, terms, speed)
    spread_push(push)
    finish_halo(1, advanced)
    stencil(1, advanced, final, 0)
    add_forcing(final, 0)
    back.wait_recv()
    load = back_in[...]
    position, rate = advance(mine, load)
    tail[0] = position
    tail[1] = rate
    tail[2] = mine[2]
    tail[3] = mine[3]
    tail[4] = STEPS * base_load[...] + load * load
    tail[5] = wait_load(1)
    for step in range(STEPS):
        everyone = load_in.at[0, pl.ds(0, count - 1)]
        wait_bytes(everyone, state_send.at[step])
        wait_bytes(everyone, load_send.at[step])
        for sends, receives, copy, dst in halo_copies(step, (field, advanced)[step]):
            pl.when(sends)(copy.wait_send)
    params.wait_send()
    back.wait_send()


def hot_response(own, omega, zeta, freq_bins, hot_nodes, stress, hot_square, copies):
    modes = stress.shape[1]
    hots = hot_nodes.shape[1]
    for copy in copies:
        copy.wait()
    nodes = jnp.concatenate([hot_nodes[p : p + 1, :] for p in range(own)], axis=1)
    part = stress.shape[0] // NODE_PARTS
    hot_rows = None
    for q in range(NODE_PARTS):
        ids = lax.broadcasted_iota(jnp.int32, (part, own * hots), 0) + q * part
        picked = (ids == nodes).astype(F32).astype(BF16)
        found = lax.dot_general(
            stress[pl.ds(q * part, part), :], picked, TN, preferred_element_type=F32
        )
        hot_rows = found if hot_rows is None else hot_rows + found
    hot_square[...] = hot_rows * hot_rows

    lists = [[], [], [], []]
    columns = []
    for q in range(freq_bins.shape[0]):
        line = freq_bins[q : q + 1, :].astype(F32) * BIN_WIDTH
        columns.append(jnp.broadcast_to(line, (modes, modes)).T)
    for p in range(own):
        omega_sq = omega[p : p + 1] * omega[p : p + 1]
        factor = 2.0 * zeta[p : p + 1] * omega[p : p + 1]
        sums = [None] * 4
        for column in columns:
            square = column * column
            detune = omega_sq - square
            damping = factor * column
            response = 1.0 / (detune * detune + damping * damping)
            second = response * square
            terms = (response, response * column, second, second * square)
            for slot in range(4):
                term = jnp.sum(terms[slot], axis=0, keepdims=True)
                sums[slot] = term if sums[slot] is None else sums[slot] + term
        for slot in range(4):
            lists[slot].append(sums[slot])
    return [jnp.concatenate(parts, axis=0) for parts in lists]


def dirlik(moment_zero, moment_one, moment_two, moment_four):
    peak_rate = jnp.sqrt(moment_four / moment_two)
    mean_freq = moment_one / moment_zero * jnp.sqrt(moment_two / moment_four)
    irregular = moment_two / jnp.sqrt(moment_zero * moment_four)
    irregular_sq = irregular * irregular
    share_one = jnp.maximum(2.0 * (mean_freq - irregular_sq) / (1.0 + irregular_sq), 0.02)
    share_sq = share_one * share_one
    denominator = jnp.maximum(1.0 - irregular - share_one + share_sq, 0.02)
    ratio_term = (irregular - mean_freq - share_sq) / denominator
    share_two = denominator / jnp.maximum(1.0 - ratio_term, 0.05)
    share_three = 1.0 - share_one - share_two
    scale_term = jnp.maximum(
        1.25 * (irregular - share_three - share_two * ratio_term) / share_one, 0.05
    )
    size = jnp.abs(ratio_term)
    bracket = 6.0 * share_one * (scale_term * scale_term * scale_term)
    bracket = bracket + 2.0**1.5 * GAMMA_HALF * (size * size * size * share_two + share_three)
    bracket = jnp.maximum(bracket, 0.1)
    return (
        jnp.log(peak_rate) + jnp.log(jnp.full_like(bracket, 8.0))
        + 1.5 * jnp.log(moment_zero) + jnp.log(bracket)
    )


def finish(
    final,
    tail,
    response,
    hot_square,
    final_out,
    disp_out,
    rate_out,
    damage_out,
    disp_last,
    rate_last,
    damage_last,
    sem,
):
    pairs = (
        (final, final_out),
        (disp_last, disp_out),
        (rate_last, rate_out),
        (damage_last, damage_out),
    )
    copies = [
        pltpu.make_async_copy(source, target, sem.at[slot])
        for slot, (source, target) in enumerate(pairs)
    ]
    copies[0].start()
    own, hots = damage_last.shape
    position, rate, omega, zeta, power, load = (tail[slot] for slot in range(6))
    rate = (rate + MODAL_STEP * (load - omega * omega * position)) / (
        1.0 + 2.0 * MODAL_STEP * zeta * omega
    )
    disp_last[...] = position + MODAL_STEP * rate
    rate_last[...] = rate
    copies[1].start()
    copies[2].start()
    power = (power + load * load) / STEPS
    full = jnp.dot(
        response[...] * jnp.concatenate([power] * 4, axis=0),
        hot_square[...],
        precision=lax.Precision.HIGHEST,
        preferred_element_type=F32,
    )
    mine = (
        lax.broadcasted_iota(jnp.int32, (own, own * hots), 1) // hots
        == lax.broadcasted_iota(jnp.int32, (own, own * hots), 0)
    )
    moments = [
        jnp.sum(jnp.where(mine, full[slot * own : (slot + 1) * own], 0.0), axis=0, keepdims=True)
        * BIN_WIDTH
        for slot in range(4)
    ]
    damage = dirlik(*moments)
    for p in range(own):
        damage_last[p : p + 1, :] = damage[:, p * hots : (p + 1) * hots]
    copies[3].start()
    for copy in copies:
        copy.wait()


def body(
    velocity,
    weights,
    tile_block,
    normals,
    marker_panel,
    mode_shape,
    modal_disp,
    modal_rate,
    mode_omega,
    mode_zeta,
    base_load,
    stress_modes,
    hot_nodes,
    freq_bins,
):
    streams = lax.axis_size("stream")
    spans = lax.axis_size("span")
    count = streams * spans
    _, planes, width, depth = velocity.shape
    markers, block_width = weights.shape
    own, modes = modal_disp.shape
    hots = hot_nodes.shape[1]
    inner = planes * width
    rows = block_width // depth
    held = pl.BlockSpec(memory_space=pltpu.VMEM)
    stay = pl.BlockSpec(memory_space=pltpu.MemorySpace.HBM)
    small = pltpu.VMEM((own, modes), F32)
    bins = freq_bins.reshape(-1, modes)
    results = pl.pallas_call(
        functools.partial(kernel, streams, spans, planes, width),
        out_shape=(
            pltpu.VMEM((3, inner, depth), F32),
            pltpu.VMEM((6, own, modes), F32),
            pltpu.VMEM((4 * own, modes), F32),
            pltpu.VMEM((modes, own * hots), F32),
        ),
        in_specs=[stay] * 14,
        out_specs=(held,) * 4,
        scratch_shapes=[
            pltpu.VMEM((4, own, modes), F32),
            pltpu.VMEM((4, own, modes), F32),
            pltpu.VMEM((1, markers), jnp.int32),
            pltpu.SMEM(tile_block.shape, jnp.int32),
            pltpu.VMEM(mode_shape.shape, BF16),
            pltpu.VMEM(weights.shape, BF16),
            pltpu.VMEM(normals.shape, F32),
            pltpu.VMEM(stress_modes.shape, BF16),
            pltpu.VMEM(hot_nodes.shape, jnp.int32),
            pltpu.VMEM(bins.shape, jnp.int32),
            small,
            pltpu.VMEM((3, inner + 2 * width, depth), F32),
            pltpu.VMEM((3, inner + 2 * width, depth), F32),
            pltpu.VMEM((2 * depth, depth), BF16),
            pltpu.VMEM((modes, markers), BF16),
            pltpu.VMEM((markers // TILE, 3, rows, depth), F32),
            pltpu.VMEM((STEPS, count, own, modes), F32),
            pltpu.VMEM((STEPS, count, own, modes), F32),
            pltpu.VMEM((STEPS, count, own, modes), F32),
            small,
            small,
            pltpu.VMEM((STEPS, 2, 3, width, depth), F32),
            pltpu.VMEM((STEPS, 2, 3, planes, depth), F32),
            pltpu.VMEM((STEPS, 2, 3, planes, depth), F32),
            pltpu.SemaphoreType.DMA((11,)),
            pltpu.SemaphoreType.DMA((STEPS,)),
            pltpu.SemaphoreType.DMA((STEPS, len(GROUPS))),
            pltpu.SemaphoreType.DMA((STEPS,)),
            pltpu.SemaphoreType.DMA((STEPS,)),
            pltpu.SemaphoreType.DMA((2,)),
            pltpu.SemaphoreType.DMA((2,)),
            pltpu.SemaphoreType.DMA((STEPS, 4)),
            pltpu.SemaphoreType.DMA((STEPS, 4)),
        ],
        compiler_params=pltpu.CompilerParams(
            collective_id=0, has_side_effects=True, vmem_limit_bytes=60 * 1024 * 1024
        ),
        name="coupled_steps",
    )(
        modal_disp,
        modal_rate,
        mode_omega,
        mode_zeta,
        marker_panel.reshape(1, markers),
        tile_block,
        velocity.reshape(3, inner, depth),
        mode_shape,
        weights,
        normals,
        stress_modes,
        hot_nodes,
        bins,
        base_load,
    )
    results = pl.pallas_call(
        finish,
        out_shape=[
            jax.ShapeDtypeStruct((3, inner, depth), F32),
            jax.ShapeDtypeStruct((own, modes), F32),
            jax.ShapeDtypeStruct((own, modes), F32),
            jax.ShapeDtypeStruct((own, hots), F32),
        ],
        in_specs=[held] * 4,
        out_specs=[stay] * 4,
        scratch_shapes=[
            small,
            small,
            pltpu.VMEM((own, hots), F32),
            pltpu.SemaphoreType.DMA((4,)),
        ],
        compiler_params=pltpu.CompilerParams(vmem_limit_bytes=4 * 1024 * 1024),
        name="finish",
    )(*results)
    return (results[0].reshape(velocity.shape),) + tuple(results[1:])


def solution(mesh):
    placed = (
        P(None, "stream", "span", None),
        P(("stream", "span"), None),
        P(("stream", "span")),
        P(None, ("stream", "span")),
        P(("stream", "span")),
        P(("stream", "span"), None),
        P(("stream", "span"), None),
        P(("stream", "span"), None),
        P(("stream", "span"), None),
        P(("stream", "span"), None),
        P(("stream", "span"), None),
        P(),
        P(("stream", "span"), None),
        P(),
    )
    return jax.shard_map(
        body,
        mesh=mesh,
        in_specs=placed,
        out_specs=(
            P(None, "stream", "span", None),
            P(("stream", "span"), None),
            P(("stream", "span"), None),
            P(("stream", "span"), None),
        ),
        check_vma=False,
    )
```

```python
import functools

import jax
import jax.numpy as jnp
from jax import lax
from jax.experimental import pallas as pl
from jax.experimental.pallas import tpu as pltpu
from jax.sharding import PartitionSpec as P

TILE = 128
STEPS = 2

PENALTY = 1.0
SPRING = 0.5
TIME_STEP = 0.2
VISCOSITY = 0.5
CONVECTION = 1.0
MODAL_STEP = 0.5
BIN_WIDTH = 0.002
GAMMA_HALF = 1.3293404

F32 = jnp.float32
BF16 = jnp.bfloat16
NT = (((1,), (1,)), ((), ()))
TN = (((0,), (0,)), ((), ()))
NODE_PARTS = 4
PLANES = 4
EVERY = 1 << 16
GROUPS = (
    [(0, 0, 2), (1, 0, 2)],
    [(0, 2, EVERY), (1, 2, EVERY)],
    [(2, 0, EVERY)],
    [(3, 0, EVERY)],
)


def split_two(value):
    high = value.astype(BF16)
    low = (value - high.astype(F32)).astype(BF16)
    return high, low


def kernel(
    streams,
    spans,
    planes,
    width,
    disp_hbm,
    rate_hbm,
    omega_hbm,
    zeta_hbm,
    panel_hbm,
    block_hbm,
    velocity_hbm,
    mode_hbm,
    weights_hbm,
    normals_hbm,
    stress_hbm,
    nodes_hbm,
    bins_hbm,
    base_hbm,
    final,
    tail,
    response_last,
    hot_square,
    mine,
    theirs,
    marker_panel,
    tile_block,
    mode,
    weights,
    normals,
    stress,
    hot_nodes,
    freq_bins,
    base_load,
    field,
    advanced,
    band,
    turned,
    spread,
    shared_state,
    load_out,
    load_in,
    back_out,
    back_in,
    stream_halo,
    span_edge,
    span_halo,
    in_sem,
    state_send,
    state_recv,
    load_send,
    load_recv,
    pair_send,
    pair_recv,
    halo_send,
    halo_recv,
):
    count = streams * spans
    stream_id = lax.axis_index("stream")
    span_id = lax.axis_index("span")
    me = stream_id * spans + span_id
    far_stream = streams - 1 - stream_id
    far_span = spans - 1 - span_id
    own = mine.shape[1]
    modes = mine.shape[2]
    home = span_id * streams + stream_id
    opposite = far_span * streams + far_stream
    plans = [
        [(span, low, min(high, streams)) for span, low, high in plan] for plan in GROUPS
    ]

    def among(step, plan):
        stream = stream_id if step == 0 else far_stream
        at_span = span_id if step == 0 else far_span
        found = None
        for span, low, high in plan:
            here = jnp.logical_and(
                at_span == span, jnp.logical_and(stream >= low, stream < high)
            )
            found = here if found is None else jnp.logical_or(found, here)
        return found

    depth = field.shape[2]
    markers = mode.shape[0]
    tiles = markers // TILE
    block_width = weights.shape[1]
    rows = block_width // depth
    inner = planes * width

    pairs = (
        (disp_hbm, mine.at[0]),
        (rate_hbm, mine.at[1]),
        (omega_hbm, mine.at[2]),
        (zeta_hbm, mine.at[3]),
        (velocity_hbm, field.at[:, pl.ds(width, inner), :]),
        (block_hbm, tile_block),
        (normals_hbm, normals),
        (weights_hbm, weights),
        (panel_hbm, marker_panel),
        (mode_hbm, mode),
        (stress_hbm, stress),
        (nodes_hbm, hot_nodes),
        (bins_hbm, freq_bins),
        (base_hbm, base_load),
    )
    copies = [
        pltpu.make_async_copy(source, target, in_sem.at[max(slot - 3, 0)])
        for slot, (source, target) in enumerate(pairs)
    ]

    if spans == 4:
        upper = span_id // 2
        nearest = [
            span_id,
            span_id + 1 - 2 * (span_id % 2),
            2 - upper,
            3 - 3 * upper,
        ]
    else:
        nearest = [(span_id + shift) % spans for shift in range(spans)]
    turn = 1 - stream_id // (streams // 2)

    def far_first(step):
        return step + (streams - 1 - 2 * step) * turn

    def place(stream, span):
        return {"stream": stream, "span": span}

    barrier = pltpu.get_barrier_semaphore()
    for near, span in reversed(list(enumerate(nearest))):

        def greet(step, carry):
            stream = far_first(step)

            def signal():
                pl.semaphore_signal(
                    barrier,
                    inc=1,
                    device_id=place(stream, span),
                    device_id_type=pl.DeviceIdType.MESH,
                )

            if near == 0:
                pl.when(stream != stream_id)(signal)
            else:
                signal()
            return carry

        lax.fori_loop(0, streams, greet, 0)
    for copy in copies:
        copy.start()

    def remote(source, target, send, recv, stream, span):
        return pltpu.make_async_remote_copy(
            src_ref=source,
            dst_ref=target,
            send_sem=send,
            recv_sem=recv,
            device_id=place(stream, span),
            device_id_type=pl.DeviceIdType.MESH,
        )

    def wait_bytes(part, sem):
        pltpu.make_async_copy(part, part, sem).wait()

    def send_state(step):
        block = shared_state.at[step, home if step == 0 else opposite]
        turn_of = len(plans) - 1
        for turn, plan in enumerate(plans[:-1]):
            turn_of = jnp.where(among(step, plan), turn, turn_of)
        for near, span in reversed(list(enumerate(nearest))):

            def one(turned, carry):
                stream = far_first(turned)
                copy = remote(
                    block,
                    block,
                    state_send.at[step],
                    state_recv.at[step, turn_of],
                    stream,
                    span,
                )
                if near == 0:
                    pl.when(stream != stream_id)(copy.start)
                else:
                    copy.start()
                return carry

            lax.fori_loop(0, streams, one, 0)

    def halo_copies(step, source):
        last = inner
        table = (
            (stream_id < streams - 1, source.at[:, pl.ds(last, width), :],
             stream_halo.at[step, 0], 0, (1, 0), stream_id > 0),
            (stream_id > 0, source.at[:, pl.ds(width, width), :],
             stream_halo.at[step, 1], 1, (-1, 0), stream_id < streams - 1),
            (span_id < spans - 1, span_edge.at[step, 1],
             span_halo.at[step, 0], 2, (0, 1), span_id > 0),
            (span_id > 0, span_edge.at[step, 0],
             span_halo.at[step, 1], 3, (0, -1), span_id < spans - 1),
        )
        result = []
        for sends, src, dst, slot, (ds, dp), receives in table:
            copy = remote(
                src,
                dst,
                halo_send.at[step, slot],
                halo_recv.at[step, slot],
                stream_id + ds,
                span_id + dp,
            )
            result.append((sends, receives, copy, dst))
        return result

    def start_halo(step, source):
        for k in range(3):
            span_edge[step, 0, k] = source[k, pl.ds(width, planes, stride=width), :]
            span_edge[step, 1, k] = source[k, pl.ds(2 * width - 1, planes, stride=width), :]
        for sends, receives, copy, dst in halo_copies(step, source):
            pl.when(sends)(copy.start)

            @pl.when(jnp.logical_not(receives))
            def _():
                dst[...] = jnp.zeros(dst.shape, F32)

    def finish_halo(step, source):
        for sends, receives, copy, dst in halo_copies(step, source):
            pl.when(receives)(copy.wait_recv)
        for k in range(3):
            source[k, pl.ds(0, width), :] = stream_halo[step, 0, k]
            source[k, pl.ds(width + inner, width), :] = stream_halo[step, 1, k]

    row_of = lax.broadcasted_iota(jnp.int32, (width, depth), 0)
    lane_from = lax.broadcasted_iota(jnp.int32, (depth, depth), 0)
    lane_to = lax.broadcasted_iota(jnp.int32, (depth, depth), 1)
    beside_lane = (jnp.abs(lane_from - lane_to) == 1).astype(F32).astype(BF16)
    band[...] = jnp.concatenate([beside_lane, beside_lane], axis=0)

    def stencil(step, source, target, offset):
        def several(c, carry):
            for k in range(3):
                first = pl.multiple_of((c * PLANES + 1) * width, width)
                block = source[k, pl.ds(first, PLANES * width), :]
                along = jnp.dot(
                    jnp.concatenate(split_two(block), axis=1),
                    band[...],
                    preferred_element_type=F32,
                )
                for q in range(PLANES):
                    start = pl.multiple_of(first + q * width, width)
                    here = block[q * width : (q + 1) * width]
                    ahead = source[k, pl.ds(start + width, width), :]
                    behind = source[k, pl.ds(start - width, width), :]
                    y_low = span_halo[step, 0, k, pl.ds(c * PLANES + q, 1), :]
                    y_high = span_halo[step, 1, k, pl.ds(c * PLANES + q, 1), :]
                    y_ahead = jnp.where(
                        row_of == width - 1, y_high, pltpu.roll(here, width - 1, 0)
                    )
                    y_behind = jnp.where(row_of == 0, y_low, pltpu.roll(here, 1, 0))
                    beside = y_ahead + y_behind + along[q * width : (q + 1) * width]
                    target[k, pl.ds(pl.multiple_of(start - width + offset, width), width), :] = (
                        (1.0 - 6.0 * TIME_STEP * VISCOSITY) * here
                        + TIME_STEP * (VISCOSITY - 0.5 * CONVECTION) * ahead
                        + TIME_STEP * (VISCOSITY + 0.5 * CONVECTION) * behind
                        + TIME_STEP * VISCOSITY * beside
                    )
            return carry

        lax.fori_loop(0, planes // PLANES, several, 0)

    def add_forcing(target, offset):
        def block(b, carry):
            start = pl.multiple_of(b * rows + offset, rows)
            spot = jnp.full((rows, depth), b, jnp.int32)
            for k in range(3):
                total = target[k, pl.ds(start, rows), :]
                for t in range(tiles):
                    total = total + jnp.where(homes[t] == spot, TIME_STEP * spread[t, k], 0.0)
                target[k, pl.ds(start, rows), :] = total
            return carry

        lax.fori_loop(0, inner // rows, block, 0)

    diagonal = (
        lax.broadcasted_iota(jnp.int32, (rows, block_width), 0)
        == lax.broadcasted_iota(jnp.int32, (rows, block_width), 1) // depth
    ).astype(F32).astype(BF16)

    def expand(part):
        return jnp.concatenate([part] * rows, axis=1) * diagonal

    def home_blocks():
        return [jnp.full((rows, depth), tile_block[t], jnp.int32) for t in range(tiles)]

    def sample(source):
        def look(b, found):
            start = pl.multiple_of(b * rows + width, rows)
            spot = jnp.full((rows, depth), b, jnp.int32)
            cells = [source[k, pl.ds(start, rows), :] for k in range(3)]
            return tuple(
                jnp.where(homes[t] == spot, cells[k], found[3 * t + k])
                for t in range(tiles)
                for k in range(3)
            )

        blank = jnp.zeros((rows, depth), F32)
        found = lax.fori_loop(0, inner // rows, look, (blank,) * (3 * tiles), unroll=4)
        speeds = []
        for t in range(tiles):
            left = jnp.concatenate(
                [expand(found[3 * t + k].astype(BF16)) for k in range(3)], axis=0
            )
            got = lax.dot_general(
                left, weights[pl.ds(t * TILE, TILE), :], NT, preferred_element_type=F32
            )
            speed = None
            for k in range(3):
                term = normals[k : k + 1, t * TILE : (t + 1) * TILE] * jnp.sum(
                    got[k * rows : (k + 1) * rows], axis=0, keepdims=True
                )
                speed = term if speed is None else speed + term
            speeds.append(speed)
        return PENALTY * jnp.concatenate(speeds, axis=1)

    def spread_push(push):
        for t in range(tiles):
            parts = []
            for k in range(3):
                half = normals[k : k + 1, t * TILE : (t + 1) * TILE] * push[
                    :, t * TILE : (t + 1) * TILE
                ]
                parts.append(expand(jnp.broadcast_to(half, (rows, TILE)).astype(BF16)))
            left = jnp.concatenate(parts, axis=0)
            right = jnp.concatenate(
                [weights[pl.ds(t * TILE, TILE), y * depth : (y + 1) * depth] for y in range(rows)],
                axis=0,
            )
            got = jnp.dot(left, right, preferred_element_type=F32)
            for k in range(3):
                spread[t, k] = got[k * rows : (k + 1) * rows]

    def panels_of(span, low, high):
        row = lax.broadcasted_iota(jnp.int32, ((high - low) * own, markers), 0)
        return row + (row // own + low) * (spans - 1) * own + (low + span) * own

    def both(value):
        high = value.astype(BF16).astype(F32)
        return jnp.concatenate([high, value - high], axis=0).astype(BF16)

    def seen_by(state, chosen):
        size = state.shape[0]
        every = jnp.dot(both(state), turned[...], preferred_element_type=F32)
        return jnp.sum(
            jnp.where(chosen, every[:size] + every[size:], 0.0), axis=0, keepdims=True
        )

    def load_of(push, chosen):
        size = chosen.shape[0]
        load = jnp.dot(
            both(jnp.where(chosen, push, 0.0)), mode[...], preferred_element_type=F32
        )
        return -(load[:size] + load[size:])

    def wait_state(step, turn):
        plan = plans[turn]
        fewer = among(step, plan)
        full = sum(high - low for _, low, high in plan)
        for lacks in (0, 1):

            @pl.when(fewer if lacks else jnp.logical_not(fewer))
            def _():
                wait_bytes(
                    shared_state.at[step, pl.ds(0, full - lacks)],
                    state_recv.at[step, turn],
                )

    def send_one(step, source, owner_stream, owner_span):
        stream = streams - 1 - owner_stream if step == 0 else owner_stream
        span = spans - 1 - owner_span if step == 0 else owner_span
        copy = remote(
            source, load_in.at[step, me], load_send.at[step], load_recv.at[step], stream, span
        )
        return stream * spans + span != me, copy

    def take_group(step, turn, speed):
        plan = plans[turn]
        wait_state(step, turn)
        chosen = jnp.concatenate(
            [panels_of(*range_of) == marker_panel[...] for range_of in plan], axis=0
        )
        state = jnp.concatenate(
            [
                shared_state[step, pl.ds(span * streams + low, high - low)].reshape(
                    (high - low) * own, modes
                )
                for span, low, high in plan
            ],
            axis=0,
        )
        term = seen_by(state, chosen)
        load = load_of(term - speed, chosen)
        at = 0
        for span, low, high in plan:
            size = (high - low) * own
            load_out[step, pl.ds(span * streams + low, high - low)] = load[
                at : at + size
            ].reshape(high - low, own, modes)
            at += size
        for span, low, high in plan:

            def one(stream, carry):
                sends, copy = send_one(
                    step, load_out.at[step, span * streams + stream], stream, span
                )
                pl.when(sends)(copy.start)
                return carry

            lax.fori_loop(low, high, one, 0)
        return term

    def close(step, terms, speed):
        load_in[step, me] = load_out[step, opposite if step == 0 else home]
        return functools.reduce(jnp.add, terms) - speed

    def wait_load(step):
        wait_bytes(load_in.at[step, pl.ds(0, count - 1)], load_recv.at[step])
        return jnp.sum(load_in[step], axis=0)

    def advance(table, load):
        position, rate, omega, zeta = (table[slot] for slot in range(4))
        rate = (rate + MODAL_STEP * (load - omega * omega * position)) / (
            1.0 + 2.0 * MODAL_STEP * zeta * omega
        )
        return position + MODAL_STEP * rate, rate

    wait_bytes(mine, in_sem.at[0])
    shared_state[0, home] = PENALTY * mine[1] - SPRING * mine[0]
    pl.semaphore_wait(barrier, count - 1)
    send_state(0)
    params = remote(mine, theirs, pair_send.at[0], pair_recv.at[0], far_stream, far_span)
    params.start()

    copies[4].wait()
    start_halo(0, field)
    for copy in copies[5:10]:
        copy.wait()
    homes = home_blocks()
    turned[...] = mode[...].astype(F32).T.astype(BF16)
    speed = sample(field)

    response = hot_response(
        own, mine[2], mine[3], freq_bins, hot_nodes, stress, hot_square, copies[10:]
    )
    for slot in range(4):
        response_last[pl.ds(slot * own, own)] = response[slot]
    terms = []
    terms.append(take_group(0, 0, speed))
    terms.append(take_group(0, 1, speed))
    terms.append(take_group(0, 2, speed))
    terms.append(take_group(0, 3, speed))
    push = close(0, terms, speed)
    spread_push(push)
    finish_halo(0, field)
    stencil(0, field, advanced, width)
    add_forcing(advanced, width)
    start_halo(1, advanced)
    params.wait_recv()
    load = wait_load(0)
    position, rate = advance(theirs, load)
    shared_state[1, opposite] = PENALTY * rate - SPRING * position
    send_state(1)
    back_out[...] = load
    back = remote(back_out, back_in, pair_send.at[1], pair_recv.at[1], far_stream, far_span)
    back.start()
    speed = sample(advanced)
    terms = []
    terms.append(take_group(1, 0, speed))
    terms.append(take_group(1, 1, speed))
    terms.append(take_group(1, 2, speed))
    terms.append(take_group(1, 3, speed))
    push = close(1, terms, speed)
    spread_push(push)
    finish_halo(1, advanced)
    stencil(1, advanced, final, 0)
    add_forcing(final, 0)
    back.wait_recv()
    load = back_in[...]
    position, rate = advance(mine, load)
    tail[0] = position
    tail[1] = rate
    tail[2] = mine[2]
    tail[3] = mine[3]
    tail[4] = STEPS * base_load[...] + load * load
    tail[5] = wait_load(1)
    for step in range(STEPS):
        everyone = load_in.at[0, pl.ds(0, count - 1)]
        wait_bytes(everyone, state_send.at[step])
        wait_bytes(everyone, load_send.at[step])
        for sends, receives, copy, dst in halo_copies(step, (field, advanced)[step]):
            pl.when(sends)(copy.wait_send)
    params.wait_send()
    back.wait_send()


def hot_response(own, omega, zeta, freq_bins, hot_nodes, stress, hot_square, copies):
    modes = stress.shape[1]
    hots = hot_nodes.shape[1]
    for copy in copies:
        copy.wait()
    nodes = jnp.concatenate([hot_nodes[p : p + 1, :] for p in range(own)], axis=1)
    part = stress.shape[0] // NODE_PARTS
    hot_rows = None
    for q in range(NODE_PARTS):
        ids = lax.broadcasted_iota(jnp.int32, (part, own * hots), 0) + q * part
        picked = (ids == nodes).astype(F32).astype(BF16)
        found = lax.dot_general(
            stress[pl.ds(q * part, part), :], picked, TN, preferred_element_type=F32
        )
        hot_rows = found if hot_rows is None else hot_rows + found
    hot_square[...] = hot_rows * hot_rows

    lists = [[], [], [], []]
    columns = []
    for q in range(freq_bins.shape[0]):
        line = freq_bins[q : q + 1, :].astype(F32) * BIN_WIDTH
        columns.append(jnp.broadcast_to(line, (modes, modes)).T)
    for p in range(own):
        omega_sq = omega[p : p + 1] * omega[p : p + 1]
        factor = 2.0 * zeta[p : p + 1] * omega[p : p + 1]
        sums = [None] * 4
        for column in columns:
            square = column * column
            detune = omega_sq - square
            damping = factor * column
            response = 1.0 / (detune * detune + damping * damping)
            second = response * square
            terms = (response, response * column, second, second * square)
            for slot in range(4):
                term = jnp.sum(terms[slot], axis=0, keepdims=True)
                sums[slot] = term if sums[slot] is None else sums[slot] + term
        for slot in range(4):
            lists[slot].append(sums[slot])
    return [jnp.concatenate(parts, axis=0) for parts in lists]


def dirlik(moment_zero, moment_one, moment_two, moment_four):
    peak_rate = jnp.sqrt(moment_four / moment_two)
    mean_freq = moment_one / moment_zero * jnp.sqrt(moment_two / moment_four)
    irregular = moment_two / jnp.sqrt(moment_zero * moment_four)
    irregular_sq = irregular * irregular
    share_one = jnp.maximum(2.0 * (mean_freq - irregular_sq) / (1.0 + irregular_sq), 0.02)
    share_sq = share_one * share_one
    denominator = jnp.maximum(1.0 - irregular - share_one + share_sq, 0.02)
    ratio_term = (irregular - mean_freq - share_sq) / denominator
    share_two = denominator / jnp.maximum(1.0 - ratio_term, 0.05)
    share_three = 1.0 - share_one - share_two
    scale_term = jnp.maximum(
        1.25 * (irregular - share_three - share_two * ratio_term) / share_one, 0.05
    )
    size = jnp.abs(ratio_term)
    bracket = 6.0 * share_one * (scale_term * scale_term * scale_term)
    bracket = bracket + 2.0**1.5 * GAMMA_HALF * (size * size * size * share_two + share_three)
    bracket = jnp.maximum(bracket, 0.1)
    return (
        jnp.log(peak_rate) + jnp.log(jnp.full_like(bracket, 8.0))
        + 1.5 * jnp.log(moment_zero) + jnp.log(bracket)
    )


def finish(
    final,
    tail,
    response,
    hot_square,
    final_out,
    disp_out,
    rate_out,
    damage_out,
    disp_last,
    rate_last,
    damage_last,
    sem,
):
    pairs = (
        (final, final_out),
        (disp_last, disp_out),
        (rate_last, rate_out),
        (damage_last, damage_out),
    )
    copies = [
        pltpu.make_async_copy(source, target, sem.at[slot])
        for slot, (source, target) in enumerate(pairs)
    ]
    copies[0].start()
    own, hots = damage_last.shape
    position, rate, omega, zeta, power, load = (tail[slot] for slot in range(6))
    rate = (rate + MODAL_STEP * (load - omega * omega * position)) / (
        1.0 + 2.0 * MODAL_STEP * zeta * omega
    )
    disp_last[...] = position + MODAL_STEP * rate
    rate_last[...] = rate
    copies[1].start()
    copies[2].start()
    power = (power + load * load) / STEPS
    full = jnp.dot(
        response[...] * jnp.concatenate([power] * 4, axis=0),
        hot_square[...],
        precision=lax.Precision.HIGHEST,
        preferred_element_type=F32,
    )
    mine = (
        lax.broadcasted_iota(jnp.int32, (own, own * hots), 1) // hots
        == lax.broadcasted_iota(jnp.int32, (own, own * hots), 0)
    )
    moments = [
        jnp.sum(jnp.where(mine, full[slot * own : (slot + 1) * own], 0.0), axis=0, keepdims=True)
        * BIN_WIDTH
        for slot in range(4)
    ]
    damage = dirlik(*moments)
    for p in range(own):
        damage_last[p : p + 1, :] = damage[:, p * hots : (p + 1) * hots]
    copies[3].start()
    for copy in copies:
        copy.wait()


def body(
    velocity,
    weights,
    tile_block,
    normals,
    marker_panel,
    mode_shape,
    modal_disp,
    modal_rate,
    mode_omega,
    mode_zeta,
    base_load,
    stress_modes,
    hot_nodes,
    freq_bins,
):
    streams = lax.axis_size("stream")
    spans = lax.axis_size("span")
    count = streams * spans
    _, planes, width, depth = velocity.shape
    markers, block_width = weights.shape
    own, modes = modal_disp.shape
    hots = hot_nodes.shape[1]
    inner = planes * width
    rows = block_width // depth
    held = pl.BlockSpec(memory_space=pltpu.VMEM)
    stay = pl.BlockSpec(memory_space=pltpu.MemorySpace.HBM)
    small = pltpu.VMEM((own, modes), F32)
    bins = freq_bins.reshape(-1, modes)
    results = pl.pallas_call(
        functools.partial(kernel, streams, spans, planes, width),
        out_shape=(
            pltpu.VMEM((3, inner, depth), F32),
            pltpu.VMEM((6, own, modes), F32),
            pltpu.VMEM((4 * own, modes), F32),
            pltpu.VMEM((modes, own * hots), F32),
        ),
        in_specs=[stay] * 14,
        out_specs=(held,) * 4,
        scratch_shapes=[
            pltpu.VMEM((4, own, modes), F32),
            pltpu.VMEM((4, own, modes), F32),
            pltpu.VMEM((1, markers), jnp.int32),
            pltpu.SMEM(tile_block.shape, jnp.int32),
            pltpu.VMEM(mode_shape.shape, BF16),
            pltpu.VMEM(weights.shape, BF16),
            pltpu.VMEM(normals.shape, F32),
            pltpu.VMEM(stress_modes.shape, BF16),
            pltpu.VMEM(hot_nodes.shape, jnp.int32),
            pltpu.VMEM(bins.shape, jnp.int32),
            small,
            pltpu.VMEM((3, inner + 2 * width, depth), F32),
            pltpu.VMEM((3, inner + 2 * width, depth), F32),
            pltpu.VMEM((2 * depth, depth), BF16),
            pltpu.VMEM((modes, markers), BF16),
            pltpu.VMEM((markers // TILE, 3, rows, depth), F32),
            pltpu.VMEM((STEPS, count, own, modes), F32),
            pltpu.VMEM((STEPS, count, own, modes), F32),
            pltpu.VMEM((STEPS, count, own, modes), F32),
            small,
            small,
            pltpu.VMEM((STEPS, 2, 3, width, depth), F32),
            pltpu.VMEM((STEPS, 2, 3, planes, depth), F32),
            pltpu.VMEM((STEPS, 2, 3, planes, depth), F32),
            pltpu.SemaphoreType.DMA((11,)),
            pltpu.SemaphoreType.DMA((STEPS,)),
            pltpu.SemaphoreType.DMA((STEPS, len(GROUPS))),
            pltpu.SemaphoreType.DMA((STEPS,)),
            pltpu.SemaphoreType.DMA((STEPS,)),
            pltpu.SemaphoreType.DMA((2,)),
            pltpu.SemaphoreType.DMA((2,)),
            pltpu.SemaphoreType.DMA((STEPS, 4)),
            pltpu.SemaphoreType.DMA((STEPS, 4)),
        ],
        compiler_params=pltpu.CompilerParams(
            collective_id=0, has_side_effects=True, vmem_limit_bytes=60 * 1024 * 1024
        ),
        name="coupled_steps",
    )(
        modal_disp,
        modal_rate,
        mode_omega,
        mode_zeta,
        marker_panel.reshape(1, markers),
        tile_block,
        velocity.reshape(3, inner, depth),
        mode_shape,
        weights,
        normals,
        stress_modes,
        hot_nodes,
        bins,
        base_load,
    )
    results = pl.pallas_call(
        finish,
        out_shape=[
            jax.ShapeDtypeStruct((3, inner, depth), F32),
            jax.ShapeDtypeStruct((own, modes), F32),
            jax.ShapeDtypeStruct((own, modes), F32),
            jax.ShapeDtypeStruct((own, hots), F32),
        ],
        in_specs=[held] * 4,
        out_specs=[stay] * 4,
        scratch_shapes=[
            small,
            small,
            pltpu.VMEM((own, hots), F32),
            pltpu.SemaphoreType.DMA((4,)),
        ],
        compiler_params=pltpu.CompilerParams(vmem_limit_bytes=4 * 1024 * 1024),
        name="finish",
    )(*results)
    return (results[0].reshape(velocity.shape),) + tuple(results[1:])


def solution(mesh):
    placed = (
        P(None, "stream", "span", None),
        P(("stream", "span"), None),
        P(("stream", "span")),
        P(None, ("stream", "span")),
        P(("stream", "span")),
        P(("stream", "span"), None),
        P(("stream", "span"), None),
        P(("stream", "span"), None),
        P(("stream", "span"), None),
        P(("stream", "span"), None),
        P(("stream", "span"), None),
        P(),
        P(("stream", "span"), None),
        P(),
    )
    return jax.shard_map(
        body,
        mesh=mesh,
        in_specs=placed,
        out_specs=(
            P(None, "stream", "span", None),
            P(("stream", "span"), None),
            P(("stream", "span"), None),
            P(("stream", "span"), None),
        ),
        check_vma=False,
    )
```

```python
import functools

import jax
import jax.numpy as jnp
from jax import lax
from jax.experimental import pallas as pl
from jax.experimental.pallas import tpu as pltpu
from jax.sharding import PartitionSpec as P

TILE = 128
STEPS = 2

PENALTY = 1.0
SPRING = 0.5
TIME_STEP = 0.2
VISCOSITY = 0.5
CONVECTION = 1.0
MODAL_STEP = 0.5
BIN_WIDTH = 0.002
GAMMA_HALF = 1.3293404

F32 = jnp.float32
BF16 = jnp.bfloat16
NT = (((1,), (1,)), ((), ()))
TN = (((0,), (0,)), ((), ()))
NODE_PARTS = 4
PLANES = 4
EVERY = 1 << 16
GROUPS = (
    ([(0, 0, 2), (1, 0, 2)], [(0, 2, EVERY), (1, 2, EVERY)], [(2, 0, EVERY), (3, 0, EVERY)]),
    ([(0, 0, 2), (1, 0, 2)], [(0, 2, EVERY), (1, 2, EVERY)], [(2, 0, EVERY)], [(3, 0, EVERY)]),
)


def split_two(value):
    high = value.astype(BF16)
    low = (value - high.astype(F32)).astype(BF16)
    return high, low


def kernel(
    streams,
    spans,
    planes,
    width,
    disp_hbm,
    rate_hbm,
    omega_hbm,
    zeta_hbm,
    panel_hbm,
    block_hbm,
    velocity_hbm,
    mode_hbm,
    weights_hbm,
    normals_hbm,
    stress_hbm,
    nodes_hbm,
    bins_hbm,
    base_hbm,
    final,
    tail,
    response_last,
    hot_square,
    mine,
    theirs,
    marker_panel,
    tile_block,
    mode,
    weights,
    normals,
    stress,
    hot_nodes,
    freq_bins,
    base_load,
    field,
    advanced,
    band,
    turned,
    spread,
    shared_state,
    load_out,
    load_in,
    back_out,
    back_in,
    stream_halo,
    span_edge,
    span_halo,
    in_sem,
    state_send,
    state_recv,
    load_send,
    load_recv,
    pair_send,
    pair_recv,
    halo_send,
    halo_recv,
):
    count = streams * spans
    stream_id = lax.axis_index("stream")
    span_id = lax.axis_index("span")
    me = stream_id * spans + span_id
    far_stream = streams - 1 - stream_id
    far_span = spans - 1 - span_id
    own = mine.shape[1]
    modes = mine.shape[2]
    home = span_id * streams + stream_id
    opposite = far_span * streams + far_stream
    plans = [
        [[(span, low, min(high, streams)) for span, low, high in plan] for plan in steps]
        for steps in GROUPS
    ]

    def among(step, plan):
        stream = stream_id if step == 0 else far_stream
        at_span = span_id if step == 0 else far_span
        found = None
        for span, low, high in plan:
            here = jnp.logical_and(
                at_span == span, jnp.logical_and(stream >= low, stream < high)
            )
            found = here if found is None else jnp.logical_or(found, here)
        return found

    depth = field.shape[2]
    markers = mode.shape[0]
    tiles = markers // TILE
    block_width = weights.shape[1]
    rows = block_width // depth
    inner = planes * width

    pairs = (
        (disp_hbm, mine.at[0]),
        (rate_hbm, mine.at[1]),
        (omega_hbm, mine.at[2]),
        (zeta_hbm, mine.at[3]),
        (velocity_hbm, field.at[:, pl.ds(width, inner), :]),
        (block_hbm, tile_block),
        (normals_hbm, normals),
        (weights_hbm, weights),
        (panel_hbm, marker_panel),
        (mode_hbm, mode),
        (stress_hbm, stress),
        (nodes_hbm, hot_nodes),
        (bins_hbm, freq_bins),
        (base_hbm, base_load),
    )
    copies = [
        pltpu.make_async_copy(source, target, in_sem.at[max(slot - 3, 0)])
        for slot, (source, target) in enumerate(pairs)
    ]

    if spans == 4:
        upper = span_id // 2
        nearest = [
            span_id,
            span_id + 1 - 2 * (span_id % 2),
            2 - upper,
            3 - 3 * upper,
        ]
    else:
        nearest = [(span_id + shift) % spans for shift in range(spans)]
    turn = 1 - stream_id // (streams // 2)

    def far_first(step):
        return step + (streams - 1 - 2 * step) * turn

    def place(stream, span):
        return {"stream": stream, "span": span}

    barrier = pltpu.get_barrier_semaphore()
    for near, span in reversed(list(enumerate(nearest))):

        def greet(step, carry):
            stream = far_first(step)

            def signal():
                pl.semaphore_signal(
                    barrier,
                    inc=1,
                    device_id=place(stream, span),
                    device_id_type=pl.DeviceIdType.MESH,
                )

            if near == 0:
                pl.when(stream != stream_id)(signal)
            else:
                signal()
            return carry

        lax.fori_loop(0, streams, greet, 0)
    for copy in copies:
        copy.start()

    def remote(source, target, send, recv, stream, span):
        return pltpu.make_async_remote_copy(
            src_ref=source,
            dst_ref=target,
            send_sem=send,
            recv_sem=recv,
            device_id=place(stream, span),
            device_id_type=pl.DeviceIdType.MESH,
        )

    def wait_bytes(part, sem):
        pltpu.make_async_copy(part, part, sem).wait()

    def send_state(step):
        block = shared_state.at[step, home if step == 0 else opposite]
        turn_of = len(plans[step]) - 1
        for turn, plan in enumerate(plans[step][:-1]):
            turn_of = jnp.where(among(step, plan), turn, turn_of)
        for near, span in reversed(list(enumerate(nearest))):

            def one(turned, carry):
                stream = far_first(turned)
                copy = remote(
                    block,
                    block,
                    state_send.at[step],
                    state_recv.at[step, turn_of],
                    stream,
                    span,
                )
                if near == 0:
                    pl.when(stream != stream_id)(copy.start)
                else:
                    copy.start()
                return carry

            lax.fori_loop(0, streams, one, 0)

    def halo_copies(step, source):
        last = inner
        table = (
            (stream_id < streams - 1, source.at[:, pl.ds(last, width), :],
             stream_halo.at[step, 0], 0, (1, 0), stream_id > 0),
            (stream_id > 0, source.at[:, pl.ds(width, width), :],
             stream_halo.at[step, 1], 1, (-1, 0), stream_id < streams - 1),
            (span_id < spans - 1, span_edge.at[step, 1],
             span_halo.at[step, 0], 2, (0, 1), span_id > 0),
            (span_id > 0, span_edge.at[step, 0],
             span_halo.at[step, 1], 3, (0, -1), span_id < spans - 1),
        )
        result = []
        for sends, src, dst, slot, (ds, dp), receives in table:
            copy = remote(
                src,
                dst,
                halo_send.at[step, slot // 2],
                halo_recv.at[step, slot // 2],
                stream_id + ds,
                span_id + dp,
            )
            result.append((sends, receives, copy, dst))
        return result

    def wait_halo(step, sem):
        sides = ((stream_halo, stream_id, streams), (span_halo, span_id, spans))
        for axis, (halo, index, size) in enumerate(sides):
            inside = jnp.logical_and(index > 0, index < size - 1)

            @pl.when(inside)
            def _():
                wait_bytes(halo.at[step], sem.at[step, axis])

            @pl.when(jnp.logical_not(inside))
            def _():
                wait_bytes(halo.at[step, 0], sem.at[step, axis])

    def start_halo(step, source):
        for k in range(3):
            span_edge[step, 0, k] = source[k, pl.ds(width, planes, stride=width), :]
            span_edge[step, 1, k] = source[k, pl.ds(2 * width - 1, planes, stride=width), :]
        for sends, receives, copy, dst in halo_copies(step, source):
            pl.when(sends)(copy.start)

            @pl.when(jnp.logical_not(receives))
            def _():
                dst[...] = jnp.zeros(dst.shape, F32)

    def finish_halo(step, source):
        wait_halo(step, halo_recv)
        for k in range(3):
            source[k, pl.ds(0, width), :] = stream_halo[step, 0, k]
            source[k, pl.ds(width + inner, width), :] = stream_halo[step, 1, k]

    row_of = lax.broadcasted_iota(jnp.int32, (width, depth), 0)
    lane_from = lax.broadcasted_iota(jnp.int32, (depth, depth), 0)
    lane_to = lax.broadcasted_iota(jnp.int32, (depth, depth), 1)
    beside_lane = (jnp.abs(lane_from - lane_to) == 1).astype(F32).astype(BF16)
    band[...] = jnp.concatenate([beside_lane, beside_lane], axis=0)

    def stencil(step, source, target, offset):
        def several(c, carry):
            for k in range(3):
                first = pl.multiple_of((c * PLANES + 1) * width, width)
                block = source[k, pl.ds(first, PLANES * width), :]
                along = jnp.dot(
                    jnp.concatenate(split_two(block), axis=1),
                    band[...],
                    preferred_element_type=F32,
                )
                for q in range(PLANES):
                    start = pl.multiple_of(first + q * width, width)
                    here = block[q * width : (q + 1) * width]
                    ahead = source[k, pl.ds(start + width, width), :]
                    behind = source[k, pl.ds(start - width, width), :]
                    y_low = span_halo[step, 0, k, pl.ds(c * PLANES + q, 1), :]
                    y_high = span_halo[step, 1, k, pl.ds(c * PLANES + q, 1), :]
                    y_ahead = jnp.where(
                        row_of == width - 1, y_high, pltpu.roll(here, width - 1, 0)
                    )
                    y_behind = jnp.where(row_of == 0, y_low, pltpu.roll(here, 1, 0))
                    beside = y_ahead + y_behind + along[q * width : (q + 1) * width]
                    target[k, pl.ds(pl.multiple_of(start - width + offset, width), width), :] = (
                        (1.0 - 6.0 * TIME_STEP * VISCOSITY) * here
                        + TIME_STEP * (VISCOSITY - 0.5 * CONVECTION) * ahead
                        + TIME_STEP * (VISCOSITY + 0.5 * CONVECTION) * behind
                        + TIME_STEP * VISCOSITY * beside
                    )
            return carry

        lax.fori_loop(0, planes // PLANES, several, 0)

    def add_forcing(target, offset):
        def block(b, carry):
            start = pl.multiple_of(b * rows + offset, rows)
            spot = jnp.full((rows, depth), b, jnp.int32)
            for k in range(3):
                total = target[k, pl.ds(start, rows), :]
                for t in range(tiles):
                    total = total + jnp.where(homes[t] == spot, TIME_STEP * spread[t, k], 0.0)
                target[k, pl.ds(start, rows), :] = total
            return carry

        lax.fori_loop(0, inner // rows, block, 0)

    diagonal = (
        lax.broadcasted_iota(jnp.int32, (rows, block_width), 0)
        == lax.broadcasted_iota(jnp.int32, (rows, block_width), 1) // depth
    ).astype(F32).astype(BF16)

    def expand(part):
        return jnp.concatenate([part] * rows, axis=1) * diagonal

    def home_blocks():
        return [jnp.full((rows, depth), tile_block[t], jnp.int32) for t in range(tiles)]

    def sample(source):
        def look(b, found):
            start = pl.multiple_of(b * rows + width, rows)
            spot = jnp.full((rows, depth), b, jnp.int32)
            cells = [source[k, pl.ds(start, rows), :] for k in range(3)]
            return tuple(
                jnp.where(homes[t] == spot, cells[k], found[3 * t + k])
                for t in range(tiles)
                for k in range(3)
            )

        blank = jnp.zeros((rows, depth), F32)
        found = lax.fori_loop(0, inner // rows, look, (blank,) * (3 * tiles), unroll=4)
        speeds = []
        for t in range(tiles):
            left = jnp.concatenate(
                [expand(found[3 * t + k].astype(BF16)) for k in range(3)], axis=0
            )
            got = lax.dot_general(
                left, weights[pl.ds(t * TILE, TILE), :], NT, preferred_element_type=F32
            )
            speed = None
            for k in range(3):
                term = normals[k : k + 1, t * TILE : (t + 1) * TILE] * jnp.sum(
                    got[k * rows : (k + 1) * rows], axis=0, keepdims=True
                )
                speed = term if speed is None else speed + term
            speeds.append(speed)
        return PENALTY * jnp.concatenate(speeds, axis=1)

    def spread_push(push):
        for t in range(tiles):
            parts = []
            for k in range(3):
                half = normals[k : k + 1, t * TILE : (t + 1) * TILE] * push[
                    :, t * TILE : (t + 1) * TILE
                ]
                parts.append(expand(jnp.broadcast_to(half, (rows, TILE)).astype(BF16)))
            left = jnp.concatenate(parts, axis=0)
            right = jnp.concatenate(
                [weights[pl.ds(t * TILE, TILE), y * depth : (y + 1) * depth] for y in range(rows)],
                axis=0,
            )
            got = jnp.dot(left, right, preferred_element_type=F32)
            for k in range(3):
                spread[t, k] = got[k * rows : (k + 1) * rows]

    def panels_of(span, low, high):
        row = lax.broadcasted_iota(jnp.int32, ((high - low) * own, markers), 0)
        return row + (row // own + low) * (spans - 1) * own + (low + span) * own

    def both(value):
        high = value.astype(BF16).astype(F32)
        return jnp.concatenate([high, value - high], axis=0).astype(BF16)

    def seen_by(state, chosen):
        size = state.shape[0]
        every = jnp.dot(both(state), turned[...], preferred_element_type=F32)
        return jnp.sum(
            jnp.where(chosen, every[:size] + every[size:], 0.0), axis=0, keepdims=True
        )

    def load_of(push, chosen):
        size = chosen.shape[0]
        load = jnp.dot(
            both(jnp.where(chosen, push, 0.0)), mode[...], preferred_element_type=F32
        )
        return -(load[:size] + load[size:])

    def wait_state(step, turn):
        plan = plans[step][turn]
        fewer = among(step, plan)
        full = sum(high - low for _, low, high in plan)
        for lacks in (0, 1):

            @pl.when(fewer if lacks else jnp.logical_not(fewer))
            def _():
                wait_bytes(
                    shared_state.at[step, pl.ds(0, full - lacks)],
                    state_recv.at[step, turn],
                )

    def send_one(step, source, owner_stream, owner_span):
        stream = streams - 1 - owner_stream if step == 0 else owner_stream
        span = spans - 1 - owner_span if step == 0 else owner_span
        copy = remote(
            source, load_in.at[step, me], load_send.at[step], load_recv.at[step], stream, span
        )
        return stream * spans + span != me, copy

    def take_group(step, turn, speed):
        plan = plans[step][turn]
        wait_state(step, turn)
        chosen = jnp.concatenate(
            [panels_of(*range_of) == marker_panel[...] for range_of in plan], axis=0
        )
        state = jnp.concatenate(
            [
                shared_state[step, pl.ds(span * streams + low, high - low)].reshape(
                    (high - low) * own, modes
                )
                for span, low, high in plan
            ],
            axis=0,
        )
        term = seen_by(state, chosen)
        load = load_of(term - speed, chosen)
        at = 0
        for span, low, high in plan:
            size = (high - low) * own
            load_out[step, pl.ds(span * streams + low, high - low)] = load[
                at : at + size
            ].reshape(high - low, own, modes)
            at += size
        for span, low, high in plan:

            def one(stream, carry):
                sends, copy = send_one(
                    step, load_out.at[step, span * streams + stream], stream, span
                )
                pl.when(sends)(copy.start)
                return carry

            lax.fori_loop(low, high, one, 0)
        return term

    def close(step, terms, speed):
        load_in[step, me] = load_out[step, opposite if step == 0 else home]
        return functools.reduce(jnp.add, terms) - speed

    def wait_load(step):
        wait_bytes(load_in.at[step, pl.ds(0, count - 1)], load_recv.at[step])
        return jnp.sum(load_in[step], axis=0)

    def advance(table, load):
        position, rate, omega, zeta = (table[slot] for slot in range(4))
        rate = (rate + MODAL_STEP * (load - omega * omega * position)) / (
            1.0 + 2.0 * MODAL_STEP * zeta * omega
        )
        return position + MODAL_STEP * rate, rate

    wait_bytes(mine, in_sem.at[0])
    shared_state[0, home] = PENALTY * mine[1] - SPRING * mine[0]
    pl.semaphore_wait(barrier, count - 1)
    send_state(0)
    params = remote(mine, theirs, pair_send.at[0], pair_recv.at[0], far_stream, far_span)
    params.start()

    copies[4].wait()
    start_halo(0, field)
    for copy in copies[5:10]:
        copy.wait()
    homes = home_blocks()
    turned[...] = mode[...].astype(F32).T.astype(BF16)
    speed = sample(field)

    response = hot_response(
        own, mine[2], mine[3], freq_bins, hot_nodes, stress, hot_square, copies[10:]
    )
    for slot in range(4):
        response_last[pl.ds(slot * own, own)] = response[slot]
    terms = []
    terms.append(take_group(0, 0, speed))
    terms.append(take_group(0, 1, speed))
    terms.append(take_group(0, 2, speed))
    push = close(0, terms, speed)
    spread_push(push)
    finish_halo(0, field)
    stencil(0, field, advanced, width)
    add_forcing(advanced, width)
    start_halo(1, advanced)
    params.wait_recv()
    load = wait_load(0)
    position, rate = advance(theirs, load)
    shared_state[1, opposite] = PENALTY * rate - SPRING * position
    send_state(1)
    back_out[...] = load
    back = remote(back_out, back_in, pair_send.at[1], pair_recv.at[1], far_stream, far_span)
    back.start()
    speed = sample(advanced)
    terms = []
    terms.append(take_group(1, 0, speed))
    terms.append(take_group(1, 1, speed))
    terms.append(take_group(1, 2, speed))
    terms.append(take_group(1, 3, speed))
    push = close(1, terms, speed)
    spread_push(push)
    finish_halo(1, advanced)
    stencil(1, advanced, final, 0)
    add_forcing(final, 0)
    back.wait_recv()
    load = back_in[...]
    position, rate = advance(mine, load)
    tail[0] = position
    tail[1] = rate
    tail[2] = mine[2]
    tail[3] = mine[3]
    tail[4] = STEPS * base_load[...] + load * load
    tail[5] = wait_load(1)
    for step in range(STEPS):
        everyone = load_in.at[0, pl.ds(0, count - 1)]
        wait_bytes(everyone, state_send.at[step])
        wait_bytes(everyone, load_send.at[step])
        wait_halo(step, halo_send)
    params.wait_send()
    back.wait_send()


def hot_response(own, omega, zeta, freq_bins, hot_nodes, stress, hot_square, copies):
    modes = stress.shape[1]
    hots = hot_nodes.shape[1]
    for copy in copies:
        copy.wait()
    nodes = jnp.concatenate([hot_nodes[p : p + 1, :] for p in range(own)], axis=1)
    part = stress.shape[0] // NODE_PARTS
    hot_rows = None
    for q in range(NODE_PARTS):
        ids = lax.broadcasted_iota(jnp.int32, (part, own * hots), 0) + q * part
        picked = (ids == nodes).astype(F32).astype(BF16)
        found = lax.dot_general(
            stress[pl.ds(q * part, part), :], picked, TN, preferred_element_type=F32
        )
        hot_rows = found if hot_rows is None else hot_rows + found
    hot_square[...] = hot_rows * hot_rows

    lists = [[], [], [], []]
    columns = []
    for q in range(freq_bins.shape[0]):
        line = freq_bins[q : q + 1, :].astype(F32) * BIN_WIDTH
        columns.append(jnp.broadcast_to(line, (modes, modes)).T)
    for p in range(own):
        omega_sq = omega[p : p + 1] * omega[p : p + 1]
        factor = 2.0 * zeta[p : p + 1] * omega[p : p + 1]
        sums = [None] * 4
        for column in columns:
            square = column * column
            detune = omega_sq - square
            damping = factor * column
            response = 1.0 / (detune * detune + damping * damping)
            second = response * square
            terms = (response, response * column, second, second * square)
            for slot in range(4):
                term = jnp.sum(terms[slot], axis=0, keepdims=True)
                sums[slot] = term if sums[slot] is None else sums[slot] + term
        for slot in range(4):
            lists[slot].append(sums[slot])
    return [jnp.concatenate(parts, axis=0) for parts in lists]


def dirlik(moment_zero, moment_one, moment_two, moment_four):
    peak_rate = jnp.sqrt(moment_four / moment_two)
    mean_freq = moment_one / moment_zero * jnp.sqrt(moment_two / moment_four)
    irregular = moment_two / jnp.sqrt(moment_zero * moment_four)
    irregular_sq = irregular * irregular
    share_one = jnp.maximum(2.0 * (mean_freq - irregular_sq) / (1.0 + irregular_sq), 0.02)
    share_sq = share_one * share_one
    denominator = jnp.maximum(1.0 - irregular - share_one + share_sq, 0.02)
    ratio_term = (irregular - mean_freq - share_sq) / denominator
    share_two = denominator / jnp.maximum(1.0 - ratio_term, 0.05)
    share_three = 1.0 - share_one - share_two
    scale_term = jnp.maximum(
        1.25 * (irregular - share_three - share_two * ratio_term) / share_one, 0.05
    )
    size = jnp.abs(ratio_term)
    bracket = 6.0 * share_one * (scale_term * scale_term * scale_term)
    bracket = bracket + 2.0**1.5 * GAMMA_HALF * (size * size * size * share_two + share_three)
    bracket = jnp.maximum(bracket, 0.1)
    return (
        jnp.log(peak_rate) + jnp.log(jnp.full_like(bracket, 8.0))
        + 1.5 * jnp.log(moment_zero) + jnp.log(bracket)
    )


def finish(
    final,
    tail,
    response,
    hot_square,
    final_out,
    disp_out,
    rate_out,
    damage_out,
    disp_last,
    rate_last,
    damage_last,
    sem,
):
    pairs = (
        (final, final_out),
        (disp_last, disp_out),
        (rate_last, rate_out),
        (damage_last, damage_out),
    )
    copies = [
        pltpu.make_async_copy(source, target, sem.at[slot])
        for slot, (source, target) in enumerate(pairs)
    ]
    copies[0].start()
    own, hots = damage_last.shape
    position, rate, omega, zeta, power, load = (tail[slot] for slot in range(6))
    rate = (rate + MODAL_STEP * (load - omega * omega * position)) / (
        1.0 + 2.0 * MODAL_STEP * zeta * omega
    )
    disp_last[...] = position + MODAL_STEP * rate
    rate_last[...] = rate
    copies[1].start()
    copies[2].start()
    power = (power + load * load) / STEPS
    full = jnp.dot(
        response[...] * jnp.concatenate([power] * 4, axis=0),
        hot_square[...],
        precision=lax.Precision.HIGHEST,
        preferred_element_type=F32,
    )
    mine = (
        lax.broadcasted_iota(jnp.int32, (own, own * hots), 1) // hots
        == lax.broadcasted_iota(jnp.int32, (own, own * hots), 0)
    )
    moments = [
        jnp.sum(jnp.where(mine, full[slot * own : (slot + 1) * own], 0.0), axis=0, keepdims=True)
        * BIN_WIDTH
        for slot in range(4)
    ]
    damage = dirlik(*moments)
    for p in range(own):
        damage_last[p : p + 1, :] = damage[:, p * hots : (p + 1) * hots]
    copies[3].start()
    for copy in copies:
        copy.wait()


def body(
    velocity,
    weights,
    tile_block,
    normals,
    marker_panel,
    mode_shape,
    modal_disp,
    modal_rate,
    mode_omega,
    mode_zeta,
    base_load,
    stress_modes,
    hot_nodes,
    freq_bins,
):
    streams = lax.axis_size("stream")
    spans = lax.axis_size("span")
    count = streams * spans
    _, planes, width, depth = velocity.shape
    markers, block_width = weights.shape
    own, modes = modal_disp.shape
    hots = hot_nodes.shape[1]
    inner = planes * width
    rows = block_width // depth
    held = pl.BlockSpec(memory_space=pltpu.VMEM)
    stay = pl.BlockSpec(memory_space=pltpu.MemorySpace.HBM)
    small = pltpu.VMEM((own, modes), F32)
    bins = freq_bins.reshape(-1, modes)
    results = pl.pallas_call(
        functools.partial(kernel, streams, spans, planes, width),
        out_shape=(
            pltpu.VMEM((3, inner, depth), F32),
            pltpu.VMEM((6, own, modes), F32),
            pltpu.VMEM((4 * own, modes), F32),
            pltpu.VMEM((modes, own * hots), F32),
        ),
        in_specs=[stay] * 14,
        out_specs=(held,) * 4,
        scratch_shapes=[
            pltpu.VMEM((4, own, modes), F32),
            pltpu.VMEM((4, own, modes), F32),
            pltpu.VMEM((1, markers), jnp.int32),
            pltpu.SMEM(tile_block.shape, jnp.int32),
            pltpu.VMEM(mode_shape.shape, BF16),
            pltpu.VMEM(weights.shape, BF16),
            pltpu.VMEM(normals.shape, F32),
            pltpu.VMEM(stress_modes.shape, BF16),
            pltpu.VMEM(hot_nodes.shape, jnp.int32),
            pltpu.VMEM(bins.shape, jnp.int32),
            small,
            pltpu.VMEM((3, inner + 2 * width, depth), F32),
            pltpu.VMEM((3, inner + 2 * width, depth), F32),
            pltpu.VMEM((2 * depth, depth), BF16),
            pltpu.VMEM((modes, markers), BF16),
            pltpu.VMEM((markers // TILE, 3, rows, depth), F32),
            pltpu.VMEM((STEPS, count, own, modes), F32),
            pltpu.VMEM((STEPS, count, own, modes), F32),
            pltpu.VMEM((STEPS, count, own, modes), F32),
            small,
            small,
            pltpu.VMEM((STEPS, 2, 3, width, depth), F32),
            pltpu.VMEM((STEPS, 2, 3, planes, depth), F32),
            pltpu.VMEM((STEPS, 2, 3, planes, depth), F32),
            pltpu.SemaphoreType.DMA((11,)),
            pltpu.SemaphoreType.DMA((STEPS,)),
            pltpu.SemaphoreType.DMA((STEPS, max(len(steps) for steps in GROUPS))),
            pltpu.SemaphoreType.DMA((STEPS,)),
            pltpu.SemaphoreType.DMA((STEPS,)),
            pltpu.SemaphoreType.DMA((2,)),
            pltpu.SemaphoreType.DMA((2,)),
            pltpu.SemaphoreType.DMA((STEPS, 2)),
            pltpu.SemaphoreType.DMA((STEPS, 2)),
        ],
        compiler_params=pltpu.CompilerParams(
            collective_id=0, has_side_effects=True, vmem_limit_bytes=60 * 1024 * 1024
        ),
        name="coupled_steps",
    )(
        modal_disp,
        modal_rate,
        mode_omega,
        mode_zeta,
        marker_panel.reshape(1, markers),
        tile_block,
        velocity.reshape(3, inner, depth),
        mode_shape,
        weights,
        normals,
        stress_modes,
        hot_nodes,
        bins,
        base_load,
    )
    results = pl.pallas_call(
        finish,
        out_shape=[
            jax.ShapeDtypeStruct((3, inner, depth), F32),
            jax.ShapeDtypeStruct((own, modes), F32),
            jax.ShapeDtypeStruct((own, modes), F32),
            jax.ShapeDtypeStruct((own, hots), F32),
        ],
        in_specs=[held] * 4,
        out_specs=[stay] * 4,
        scratch_shapes=[
            small,
            small,
            pltpu.VMEM((own, hots), F32),
            pltpu.SemaphoreType.DMA((4,)),
        ],
        compiler_params=pltpu.CompilerParams(vmem_limit_bytes=4 * 1024 * 1024),
        name="finish",
    )(*results)
    return (results[0].reshape(velocity.shape),) + tuple(results[1:])


def solution(mesh):
    placed = (
        P(None, "stream", "span", None),
        P(("stream", "span"), None),
        P(("stream", "span")),
        P(None, ("stream", "span")),
        P(("stream", "span")),
        P(("stream", "span"), None),
        P(("stream", "span"), None),
        P(("stream", "span"), None),
        P(("stream", "span"), None),
        P(("stream", "span"), None),
        P(("stream", "span"), None),
        P(),
        P(("stream", "span"), None),
        P(),
    )
    return jax.shard_map(
        body,
        mesh=mesh,
        in_specs=placed,
        out_specs=(
            P(None, "stream", "span", None),
            P(("stream", "span"), None),
            P(("stream", "span"), None),
            P(("stream", "span"), None),
        ),
        check_vma=False,
    )
```

```python
import functools

import jax
import jax.numpy as jnp
from jax import lax
from jax.experimental import pallas as pl
from jax.experimental.pallas import tpu as pltpu
from jax.sharding import PartitionSpec as P

TILE = 128
STEPS = 2

PENALTY = 1.0
SPRING = 0.5
TIME_STEP = 0.2
VISCOSITY = 0.5
CONVECTION = 1.0
MODAL_STEP = 0.5
BIN_WIDTH = 0.002
GAMMA_HALF = 1.3293404

F32 = jnp.float32
BF16 = jnp.bfloat16
NT = (((1,), (1,)), ((), ()))
TN = (((0,), (0,)), ((), ()))
NODE_PARTS = 4
PLANES = 4
EVERY = 1 << 16
GROUPS = (
    ([(0, 0, 2), (1, 0, 2)], [(0, 2, EVERY), (1, 2, EVERY)], [(2, 0, EVERY), (3, 0, EVERY)]),
    ([(0, 0, 2), (1, 0, 2)], [(0, 2, EVERY), (1, 2, EVERY)], [(2, 0, EVERY)], [(3, 0, EVERY)]),
)


def split_two(value):
    high = value.astype(BF16)
    low = (value - high.astype(F32)).astype(BF16)
    return high, low


def kernel(
    streams,
    spans,
    planes,
    width,
    disp_hbm,
    rate_hbm,
    omega_hbm,
    zeta_hbm,
    panel_hbm,
    block_hbm,
    velocity_hbm,
    mode_hbm,
    weights_hbm,
    normals_hbm,
    stress_hbm,
    nodes_hbm,
    bins_hbm,
    base_hbm,
    final,
    tail,
    response_last,
    hot_square,
    mine,
    theirs,
    marker_panel,
    tile_block,
    mode,
    weights,
    normals,
    stress,
    hot_nodes,
    freq_bins,
    base_load,
    field,
    advanced,
    band,
    turned,
    spread,
    shared_state,
    load_out,
    load_in,
    back_out,
    back_in,
    stream_halo,
    span_edge,
    span_halo,
    in_sem,
    all_send,
    state_recv,
    load_recv,
    pair_send,
    pair_recv,
    halo_send,
    halo_recv,
):
    count = streams * spans
    stream_id = lax.axis_index("stream")
    span_id = lax.axis_index("span")
    me = stream_id * spans + span_id
    far_stream = streams - 1 - stream_id
    far_span = spans - 1 - span_id
    own = mine.shape[1]
    modes = mine.shape[2]
    home = span_id * streams + stream_id
    opposite = far_span * streams + far_stream
    plans = [
        [[(span, low, min(high, streams)) for span, low, high in plan] for plan in steps]
        for steps in GROUPS
    ]

    def among(step, plan):
        stream = stream_id if step == 0 else far_stream
        at_span = span_id if step == 0 else far_span
        found = None
        for span, low, high in plan:
            here = jnp.logical_and(
                at_span == span, jnp.logical_and(stream >= low, stream < high)
            )
            found = here if found is None else jnp.logical_or(found, here)
        return found

    depth = field.shape[2]
    markers = mode.shape[0]
    tiles = markers // TILE
    block_width = weights.shape[1]
    rows = block_width // depth
    inner = planes * width

    pairs = (
        (disp_hbm, mine.at[0]),
        (rate_hbm, mine.at[1]),
        (omega_hbm, mine.at[2]),
        (zeta_hbm, mine.at[3]),
        (velocity_hbm, field.at[:, pl.ds(width, inner), :]),
        (block_hbm, tile_block),
        (normals_hbm, normals),
        (weights_hbm, weights),
        (panel_hbm, marker_panel),
        (mode_hbm, mode),
        (stress_hbm, stress),
        (nodes_hbm, hot_nodes),
        (bins_hbm, freq_bins),
        (base_hbm, base_load),
    )
    copies = [
        pltpu.make_async_copy(source, target, in_sem.at[max(slot - 3, 0)])
        for slot, (source, target) in enumerate(pairs)
    ]

    if spans == 4:
        upper = span_id // 2
        nearest = [
            span_id,
            span_id + 1 - 2 * (span_id % 2),
            2 - upper,
            3 - 3 * upper,
        ]
    else:
        nearest = [(span_id + shift) % spans for shift in range(spans)]
    turn = 1 - stream_id // (streams // 2)

    def far_first(step):
        return step + (streams - 1 - 2 * step) * turn

    def place(stream, span):
        return {"stream": stream, "span": span}

    barrier = pltpu.get_barrier_semaphore()
    for near, span in reversed(list(enumerate(nearest))):

        def greet(step, carry):
            stream = far_first(step)

            def signal():
                pl.semaphore_signal(
                    barrier,
                    inc=1,
                    device_id=place(stream, span),
                    device_id_type=pl.DeviceIdType.MESH,
                )

            if near == 0:
                pl.when(stream != stream_id)(signal)
            else:
                signal()
            return carry

        lax.fori_loop(0, streams, greet, 0)
    for copy in copies:
        copy.start()

    def remote(source, target, send, recv, stream, span):
        return pltpu.make_async_remote_copy(
            src_ref=source,
            dst_ref=target,
            send_sem=send,
            recv_sem=recv,
            device_id=place(stream, span),
            device_id_type=pl.DeviceIdType.MESH,
        )

    def wait_bytes(part, sem):
        pltpu.make_async_copy(part, part, sem).wait()

    def send_state(step):
        block = shared_state.at[step, home if step == 0 else opposite]
        turn_of = len(plans[step]) - 1
        for turn, plan in enumerate(plans[step][:-1]):
            turn_of = jnp.where(among(step, plan), turn, turn_of)
        for near, span in reversed(list(enumerate(nearest))):

            def one(turned, carry):
                stream = far_first(turned)
                copy = remote(
                    block,
                    block,
                    all_send.at[0],
                    state_recv.at[step, turn_of],
                    stream,
                    span,
                )
                if near == 0:
                    pl.when(stream != stream_id)(copy.start)
                else:
                    copy.start()
                return carry

            lax.fori_loop(0, streams, one, 0)

    def halo_copies(step, source):
        last = inner
        table = (
            (stream_id < streams - 1, source.at[:, pl.ds(last, width), :],
             stream_halo.at[step, 0], 0, (1, 0), stream_id > 0),
            (stream_id > 0, source.at[:, pl.ds(width, width), :],
             stream_halo.at[step, 1], 1, (-1, 0), stream_id < streams - 1),
            (span_id < spans - 1, span_edge.at[step, 1],
             span_halo.at[step, 0], 2, (0, 1), span_id > 0),
            (span_id > 0, span_edge.at[step, 0],
             span_halo.at[step, 1], 3, (0, -1), span_id < spans - 1),
        )
        result = []
        for sends, src, dst, slot, (ds, dp), receives in table:
            copy = remote(
                src,
                dst,
                halo_send.at[step, slot // 2],
                halo_recv.at[step, slot // 2],
                stream_id + ds,
                span_id + dp,
            )
            result.append((sends, receives, copy, dst))
        return result

    def wait_halo(step, sem):
        sides = ((stream_halo, stream_id, streams), (span_halo, span_id, spans))
        for axis, (halo, index, size) in enumerate(sides):
            inside = jnp.logical_and(index > 0, index < size - 1)

            @pl.when(inside)
            def _():
                wait_bytes(halo.at[step], sem.at[step, axis])

            @pl.when(jnp.logical_not(inside))
            def _():
                wait_bytes(halo.at[step, 0], sem.at[step, axis])

    def start_halo(step, source):
        for k in range(3):
            span_edge[step, 0, k] = source[k, pl.ds(width, planes, stride=width), :]
            span_edge[step, 1, k] = source[k, pl.ds(2 * width - 1, planes, stride=width), :]
        for sends, receives, copy, dst in halo_copies(step, source):
            pl.when(sends)(copy.start)

            @pl.when(jnp.logical_not(receives))
            def _():
                dst[...] = jnp.zeros(dst.shape, F32)

    def finish_halo(step, source):
        wait_halo(step, halo_recv)
        for k in range(3):
            source[k, pl.ds(0, width), :] = stream_halo[step, 0, k]
            source[k, pl.ds(width + inner, width), :] = stream_halo[step, 1, k]

    row_of = lax.broadcasted_iota(jnp.int32, (width, depth), 0)
    lane_from = lax.broadcasted_iota(jnp.int32, (depth, depth), 0)
    lane_to = lax.broadcasted_iota(jnp.int32, (depth, depth), 1)
    beside_lane = (jnp.abs(lane_from - lane_to) == 1).astype(F32).astype(BF16)
    band[...] = jnp.concatenate([beside_lane, beside_lane], axis=0)

    def stencil(step, source, target, offset):
        def several(c, carry):
            for k in range(3):
                first = pl.multiple_of((c * PLANES + 1) * width, width)
                block = source[k, pl.ds(first, PLANES * width), :]
                along = jnp.dot(
                    jnp.concatenate(split_two(block), axis=1),
                    band[...],
                    preferred_element_type=F32,
                )
                for q in range(PLANES):
                    start = pl.multiple_of(first + q * width, width)
                    here = block[q * width : (q + 1) * width]
                    ahead = source[k, pl.ds(start + width, width), :]
                    behind = source[k, pl.ds(start - width, width), :]
                    y_low = span_halo[step, 0, k, pl.ds(c * PLANES + q, 1), :]
                    y_high = span_halo[step, 1, k, pl.ds(c * PLANES + q, 1), :]
                    y_ahead = jnp.where(
                        row_of == width - 1, y_high, pltpu.roll(here, width - 1, 0)
                    )
                    y_behind = jnp.where(row_of == 0, y_low, pltpu.roll(here, 1, 0))
                    beside = y_ahead + y_behind + along[q * width : (q + 1) * width]
                    target[k, pl.ds(pl.multiple_of(start - width + offset, width), width), :] = (
                        (1.0 - 6.0 * TIME_STEP * VISCOSITY) * here
                        + TIME_STEP * (VISCOSITY - 0.5 * CONVECTION) * ahead
                        + TIME_STEP * (VISCOSITY + 0.5 * CONVECTION) * behind
                        + TIME_STEP * VISCOSITY * beside
                    )
            return carry

        lax.fori_loop(0, planes // PLANES, several, 0)

    def add_forcing(target, offset):
        def block(b, carry):
            start = pl.multiple_of(b * rows + offset, rows)
            spot = jnp.full((rows, depth), b, jnp.int32)
            for k in range(3):
                total = target[k, pl.ds(start, rows), :]
                for t in range(tiles):
                    total = total + jnp.where(homes[t] == spot, TIME_STEP * spread[t, k], 0.0)
                target[k, pl.ds(start, rows), :] = total
            return carry

        lax.fori_loop(0, inner // rows, block, 0)

    diagonal = (
        lax.broadcasted_iota(jnp.int32, (rows, block_width), 0)
        == lax.broadcasted_iota(jnp.int32, (rows, block_width), 1) // depth
    ).astype(F32).astype(BF16)

    def expand(part):
        return jnp.concatenate([part] * rows, axis=1) * diagonal

    def home_blocks():
        return [jnp.full((rows, depth), tile_block[t], jnp.int32) for t in range(tiles)]

    def sample(source):
        def look(b, found):
            start = pl.multiple_of(b * rows + width, rows)
            spot = jnp.full((rows, depth), b, jnp.int32)
            cells = [source[k, pl.ds(start, rows), :] for k in range(3)]
            return tuple(
                jnp.where(homes[t] == spot, cells[k], found[3 * t + k])
                for t in range(tiles)
                for k in range(3)
            )

        blank = jnp.zeros((rows, depth), F32)
        found = lax.fori_loop(0, inner // rows, look, (blank,) * (3 * tiles), unroll=4)
        speeds = []
        for t in range(tiles):
            left = jnp.concatenate(
                [expand(found[3 * t + k].astype(BF16)) for k in range(3)], axis=0
            )
            got = lax.dot_general(
                left, weights[pl.ds(t * TILE, TILE), :], NT, preferred_element_type=F32
            )
            speed = None
            for k in range(3):
                term = normals[k : k + 1, t * TILE : (t + 1) * TILE] * jnp.sum(
                    got[k * rows : (k + 1) * rows], axis=0, keepdims=True
                )
                speed = term if speed is None else speed + term
            speeds.append(speed)
        return PENALTY * jnp.concatenate(speeds, axis=1)

    def spread_push(push):
        for t in range(tiles):
            parts = []
            for k in range(3):
                half = normals[k : k + 1, t * TILE : (t + 1) * TILE] * push[
                    :, t * TILE : (t + 1) * TILE
                ]
                parts.append(expand(jnp.broadcast_to(half, (rows, TILE)).astype(BF16)))
            left = jnp.concatenate(parts, axis=0)
            right = jnp.concatenate(
                [weights[pl.ds(t * TILE, TILE), y * depth : (y + 1) * depth] for y in range(rows)],
                axis=0,
            )
            got = jnp.dot(left, right, preferred_element_type=F32)
            for k in range(3):
                spread[t, k] = got[k * rows : (k + 1) * rows]

    def panels_of(span, low, high):
        row = lax.broadcasted_iota(jnp.int32, ((high - low) * own, markers), 0)
        return row + (row // own + low) * (spans - 1) * own + (low + span) * own

    def both(value):
        high = value.astype(BF16).astype(F32)
        return jnp.concatenate([high, value - high], axis=0).astype(BF16)

    def seen_by(state, chosen):
        size = state.shape[0]
        every = jnp.dot(both(state), turned[...], preferred_element_type=F32)
        return jnp.sum(
            jnp.where(chosen, every[:size] + every[size:], 0.0), axis=0, keepdims=True
        )

    def load_of(push, chosen):
        size = chosen.shape[0]
        load = jnp.dot(
            both(jnp.where(chosen, push, 0.0)), mode[...], preferred_element_type=F32
        )
        return -(load[:size] + load[size:])

    def wait_state(step, turn):
        plan = plans[step][turn]
        fewer = among(step, plan)
        full = sum(high - low for _, low, high in plan)
        for lacks in (0, 1):

            @pl.when(fewer if lacks else jnp.logical_not(fewer))
            def _():
                wait_bytes(
                    shared_state.at[step, pl.ds(0, full - lacks)],
                    state_recv.at[step, turn],
                )

    def send_one(step, source, owner_stream, owner_span):
        stream = streams - 1 - owner_stream if step == 0 else owner_stream
        span = spans - 1 - owner_span if step == 0 else owner_span
        copy = remote(
            source, load_in.at[step, me], all_send.at[0], load_recv.at[step], stream, span
        )
        return stream * spans + span != me, copy

    def take_group(step, turn, speed):
        plan = plans[step][turn]
        wait_state(step, turn)
        chosen = jnp.concatenate(
            [panels_of(*range_of) == marker_panel[...] for range_of in plan], axis=0
        )
        state = jnp.concatenate(
            [
                shared_state[step, pl.ds(span * streams + low, high - low)].reshape(
                    (high - low) * own, modes
                )
                for span, low, high in plan
            ],
            axis=0,
        )
        term = seen_by(state, chosen)
        load = load_of(term - speed, chosen)
        at = 0
        for span, low, high in plan:
            size = (high - low) * own
            load_out[step, pl.ds(span * streams + low, high - low)] = load[
                at : at + size
            ].reshape(high - low, own, modes)
            at += size
        for span, low, high in plan:

            def one(stream, carry):
                sends, copy = send_one(
                    step, load_out.at[step, span * streams + stream], stream, span
                )
                pl.when(sends)(copy.start)
                return carry

            lax.fori_loop(low, high, one, 0)
        return term

    def close(step, terms, speed):
        load_in[step, me] = load_out[step, opposite if step == 0 else home]
        return functools.reduce(jnp.add, terms) - speed

    def wait_load(step):
        wait_bytes(load_in.at[step, pl.ds(0, count - 1)], load_recv.at[step])
        return jnp.sum(load_in[step], axis=0)

    def advance(table, load):
        position, rate, omega, zeta = (table[slot] for slot in range(4))
        rate = (rate + MODAL_STEP * (load - omega * omega * position)) / (
            1.0 + 2.0 * MODAL_STEP * zeta * omega
        )
        return position + MODAL_STEP * rate, rate

    wait_bytes(mine, in_sem.at[0])
    shared_state[0, home] = PENALTY * mine[1] - SPRING * mine[0]
    pl.semaphore_wait(barrier, count - 1)
    send_state(0)
    params = remote(mine, theirs, pair_send.at[0], pair_recv.at[0], far_stream, far_span)
    params.start()

    copies[4].wait()
    start_halo(0, field)
    for copy in copies[5:10]:
        copy.wait()
    homes = home_blocks()
    turned[...] = mode[...].astype(F32).T.astype(BF16)
    speed = sample(field)

    response = hot_response(
        own, mine[2], mine[3], freq_bins, hot_nodes, stress, hot_square, copies[10:]
    )
    for slot in range(4):
        response_last[pl.ds(slot * own, own)] = response[slot]
    terms = []
    terms.append(take_group(0, 0, speed))
    terms.append(take_group(0, 1, speed))
    terms.append(take_group(0, 2, speed))
    push = close(0, terms, speed)
    spread_push(push)
    finish_halo(0, field)
    stencil(0, field, advanced, width)
    add_forcing(advanced, width)
    start_halo(1, advanced)
    params.wait_recv()
    load = wait_load(0)
    position, rate = advance(theirs, load)
    shared_state[1, opposite] = PENALTY * rate - SPRING * position
    send_state(1)
    back_out[...] = load
    back = remote(back_out, back_in, pair_send.at[1], pair_recv.at[1], far_stream, far_span)
    back.start()
    speed = sample(advanced)
    terms = []
    terms.append(take_group(1, 0, speed))
    terms.append(take_group(1, 1, speed))
    terms.append(take_group(1, 2, speed))
    terms.append(take_group(1, 3, speed))
    push = close(1, terms, speed)
    spread_push(push)
    finish_halo(1, advanced)
    stencil(1, advanced, final, 0)
    add_forcing(final, 0)
    back.wait_recv()
    load = back_in[...]
    position, rate = advance(mine, load)
    tail[0] = position
    tail[1] = rate
    tail[2] = mine[2]
    tail[3] = mine[3]
    tail[4] = STEPS * base_load[...] + load * load
    tail[5] = wait_load(1)
    for step in range(STEPS):
        everyone = load_in.at[0, pl.ds(0, count - 1)]
        wait_bytes(everyone, all_send.at[0])
        wait_bytes(everyone, all_send.at[0])
        wait_halo(step, halo_send)
    params.wait_send()
    back.wait_send()


def hot_response(own, omega, zeta, freq_bins, hot_nodes, stress, hot_square, copies):
    modes = stress.shape[1]
    hots = hot_nodes.shape[1]
    for copy in copies:
        copy.wait()
    nodes = jnp.concatenate([hot_nodes[p : p + 1, :] for p in range(own)], axis=1)
    part = stress.shape[0] // NODE_PARTS
    hot_rows = None
    for q in range(NODE_PARTS):
        ids = lax.broadcasted_iota(jnp.int32, (part, own * hots), 0) + q * part
        picked = (ids == nodes).astype(F32).astype(BF16)
        found = lax.dot_general(
            stress[pl.ds(q * part, part), :], picked, TN, preferred_element_type=F32
        )
        hot_rows = found if hot_rows is None else hot_rows + found
    hot_square[...] = hot_rows * hot_rows

    lists = [[], [], [], []]
    columns = []
    for q in range(freq_bins.shape[0]):
        line = freq_bins[q : q + 1, :].astype(F32) * BIN_WIDTH
        columns.append(jnp.broadcast_to(line, (modes, modes)).T)
    for p in range(own):
        omega_sq = omega[p : p + 1] * omega[p : p + 1]
        factor = 2.0 * zeta[p : p + 1] * omega[p : p + 1]
        sums = [None] * 4
        for column in columns:
            square = column * column
            detune = omega_sq - square
            damping = factor * column
            response = 1.0 / (detune * detune + damping * damping)
            second = response * square
            terms = (response, response * column, second, second * square)
            for slot in range(4):
                term = jnp.sum(terms[slot], axis=0, keepdims=True)
                sums[slot] = term if sums[slot] is None else sums[slot] + term
        for slot in range(4):
            lists[slot].append(sums[slot])
    return [jnp.concatenate(parts, axis=0) for parts in lists]


def dirlik(moment_zero, moment_one, moment_two, moment_four):
    peak_rate = jnp.sqrt(moment_four / moment_two)
    mean_freq = moment_one / moment_zero * jnp.sqrt(moment_two / moment_four)
    irregular = moment_two / jnp.sqrt(moment_zero * moment_four)
    irregular_sq = irregular * irregular
    share_one = jnp.maximum(2.0 * (mean_freq - irregular_sq) / (1.0 + irregular_sq), 0.02)
    share_sq = share_one * share_one
    denominator = jnp.maximum(1.0 - irregular - share_one + share_sq, 0.02)
    ratio_term = (irregular - mean_freq - share_sq) / denominator
    share_two = denominator / jnp.maximum(1.0 - ratio_term, 0.05)
    share_three = 1.0 - share_one - share_two
    scale_term = jnp.maximum(
        1.25 * (irregular - share_three - share_two * ratio_term) / share_one, 0.05
    )
    size = jnp.abs(ratio_term)
    bracket = 6.0 * share_one * (scale_term * scale_term * scale_term)
    bracket = bracket + 2.0**1.5 * GAMMA_HALF * (size * size * size * share_two + share_three)
    bracket = jnp.maximum(bracket, 0.1)
    return (
        jnp.log(peak_rate) + jnp.log(jnp.full_like(bracket, 8.0))
        + 1.5 * jnp.log(moment_zero) + jnp.log(bracket)
    )


def finish(
    final,
    tail,
    response,
    hot_square,
    final_out,
    disp_out,
    rate_out,
    damage_out,
    disp_last,
    rate_last,
    damage_last,
    sem,
):
    pairs = (
        (final, final_out),
        (disp_last, disp_out),
        (rate_last, rate_out),
        (damage_last, damage_out),
    )
    copies = [
        pltpu.make_async_copy(source, target, sem.at[slot])
        for slot, (source, target) in enumerate(pairs)
    ]
    copies[0].start()
    own, hots = damage_last.shape
    position, rate, omega, zeta, power, load = (tail[slot] for slot in range(6))
    rate = (rate + MODAL_STEP * (load - omega * omega * position)) / (
        1.0 + 2.0 * MODAL_STEP * zeta * omega
    )
    disp_last[...] = position + MODAL_STEP * rate
    rate_last[...] = rate
    copies[1].start()
    copies[2].start()
    power = (power + load * load) / STEPS
    full = jnp.dot(
        response[...] * jnp.concatenate([power] * 4, axis=0),
        hot_square[...],
        precision=lax.Precision.HIGHEST,
        preferred_element_type=F32,
    )
    mine = (
        lax.broadcasted_iota(jnp.int32, (own, own * hots), 1) // hots
        == lax.broadcasted_iota(jnp.int32, (own, own * hots), 0)
    )
    moments = [
        jnp.sum(jnp.where(mine, full[slot * own : (slot + 1) * own], 0.0), axis=0, keepdims=True)
        * BIN_WIDTH
        for slot in range(4)
    ]
    damage = dirlik(*moments)
    for p in range(own):
        damage_last[p : p + 1, :] = damage[:, p * hots : (p + 1) * hots]
    copies[3].start()
    for copy in copies:
        copy.wait()


def body(
    velocity,
    weights,
    tile_block,
    normals,
    marker_panel,
    mode_shape,
    modal_disp,
    modal_rate,
    mode_omega,
    mode_zeta,
    base_load,
    stress_modes,
    hot_nodes,
    freq_bins,
):
    streams = lax.axis_size("stream")
    spans = lax.axis_size("span")
    count = streams * spans
    _, planes, width, depth = velocity.shape
    markers, block_width = weights.shape
    own, modes = modal_disp.shape
    hots = hot_nodes.shape[1]
    inner = planes * width
    rows = block_width // depth
    held = pl.BlockSpec(memory_space=pltpu.VMEM)
    stay = pl.BlockSpec(memory_space=pltpu.MemorySpace.HBM)
    small = pltpu.VMEM((own, modes), F32)
    bins = freq_bins.reshape(-1, modes)
    results = pl.pallas_call(
        functools.partial(kernel, streams, spans, planes, width),
        out_shape=(
            pltpu.VMEM((3, inner, depth), F32),
            pltpu.VMEM((6, own, modes), F32),
            pltpu.VMEM((4 * own, modes), F32),
            pltpu.VMEM((modes, own * hots), F32),
        ),
        in_specs=[stay] * 14,
        out_specs=(held,) * 4,
        scratch_shapes=[
            pltpu.VMEM((4, own, modes), F32),
            pltpu.VMEM((4, own, modes), F32),
            pltpu.VMEM((1, markers), jnp.int32),
            pltpu.SMEM(tile_block.shape, jnp.int32),
            pltpu.VMEM(mode_shape.shape, BF16),
            pltpu.VMEM(weights.shape, BF16),
            pltpu.VMEM(normals.shape, F32),
            pltpu.VMEM(stress_modes.shape, BF16),
            pltpu.VMEM(hot_nodes.shape, jnp.int32),
            pltpu.VMEM(bins.shape, jnp.int32),
            small,
            pltpu.VMEM((3, inner + 2 * width, depth), F32),
            pltpu.VMEM((3, inner + 2 * width, depth), F32),
            pltpu.VMEM((2 * depth, depth), BF16),
            pltpu.VMEM((modes, markers), BF16),
            pltpu.VMEM((markers // TILE, 3, rows, depth), F32),
            pltpu.VMEM((STEPS, count, own, modes), F32),
            pltpu.VMEM((STEPS, count, own, modes), F32),
            pltpu.VMEM((STEPS, count, own, modes), F32),
            small,
            small,
            pltpu.VMEM((STEPS, 2, 3, width, depth), F32),
            pltpu.VMEM((STEPS, 2, 3, planes, depth), F32),
            pltpu.VMEM((STEPS, 2, 3, planes, depth), F32),
            pltpu.SemaphoreType.DMA((11,)),
            pltpu.SemaphoreType.DMA((1,)),
            pltpu.SemaphoreType.DMA((STEPS, max(len(steps) for steps in GROUPS))),
            pltpu.SemaphoreType.DMA((STEPS,)),
            pltpu.SemaphoreType.DMA((2,)),
            pltpu.SemaphoreType.DMA((2,)),
            pltpu.SemaphoreType.DMA((STEPS, 2)),
            pltpu.SemaphoreType.DMA((STEPS, 2)),
        ],
        compiler_params=pltpu.CompilerParams(
            collective_id=0, has_side_effects=True, vmem_limit_bytes=60 * 1024 * 1024
        ),
        name="coupled_steps",
    )(
        modal_disp,
        modal_rate,
        mode_omega,
        mode_zeta,
        marker_panel.reshape(1, markers),
        tile_block,
        velocity.reshape(3, inner, depth),
        mode_shape,
        weights,
        normals,
        stress_modes,
        hot_nodes,
        bins,
        base_load,
    )
    results = pl.pallas_call(
        finish,
        out_shape=[
            jax.ShapeDtypeStruct((3, inner, depth), F32),
            jax.ShapeDtypeStruct((own, modes), F32),
            jax.ShapeDtypeStruct((own, modes), F32),
            jax.ShapeDtypeStruct((own, hots), F32),
        ],
        in_specs=[held] * 4,
        out_specs=[stay] * 4,
        scratch_shapes=[
            small,
            small,
            pltpu.VMEM((own, hots), F32),
            pltpu.SemaphoreType.DMA((4,)),
        ],
        compiler_params=pltpu.CompilerParams(vmem_limit_bytes=4 * 1024 * 1024),
        name="finish",
    )(*results)
    return (results[0].reshape(velocity.shape),) + tuple(results[1:])


def solution(mesh):
    placed = (
        P(None, "stream", "span", None),
        P(("stream", "span"), None),
        P(("stream", "span")),
        P(None, ("stream", "span")),
        P(("stream", "span")),
        P(("stream", "span"), None),
        P(("stream", "span"), None),
        P(("stream", "span"), None),
        P(("stream", "span"), None),
        P(("stream", "span"), None),
        P(("stream", "span"), None),
        P(),
        P(("stream", "span"), None),
        P(),
    )
    return jax.shard_map(
        body,
        mesh=mesh,
        in_specs=placed,
        out_specs=(
            P(None, "stream", "span", None),
            P(("stream", "span"), None),
            P(("stream", "span"), None),
            P(("stream", "span"), None),
        ),
        check_vma=False,
    )
```
